128 devices in a mesh: ctx: 32 (over z, y, core), ch: 4 (over x).
Axes of the slice: x: 4, y: 4, z: 4, core: 2. Of those that a mesh axis runs over, the one named last changes fastest.
Arguments:
- query_in: bfloat16 [5120, 8192], P('ctx', 'ch'), may hold values from -6 to 6
- key_in: bfloat16 [5120, 8192], P('ctx', 'ch'), may hold values from -6 to 6
- value_in: bfloat16 [5120, 8192], P('ctx', 'ch'), may hold values from -6 to 6
- row_place: int32 [5120], P('ctx'), may hold values from 0 to 5119, as said below
- short_weight: bfloat16 [3, 7, 8192], P(None, None, 'ch'), may hold values from -2 to 2
- long_filter: bfloat16 [128, 8192], P(None, 'ch'), may hold values from -0.5 to 0.5
- target: bfloat16 [5120, 8192], P('ctx', 'ch'), may hold values from -6 to 6
- taxon_ids: int32 [5120], P('ctx'), may hold values from 0 to 15
- taxon_weight: float32 [16], replicated, may hold values from 0.5 to 2
Outputs:
- gated_out: bfloat16 [5120, 8192], P('ctx', 'ch')
- query_grad: bfloat16 [5120, 8192], P('ctx', 'ch')
- key_grad: bfloat16 [5120, 8192], P('ctx', 'ch')
- value_grad: bfloat16 [5120, 8192], P('ctx', 'ch')
- filter_grad: float32 [128, 8192], P(None, 'ch')
- short_grad: float32 [3, 7, 8192], P(None, None, 'ch')
- taxon_loss: float32 [16], replicated
The draws below stay inside these ranges and needn't reach their ends.
Inputs may be any that keep to these rules, and one draw needn't show every extreme that they name: row_place is a permutation of the 5120 positions. Of the 160 rows that one device of index k holds, exactly 10 have positions in the block of 160 positions of device (k + 1) mod 32, exactly 5 in the block of every other device but one, and none in the block of that one.
All inputs are finite; a program needn't handle non-finite values.
Results may differ from the reference program's by a relative error of at most 0.0052.
Values may be sent and summed in bfloat16 or wider, within the bound.
A program may use at most 320 MiB of HBM per device.

```python
import math
import jax
import jax.numpy as jnp
import numpy as np
from jax import lax

D = 8192
TOK_DEV = 160
FILT = 128
SHORT = 7
NTAX = 16
TOKENS = 5120


def draw_row_place(key, part):
    peer_count = TOKENS // TOK_DEV
    unit_rows = TOK_DEV // peer_count
    keys = jax.random.split(jax.random.fold_in(key, 17), 5)
    others = (1 + jax.random.permutation(keys[0], peer_count - 1)).astype(jnp.int32)
    zero_at = jax.random.randint(keys[1], (), 0, peer_count - 1).astype(jnp.int32)
    others = jnp.where(jnp.arange(peer_count - 1, dtype=jnp.int32) == zero_at, 0, others).astype(jnp.int32)
    offsets = jnp.concatenate([others, jnp.zeros((1,), jnp.int32)])
    sources = jnp.arange(peer_count, dtype=jnp.int32)
    owner = ((sources[:, None] + 1 + offsets[None, :]) % peer_count).astype(jnp.int32)

    def order_rows(subkey):
        return jax.random.permutation(subkey, TOK_DEV).astype(jnp.int32)
    dest_order = jax.vmap(order_rows)(jax.random.split(keys[3], peer_count))
    source_order = jax.vmap(order_rows)(jax.random.split(keys[4], peer_count))
    slot_index = jnp.arange(TOK_DEV, dtype=jnp.int32)
    block_index = slot_index // unit_rows
    owner_rows = owner[:, block_index]
    landing = owner_rows * TOK_DEV + dest_order[owner_rows, slot_index[None, :]]
    source_rows = jnp.arange(peer_count, dtype=jnp.int32)[:, None] * TOK_DEV + source_order
    return jnp.zeros((TOKENS,), jnp.int32).at[source_rows.reshape(-1)].set(landing.reshape(-1).astype(jnp.int32))


def with_ends(array, stream_key, smallest, top_value):
    spot = [jax.random.randint(jax.random.fold_in(stream_key, axis), (), 0, length) for axis, length in enumerate(array.shape)]
    main_axis = array.shape.index(max(array.shape))
    next_to = spot[:main_axis] + [(spot[main_axis] + 1) % array.shape[main_axis]] + spot[main_axis + 1:]
    return array.at[tuple(spot)].set(smallest).at[tuple(next_to)].set(top_value)


def shard_levels(rng, extent, cuts, least, high):
    factor_of, own = 1.0, jax.random.fold_in(rng, 6)
    for axis_at, shards_of in cuts:
        heights = jnp.exp(jax.random.uniform(jax.random.fold_in(own, axis_at), (shards_of,), jnp.float32, least / len(cuts), high / len(cuts)))
        factor_of = factor_of * jnp.repeat(heights, extent[axis_at] // shards_of).reshape([-1 if axis == axis_at else 1 for axis in range(len(extent))])
    return factor_of


def cumulative_ranks(number_of, lean):
    loads = [(1 << 20) // math.isqrt(standing ** lean) + 1 for standing in range(1, number_of + 1)]
    deviation = 1 + sum(loads) // (1 << 30)
    return np.cumsum(np.array([max(1, weight // deviation) for weight in loads]))


def skewed_ids(rng, shape, number_of, skew):
    table = cumulative_ranks(number_of, skew)
    lot = jax.random.randint(jax.random.fold_in(rng, 1), shape, 0, int(table[number_of - 1]))
    grade = jnp.searchsorted(jnp.asarray(table, jnp.int32), lot, side="right")
    return jax.random.permutation(jax.random.fold_in(rng, 2), number_of)[grade].astype(jnp.int32)


def bell_draw(key, shape, scale, bound, cuts=(), kind=jnp.bfloat16):
    array = scale * jax.random.normal(key, shape, jnp.float32)
    if cuts:
        array = array * shard_levels(key, shape, cuts, -0.22, 0.18)
    return jnp.clip(array, -bound, bound).astype(kind)


def setup_inputs(seed: int = 0) -> dict:
    key_of = jax.random.split(jax.random.key(seed), 10)
    return {
        "query_in": bell_draw(key_of[0], (TOKENS, D), 1.0, 6.0, ((0, 32), (1, 4))),
        "key_in": bell_draw(key_of[1], (TOKENS, D), 1.0, 6.0, ((0, 32), (1, 4))),
        "value_in": bell_draw(key_of[2], (TOKENS, D), 1.0, 6.0, ((0, 32), (1, 4))),
        "row_place": draw_row_place(jax.random.fold_in(key_of[9], 71), 0),
        "short_weight": bell_draw(key_of[4], (3, SHORT, D), SHORT ** -0.5, 2.0, ((2, 4),)),
        "long_filter": bell_draw(key_of[5], (FILT, D), FILT ** -0.5, 0.5, ((1, 4),)),
        "target": bell_draw(key_of[6], (TOKENS, D), 1.0, 6.0, ((0, 32), (1, 4))),
        "taxon_ids": with_ends(skewed_ids(key_of[7], (TOKENS,), NTAX, 2), jax.random.fold_in(key_of[7], 3), 0, NTAX - 1).astype(jnp.int32),
        "taxon_weight": jnp.clip(jnp.exp(jax.random.uniform(key_of[8], (NTAX,), jnp.float32, math.log(0.5), math.log(2.0))), 0.5, 2.0),
    }


tile_rows = 32

def skew_rows(row, span_width):
    channels = row.shape[1]
    table = (np.arange(span_width)[None, :] - np.arange(tile_rows)[:, None]) % (span_width + 1)
    picked = jnp.take(row, jnp.asarray(table.reshape(-1), dtype=jnp.int32), axis=0)
    return picked.reshape(tile_rows, span_width, channels)

def forward_matrix(long_filter):
    filter_len, channels = long_filter.shape
    zero_row = jnp.zeros((1, channels), long_filter.dtype)
    tail_rows = jnp.zeros((tile_rows, channels), long_filter.dtype)
    return skew_rows(jnp.concatenate([zero_row, long_filter[::-1], tail_rows], axis=0), tile_rows + filter_len)

def backward_matrix(long_filter):
    filter_len, channels = long_filter.shape
    tail_rows = jnp.zeros((tile_rows + 1, channels), long_filter.dtype)
    return skew_rows(jnp.concatenate([long_filter, tail_rows], axis=0), tile_rows + filter_len)

def windows(padded, filter_len):
    row_total = padded.shape[0] - filter_len
    blocks = row_total // tile_rows
    pieces = [padded[piece_index * tile_rows:piece_index * tile_rows + row_total].reshape(blocks, tile_rows, padded.shape[1]) for piece_index in range(filter_len // tile_rows + 1)]
    return jnp.concatenate(pieces, axis=1)

def diagonal_sums(grid_sums, filter_len):
    span_width = grid_sums.shape[1]
    channels = grid_sums.shape[2]
    flattened = grid_sums.reshape(tile_rows * span_width, channels)
    flattened = jnp.concatenate([flattened, jnp.zeros((tile_rows, channels), jnp.float32)], axis=0)
    skewed = flattened.reshape(tile_rows, span_width + 1, channels)[:, 1:filter_len + 1]
    return lax.optimization_barrier(jnp.sum(skewed, axis=0))[::-1]

def causal_taps(extended, weights, row_total):
    short_taps = weights.shape[0]
    summed = jnp.zeros((row_total, extended.shape[1]), jnp.float32)
    for offset in range(short_taps):
        begin_at = short_taps - 1 - offset
        summed = summed + weights[offset].astype(jnp.float32) * extended[begin_at:begin_at + row_total].astype(jnp.float32)
    return summed

def reverse_taps(extended, weights, row_total):
    summed = jnp.zeros((row_total, extended.shape[1]), jnp.float32)
    for offset in range(weights.shape[0]):
        summed = summed + weights[offset].astype(jnp.float32) * extended[offset:offset + row_total].astype(jnp.float32)
    return summed

def tap_products(grads, extended, short_taps):
    row_total = grads.shape[0]
    rows_out = []
    for offset in range(short_taps):
        begin_at = short_taps - 1 - offset
        rows_out.append(lax.optimization_barrier(jnp.sum(grads * extended[begin_at:begin_at + row_total].astype(jnp.float32), axis=0)))
    return jnp.stack(rows_out)

def channel_block(block_in, row_weight):
    query_rows, key_rows, value_rows, short_block, filter_block, target_block = block_in
    seg_rows, channels = query_rows.shape
    short_taps = short_block.shape[1]
    filter_len = filter_block.shape[0]
    margin = short_taps - 1
    grad_scale = 1.0 / math.sqrt(seg_rows)
    lead_zero = jnp.zeros((margin, channels), jnp.bfloat16)
    query_ext = jnp.concatenate([lead_zero, query_rows], axis=0)
    key_ext = jnp.concatenate([lead_zero, key_rows], axis=0)
    value_ext = jnp.concatenate([lead_zero, value_rows], axis=0)
    query_conv = causal_taps(query_ext, short_block[0], seg_rows)
    key_conv = causal_taps(key_ext, short_block[1], seg_rows)
    value_conv = causal_taps(value_ext, short_block[2], seg_rows)
    gated = (key_conv * value_conv).astype(jnp.bfloat16)
    gated_pad = jnp.concatenate([jnp.zeros((filter_len, channels), jnp.bfloat16), gated], axis=0)
    window_rows = windows(gated_pad, filter_len).astype(jnp.float32)
    mixed = jnp.einsum('abc,nbc->nac', forward_matrix(filter_block).astype(jnp.float32), window_rows).reshape(seg_rows, channels)
    gated_out = (query_conv * mixed).astype(jnp.bfloat16)
    target_f = target_block.astype(jnp.float32)
    row_loss = lax.optimization_barrier(jnp.sum(gated_out.astype(jnp.float32) * target_f, axis=1))
    grad_out = row_weight[:, None] * target_f
    grad_qconv = grad_out * mixed
    grad_mixed = (grad_out * query_conv).astype(jnp.bfloat16)
    mixed_pad = jnp.concatenate([grad_mixed, jnp.zeros((filter_len, channels), jnp.bfloat16)], axis=0)
    back_rows = windows(mixed_pad, filter_len).astype(jnp.float32)
    grad_gated = jnp.einsum('abc,nbc->nac', backward_matrix(filter_block).astype(jnp.float32), back_rows).reshape(seg_rows, channels)
    grad_kconv = grad_gated * value_conv
    grad_vconv = grad_gated * key_conv
    tile_grads = jnp.einsum('nac,nbc->abc', grad_mixed.astype(jnp.float32).reshape(-1, tile_rows, channels), window_rows)
    filter_part = diagonal_sums(tile_grads, filter_len) * grad_scale
    short_part = jnp.stack([tap_products(grad_qconv, query_ext, short_taps), tap_products(grad_kconv, key_ext, short_taps), tap_products(grad_vconv, value_ext, short_taps)]) * grad_scale
    tail_zero = jnp.zeros((margin, channels), jnp.float32)
    grad_query = reverse_taps(jnp.concatenate([grad_qconv, tail_zero], axis=0), short_block[0], seg_rows).astype(jnp.bfloat16)
    grad_key = reverse_taps(jnp.concatenate([grad_kconv, tail_zero], axis=0), short_block[1], seg_rows).astype(jnp.bfloat16)
    grad_value = reverse_taps(jnp.concatenate([grad_vconv, tail_zero], axis=0), short_block[2], seg_rows).astype(jnp.bfloat16)
    return (gated_out, grad_query, grad_key, grad_value, filter_part, short_part, row_loss)

def reference(query_in, key_in, value_in, row_place, short_weight, long_filter, target, taxon_ids, taxon_weight):
    seg_rows = query_in.shape[0]
    width_all = query_in.shape[1]
    query_rows = jnp.zeros_like(query_in).at[row_place].set(query_in)
    key_rows = jnp.zeros_like(key_in).at[row_place].set(key_in)
    value_rows = jnp.zeros_like(value_in).at[row_place].set(value_in)
    row_weight = taxon_weight[taxon_ids].astype(jnp.float32)
    block_width = 512 if width_all % 512 == 0 else width_all
    block_count = width_all // block_width

    def split_rows(rows):
        return rows.reshape(rows.shape[0], block_count, block_width).transpose(1, 0, 2)

    def split_taps(taps_in):
        return taps_in.reshape(taps_in.shape[0], taps_in.shape[1], block_count, block_width).transpose(2, 0, 1, 3)

    def split_filter(filt_in):
        return filt_in.reshape(filt_in.shape[0], block_count, block_width).transpose(1, 0, 2)
    stacked = (split_rows(query_rows), split_rows(key_rows), split_rows(value_rows), split_taps(short_weight), split_filter(long_filter), split_rows(target))
    results = lax.map(lambda block_in: channel_block(block_in, row_weight), stacked)
    gated_blocks, query_blocks, key_blocks, value_blocks, filter_blocks, short_blocks, loss_blocks = results

    def join_rows(blocks):
        return blocks.transpose(1, 0, 2).reshape(blocks.shape[1], width_all)
    gated_out = join_rows(gated_blocks)
    grad_query = join_rows(query_blocks)
    grad_key = join_rows(key_blocks)
    grad_value = join_rows(value_blocks)
    filter_grad = filter_blocks.transpose(1, 0, 2).reshape(filter_blocks.shape[1], width_all)
    short_grad = short_blocks.transpose(1, 2, 0, 3).reshape(3, short_blocks.shape[2], width_all)
    row_loss = lax.optimization_barrier(jnp.sum(loss_blocks, axis=0))
    loss_scale = 1.0 / math.sqrt(D * seg_rows / NTAX)
    taxon_loss = jax.ops.segment_sum(row_loss, taxon_ids, num_segments=NTAX) * loss_scale
    return (gated_out, grad_query[row_place], grad_key[row_place], grad_value[row_place], filter_grad, short_grad, taxon_loss)
```

```python
import math

import jax
import jax.numpy as jnp
import numpy as np
from jax import lax
from jax.experimental import pallas as pl
from jax.experimental.pallas import tpu as pltpu
from jax.sharding import PartitionSpec as P

MESH = pl.DeviceIdType.MESH
F32 = jnp.float32
BF16 = jnp.bfloat16
unit = 5
block_rows = 16
lanes = 128
edge = 16
chunks = 4
stream_step = 1024.0


def split_constant(array):
    high = array.astype(np.float32).astype(jnp.bfloat16)
    low = (array - high.astype(np.float64)).astype(np.float32).astype(jnp.bfloat16)
    return high, low


def dft_tables(rows, taps):
    half = rows
    size = 2 * rows
    span = taps + rows + edge
    theta = np.pi * (2 * np.arange(half) + 1) / size

    def ahead(index):
        angle = theta[:, None] * index[None, :]
        return np.concatenate([np.cos(angle), -np.sin(angle)], axis=0)

    def back(index):
        angle = theta[None, :] * index[:, None]
        return np.concatenate([np.cos(angle), -np.sin(angle)], axis=1) * (2.0 / size)

    tables = {
        "ahead": ahead(np.arange(span)),
        "own": ahead(np.arange(rows)),
        "later": ahead(np.arange(rows, rows + taps + edge)),
        "taps": ahead(np.arange(taps)),
        "mixed": back(np.arange(rows + edge) + taps),
        "gated": back(np.arange(rows + edge)),
        "filter": back(taps - np.arange(taps)),
    }
    return tables


table_names = ("ahead", "own", "later", "taps", "mixed", "gated", "filter")


def payload_rows(taps, short_taps):
    return -(-(taps + 3 * short_taps) // 32) * 32


def iota(shape, axis):
    return lax.broadcasted_iota(jnp.int32, shape, axis)


def slot_facts(index):
    block = lax.shift_right_logical(index, 4)
    row = jnp.bitwise_and(index, block_rows - 1)
    stream = jnp.where(row >= unit, 1, 0) + jnp.where(row >= 2 * unit, 1, 0)
    rank = row - unit * stream
    valid = row < 3 * unit
    return block, stream, rank, valid


def whole_kernel(
    peers,
    groups,
    q_ref,
    k_ref,
    v_ref,
    place_ref,
    place3_ref,
    short_ref,
    filter_ref,
    target_ref,
    taxon_ref,
    weight_ref,
    ahead_hi,
    ahead_lo,
    own_hi,
    own_lo,
    later_hi,
    later_lo,
    taps_hi,
    taps_lo,
    mixed_hi,
    mixed_lo,
    gated_hi,
    gated_lo,
    filter_hi,
    filter_lo,
    out_ref,
    qg_ref,
    kg_ref,
    vg_ref,
    fg_ref,
    sg_ref,
    loss_ref,
    pack_m,
    unpack_m,
    place_m,
    return_m,
    send_b,
    recv_b,
    meta_s,
    meta_r,
    bsend_b,
    brecv_b,
    rows_b,
    prev_s,
    prev_r,
    next_s,
    next_r,
    tnext_s,
    tnext_r,
    wnext_s,
    wnext_r,
    qc_b,
    kc_b,
    vc_b,
    go_b,
    gext_b,
    gm_b,
    spec_b,
    short_b,
    gbuf,
    gr_b,
    lacc,
    par_b,
    rs_s,
    rs_r,
    ag_s,
    ag_r,
    lch_s,
    lch_r,
    lct_s,
    lct_r,
    sem_as,
    sem_ar,
    sem_bs,
    sem_br,
    sem_ps,
    sem_pr,
    sem_ns,
    sem_nr,
    sem_gs,
    sem_gr,
    sem_ms,
    sem_mr,
    sem_x,
):
    rows, channels = q_ref.shape
    taps = filter_ref.shape[0]
    short_taps = short_ref.shape[1]
    width = channels // chunks
    col_tiles = channels // lanes
    tiles = width // lanes
    pairs = tiles // 2
    blocks = peers + 1
    slots = blocks * block_rows
    ext = rows + edge
    payload = payload_rows(taps, short_taps)
    half_rows = payload // 2
    me = lax.axis_index("ctx")
    ch = lax.axis_index("ch")
    right = lax.rem(me + 1, peers)
    left = lax.rem(me + peers - 1, peers)
    grad_scale = 1.0 / math.sqrt(rows * peers)
    loss_scale = 1.0 / math.sqrt(channels * groups * rows * peers / weight_ref.shape[1])

    barrier = pltpu.get_barrier_semaphore()

    def greet(step, carry):
        pl.semaphore_signal(
            barrier, inc=1, device_id=(lax.rem(me + step, peers), ch), device_id_type=MESH
        )
        return carry

    lax.fori_loop(1, peers, greet, 0)
    for step in range(1, groups):
        pl.semaphore_signal(
            barrier, inc=1, device_id=(me, lax.rem(ch + step, groups)), device_id_type=MESH
        )

    def push(src, dst, send_sem, recv_sem, ctx_to, ch_to):
        return pltpu.make_async_remote_copy(
            src_ref=src,
            dst_ref=dst,
            send_sem=send_sem,
            recv_sem=recv_sem,
            device_id=(ctx_to, ch_to),
            device_id_type=MESH,
        )

    def drain(ref, sem):
        pltpu.make_async_copy(ref, ref, sem).wait()

    def column(row_vector, count):
        eye = iota((count, count), 0) == iota((count, count), 1)
        return jnp.sum(jnp.where(eye, row_vector, 0.0), axis=1, keepdims=True)

    place_row = place_ref[...].astype(F32)
    place3_row = place3_ref[...].astype(F32)
    owner_row = jnp.floor((place_row + 0.5) * (1.0 / rows))
    owner3_row = jnp.floor((place3_row + 0.5) * (1.0 / rows))
    owner_col = column(owner_row, rows)
    place_col = column(place_row, rows)
    local_col = place_col - owner_col * rows

    def slot_key(owner, rank):
        return jnp.where(
            rank < unit - 0.5, owner * unit + rank, float(peers * unit) + rank - unit
        )

    order3 = iota((rows, 3 * rows), 1)
    stream3 = jnp.where(order3 >= rows, 1, 0) + jnp.where(order3 >= 2 * rows, 1, 0)
    before3 = iota((rows, 3 * rows), 0) < order3 - rows * stream3
    rank3_row = jnp.sum(
        jnp.where(jnp.logical_and(owner_col == owner3_row, before3), 1.0, 0.0),
        axis=0,
        keepdims=True,
    )
    key3_row = slot_key(owner3_row, rank3_row)
    before = iota((rows, rows), 1) < iota((rows, rows), 0)
    rank_col = jnp.sum(
        jnp.where(jnp.logical_and(owner_col == owner_row, before), 1.0, 0.0),
        axis=1,
        keepdims=True,
    )
    key_col = slot_key(owner_col, rank_col)

    lane3 = iota((1, 3 * rows), 1)
    lane_stream = jnp.where(lane3 >= rows, 1, 0) + jnp.where(lane3 >= 2 * rows, 1, 0)
    lane_local = lane3 - rows * lane_stream

    def static_key(shape, axis):
        block, stream, rank, valid = slot_facts(iota(shape, axis))
        key = jnp.where(valid, stream * 1024 + block * unit + rank, -1)
        return key.astype(F32), jnp.where(valid, stream * 1024, -4096).astype(F32)

    slot_key_col, slot_stream_col = static_key((slots, 1), 0)
    slot_key_row, slot_stream_row = static_key((1, slots), 1)
    full3_row = key3_row + lane_stream.astype(F32) * stream_step
    pack_m[...] = jnp.where(slot_key_col == full3_row, 1.0, 0.0).astype(BF16)
    for s in range(3):
        return_m[s * rows : (s + 1) * rows, :] = jnp.where(
            key_col + s * stream_step == slot_key_row, 1.0, 0.0
        ).astype(BF16)

    meta_col = jnp.broadcast_to(local_col + 1.0, (rows, lanes)).astype(BF16)
    meta3 = jnp.concatenate([meta_col] * 3, axis=0)
    meta_s[...] = (
        jnp.dot(pack_m[...], meta3, preferred_element_type=F32)
        .astype(BF16)
        .reshape(blocks, block_rows, lanes)
    )

    pair_lanes = 2 * lanes

    def pack(c, carry):
        def body(u, inner):
            base = pl.multiple_of(c * width + u * pair_lanes, pair_lanes)
            cols = pl.ds(base, pair_lanes)
            stacked = jnp.concatenate([q_ref[:, cols], k_ref[:, cols], v_ref[:, cols]], axis=0)
            packed = jnp.dot(pack_m[...], stacked, preferred_element_type=F32).astype(BF16)
            local = pl.ds(pl.multiple_of(u * pair_lanes, pair_lanes), pair_lanes)
            send_b[c, :, :, local] = packed.reshape(blocks, block_rows, pair_lanes)
            return inner

        lax.fori_loop(0, pairs, body, 0)
        return carry

    ids_row = taxon_ref[...].astype(F32)
    ids_col = column(ids_row, rows)
    count = weight_ref.shape[1]
    taxon_hot = iota((rows, lanes), 1).astype(F32) == ids_col
    weights = jnp.concatenate([weight_ref[...], jnp.zeros((1, lanes - count), F32)], axis=1)
    weight_col = jnp.sum(jnp.where(taxon_hot, weights, 0.0), axis=1, keepdims=True)
    tnext_s[...] = target_ref[0:edge, :]
    wnext_s[...] = jnp.broadcast_to(weight_col[0:edge], (edge, lanes))
    wait_for = peers - 1 + groups - 1

    def exchange(source, landing, send_sem, recv_sem):
        pltpu.make_async_copy(source.at[me], landing.at[me], recv_sem).start()
        push(source.at[peers], landing.at[peers], send_sem, recv_sem, right, ch).start()

        def body(step, carry):
            to = lax.rem(me + step, peers)
            push(source.at[to], landing.at[me], send_sem, recv_sem, to, ch).start()
            return carry

        lax.fori_loop(1, peers, body, 0)

    def exchange_back(source, landing, send_sem, recv_sem):
        pltpu.make_async_copy(source.at[me], landing.at[me], recv_sem).start()
        push(source.at[peers], landing.at[peers], send_sem, recv_sem, left, ch).start()

        def body(step, carry):
            to = lax.rem(me + step, peers)
            push(source.at[to], landing.at[me], send_sem, recv_sem, to, ch).start()
            return carry

        lax.fori_loop(1, peers, body, 0)

    pack(0, 0)
    pl.semaphore_wait(barrier, wait_for)
    exchange(meta_s, meta_r, sem_ms.at[0], sem_mr.at[0])
    target_push = push(tnext_s, tnext_r, sem_x.at[0], sem_x.at[1], left, ch)
    weight_push = push(wnext_s, wnext_r, sem_x.at[12], sem_x.at[13], left, ch)
    exchange(send_b.at[0], recv_b.at[0], sem_as.at[0], sem_ar.at[0])

    def pack_and_send(c, carry):
        pack(c, 0)
        exchange(send_b.at[c], recv_b.at[c], sem_as.at[c], sem_ar.at[c])
        return carry

    lax.fori_loop(1, chunks, pack_and_send, 0)
    target_push.start()
    weight_push.start()

    short_b[:, 0:short_taps, :] = short_ref[...].astype(F32)

    def filter_spectrum(u, carry):
        cols = pl.ds(pl.multiple_of(u * pair_lanes, pair_lanes), pair_lanes)
        x = filter_ref[:, cols]
        found = jnp.dot(taps_hi[...], x, preferred_element_type=F32) + jnp.dot(
            taps_lo[...], x, preferred_element_type=F32
        )
        spec_b[2 * u] = found[:, :lanes]
        spec_b[2 * u + 1] = found[:, lanes:]
        return carry

    lax.fori_loop(0, col_tiles // 2, filter_spectrum, 0)
    lacc[...] = jnp.zeros_like(lacc)

    drain(meta_r, sem_mr.at[0])
    meta = meta_r[...].reshape(slots, lanes)
    pick = jnp.where(iota((8, lanes), 1) == 0, 1.0, 0.0).astype(BF16)
    found_row = lax.dot_general(
        pick, meta, (((1,), (1,)), ((), ())), preferred_element_type=F32
    )[0:1, :]
    landed_row = found_row + slot_stream_row
    landed_col = meta[:, 0:1].astype(F32) + slot_stream_col
    target_lane = (lane_local + 1).astype(F32) + lane_stream.astype(F32) * stream_step
    place_m[...] = jnp.where(landed_col == target_lane, 1.0, 0.0).astype(BF16)
    own_index = (iota((rows, 1), 0) + 1).astype(F32)
    for s in range(3):
        unpack_m[s * rows : (s + 1) * rows, :] = jnp.where(
            own_index + s * stream_step == landed_row, 1.0, 0.0
        ).astype(BF16)
    target_push.wait()
    weight_push.wait()
    not_first = jnp.where(me > 0, 1.0, 0.0)
    not_last = jnp.where(me < peers - 1, 1.0, 0.0)

    def tile_range(c):
        return pl.ds(c * tiles, tiles)

    def prev_push(c):
        return push(prev_s.at[c], prev_r.at[c], sem_ps.at[c], sem_pr.at[c], right, ch)

    def next_push(c):
        return push(next_s.at[c], next_r.at[c], sem_ns.at[c], sem_nr.at[c], left, ch)

    def gated_push(c):
        return push(
            gext_b.at[tile_range(c), taps_at : taps_at + taps, :],
            gext_b.at[tile_range(c), 0:taps, :],
            sem_gs.at[c],
            sem_gr.at[c],
            right,
            ch,
        )

    taps_at = rows

    def mixed_push(c):
        return push(
            gm_b.at[tile_range(c), 0 : taps + edge, :],
            gm_b.at[tile_range(c), rows : rows + taps + edge, :],
            sem_gs.at[chunks + c],
            sem_gr.at[chunks + c],
            left,
            ch,
        )

    def land(c):
        drain(recv_b.at[c], sem_ar.at[c])

        def body(u, carry):
            local = pl.ds(pl.multiple_of(u * pair_lanes, pair_lanes), pair_lanes)
            got = recv_b[c, :, :, local].reshape(slots, pair_lanes)
            placed = jnp.dot(unpack_m[...], got, preferred_element_type=F32)
            for part in range(2):
                at = c * tiles + 2 * u + part
                piece = placed[:, part * lanes : (part + 1) * lanes]
                for s in range(3):
                    rows_b[s, at, edge : edge + rows, :] = piece[s * rows : (s + 1) * rows]
                    prev_s[c, s, 2 * u + part] = piece[
                        (s + 1) * rows - edge : (s + 1) * rows
                    ].astype(BF16)
                    if s > 0:
                        next_s[c, s - 1, 2 * u + part] = piece[
                            s * rows : s * rows + edge
                        ].astype(BF16)
            return carry

        lax.fori_loop(0, pairs, body, 0)
        prev_push(c).start()
        next_push(c).start()

    def convolve(c):
        prev_push(c).wait()
        next_push(c).wait()

        def body(u, carry):
            at = c * tiles + u
            cols = pl.ds(pl.multiple_of(at * lanes, lanes), lanes)
            for s in range(3):
                rows_b[s, at, 0:edge, :] = prev_r[c, s, u].astype(F32) * not_first
            for s in range(2):
                rows_b[s + 1, at, edge + rows : 2 * edge + rows, :] = next_r[c, s, u].astype(F32)

            def conv(s, total):
                summed = None
                for j in range(short_taps):
                    term = (
                        short_b[s, j : j + 1, cols]
                        * rows_b[s, at, edge - j : edge - j + total, :]
                    )
                    summed = term if summed is None else summed + term
                return summed

            k_conv = conv(1, ext)
            v_conv = conv(2, ext)
            kc_b[at] = k_conv
            vc_b[at] = v_conv
            gext_b[at, taps : taps + ext, :] = (k_conv * v_conv).astype(BF16)
            q_conv = conv(0, rows)
            qc_b[at] = q_conv
            out_grad = weight_col[0:rows] * target_ref[:, cols].astype(F32)
            go_b[at, 0:rows, :] = out_grad
            go_b[at, rows:ext, :] = (
                wnext_r[...] * tnext_r[:, cols].astype(F32) * not_last
            )
            gm_b[at, 0:rows, :] = (out_grad * q_conv).astype(BF16)
            return carry

        lax.fori_loop(0, tiles, body, 0)
        gated_push(c).start()
        mixed_push(c).start()

    def both(high, low, x):
        return jnp.dot(high, x, preferred_element_type=F32) + jnp.dot(
            low, x, preferred_element_type=F32
        )

    def inverse(high, low, real, imag):
        y = jnp.concatenate([real, imag], axis=0)
        y_hi = y.astype(BF16)
        y_lo = (y - y_hi.astype(F32)).astype(BF16)
        return both(high[...], low[...], y_hi) + jnp.dot(
            high[...], y_lo, preferred_element_type=F32
        )

    def backward(c):
        gated_push(c).wait()
        mixed_push(c).wait()

        @pl.when(me == 0)
        def _():
            def clear(u, carry):
                gext_b[c * tiles + u, 0:taps, :] = jnp.zeros((taps, lanes), BF16)
                return carry

            lax.fori_loop(0, tiles, clear, 0)

        @pl.when(me == peers - 1)
        def _():
            def clear(u, carry):
                gm_b[c * tiles + u, rows : rows + taps + edge, :] = jnp.zeros(
                    (taps + edge, lanes), BF16
                )
                return carry

            lax.fori_loop(0, tiles, clear, 0)

        def body(u, carry):
            first = c * tiles + 2 * u
            gx = jnp.concatenate([gext_b[first], gext_b[first + 1]], axis=1)
            g_own = jnp.concatenate(
                [gm_b[first, 0:rows, :], gm_b[first + 1, 0:rows, :]], axis=1
            )
            g_later = jnp.concatenate(
                [
                    gm_b[first, rows : rows + taps + edge, :],
                    gm_b[first + 1, rows : rows + taps + edge, :],
                ],
                axis=1,
            )
            spec = jnp.concatenate([spec_b[first], spec_b[first + 1]], axis=1)
            fr, fi = spec[:rows], spec[rows:]
            sg = both(ahead_hi[...], ahead_lo[...], gx)
            gr, gi = sg[:rows], sg[rows:]
            mixed = inverse(mixed_hi, mixed_lo, fr * gr - fi * gi, fr * gi + fi * gr)
            so = both(own_hi[...], own_lo[...], g_own)
            mr, mi = so[:rows], so[rows:]
            taps_grad = inverse(filter_hi, filter_lo, mr * gr + mi * gi, mr * gi - mi * gr)
            sl = both(later_hi[...], later_lo[...], g_later)
            ar, ai = mr + sl[:rows], mi + sl[rows:]
            gated_grad = inverse(gated_hi, gated_lo, fr * ar + fi * ai, fr * ai - fi * ar)
            for part in range(2):
                at = first + part
                cols = pl.ds(pl.multiple_of(at * lanes, lanes), lanes)
                lane_cut = slice(part * lanes, (part + 1) * lanes)
                mix = mixed[:, lane_cut]
                gg = gated_grad[:, lane_cut]
                par_b[at, 0:taps, :] = taps_grad[:, lane_cut] * grad_scale
                par_b[at, payload - 32 : payload, :] = jnp.zeros((32, lanes), F32)
                out = (qc_b[at] * mix[:rows]).astype(BF16)
                out_ref[:, cols] = out
                lacc[...] += out.astype(F32) * target_ref[:, cols].astype(F32)
                gbuf[0] = go_b[at] * mix
                gbuf[1] = gg * vc_b[at]
                gbuf[2] = gg * kc_b[at]
                for s in range(3):
                    own = gbuf[s, 0:rows, :]
                    back = None
                    for j in range(short_taps):
                        found = jnp.sum(
                            own * rows_b[s, at, edge - j : edge - j + rows, :],
                            axis=0,
                            keepdims=True,
                        )
                        par_b[at, taps + s * short_taps + j : taps + s * short_taps + j + 1, :] = (
                            found * grad_scale
                        )
                        term = short_b[s, j : j + 1, cols] * gbuf[s, j : j + rows, :]
                        back = term if back is None else back + term
                    gr_b[s * rows : (s + 1) * rows, lane_cut] = back.astype(BF16)
            local = pl.ds(pl.multiple_of(u * pair_lanes, pair_lanes), pair_lanes)
            packed = jnp.dot(place_m[...], gr_b[...], preferred_element_type=F32).astype(BF16)
            bsend_b[c, :, :, local] = packed.reshape(blocks, block_rows, pair_lanes)
            return carry

        lax.fori_loop(0, pairs, body, 0)
        exchange_back(bsend_b.at[c], brecv_b.at[c], sem_bs.at[c], sem_br.at[c])

    def steps(t, carry):
        @pl.when(jnp.logical_and(t >= 2, t < chunks + 2))
        def _():
            backward(t - 2)

        @pl.when(jnp.logical_and(t >= 1, t < chunks + 1))
        def _():
            convolve(t - 1)

        @pl.when(t < chunks)
        def _():
            land(t)

        return carry

    lax.fori_loop(0, chunks + 2, steps, 0)

    row_loss = jnp.sum(lacc[...], axis=1, keepdims=True)
    taxon_part = (
        jnp.sum(jnp.where(taxon_hot[0:rows], row_loss, 0.0), axis=0, keepdims=True) * loss_scale
    )
    lch_s[...] = jnp.broadcast_to(taxon_part, (8, lanes))
    lch_r[ch] = jnp.broadcast_to(taxon_part, (8, lanes))

    def loss_push(step):
        return push(
            lch_s, lch_r.at[ch], sem_x.at[8 + step], sem_x.at[2], me, lax.rem(ch + step, groups)
        )

    for step in range(1, groups):
        loss_push(step).start()

    def fill(j, carry):
        rs_s[2 * j] = par_b[j, 0:half_rows, :].astype(BF16)
        rs_s[2 * j + 1] = par_b[j, half_rows:payload, :].astype(BF16)
        return carry

    lax.fori_loop(0, col_tiles, fill, 0)

    def scatter(step, carry):
        to = lax.rem(me + step, peers)
        push(rs_s.at[to], rs_r.at[me], sem_x.at[3], sem_x.at[4], to, ch).start()
        return carry

    pltpu.make_async_copy(rs_s.at[me], rs_r.at[me], sem_x.at[4]).start()
    lax.fori_loop(1, peers, scatter, 0)

    def finish(c, carry):
        drain(brecv_b.at[c], sem_br.at[c])

        def body(u, inner):
            local = pl.ds(pl.multiple_of(u * pair_lanes, pair_lanes), pair_lanes)
            cols = pl.ds(pl.multiple_of(c * width + u * pair_lanes, pair_lanes), pair_lanes)
            got = brecv_b[c, :, :, local].reshape(slots, pair_lanes)
            back = jnp.dot(return_m[...], got, preferred_element_type=F32).astype(BF16)
            qg_ref[:, cols] = back[0:rows]
            kg_ref[:, cols] = back[rows : 2 * rows]
            vg_ref[:, cols] = back[2 * rows : 3 * rows]
            return inner

        lax.fori_loop(0, pairs, body, 0)
        return carry

    lax.fori_loop(0, chunks - 1, finish, 0)

    if groups > 1:
        drain(lch_r.at[0 : groups - 1], sem_x.at[2])
    total = lch_r[0]
    for g in range(1, groups):
        total = total + lch_r[g]
    lct_s[...] = total
    lct_r[me] = total

    def share_loss(step, carry):
        to = lax.rem(me + step, peers)
        push(lct_s, lct_r.at[me], sem_x.at[5], sem_x.at[6], to, ch).start()
        return carry

    lax.fori_loop(1, peers, share_loss, 0)

    drain(rs_r, sem_x.at[4])

    def add(j, summed):
        return summed + rs_r[j].astype(F32)

    ag_s[...] = lax.fori_loop(1, peers, add, rs_r[0].astype(F32)).astype(BF16)

    def gather(step, carry):
        to = lax.rem(me + step, peers)
        push(ag_s, ag_r.at[me], sem_x.at[7], sem_x.at[8], to, ch).start()
        return carry

    pltpu.make_async_copy(ag_s, ag_r.at[me], sem_x.at[8]).start()
    lax.fori_loop(1, peers, gather, 0)

    finish(chunks - 1, 0)
    drain(lct_r.at[0 : peers - 1], sem_x.at[6])

    def add_loss(j, summed):
        return summed + lct_r[j]

    loss_ref[...] = lax.fori_loop(1, peers, add_loss, lct_r[0])
    drain(ag_r, sem_x.at[8])

    def emit(j, carry):
        cols = pl.ds(pl.multiple_of(j * lanes, lanes), lanes)
        par_b[j, 0:half_rows, :] = ag_r[2 * j].astype(F32)
        par_b[j, half_rows:payload, :] = ag_r[2 * j + 1].astype(F32)
        fg_ref[:, cols] = par_b[j, 0:taps, :]
        for s in range(3):
            sg_ref[s, :, cols] = par_b[
                j, taps + s * short_taps : taps + (s + 1) * short_taps, :
            ]
        return carry

    lax.fori_loop(0, col_tiles, emit, 0)

    drain(meta_s.at[0:peers], sem_ms.at[0])
    for step in range(1, groups):
        loss_push(step).wait_send()
    drain(rs_s.at[0 : peers - 1], sem_x.at[3])
    drain(lct_r.at[0 : peers - 1], sem_x.at[5])
    drain(ag_r.at[0 : peers - 1], sem_x.at[7])

    def sent(c, carry):
        drain(send_b.at[c, 0:peers], sem_as.at[c])
        drain(bsend_b.at[c, 0:peers], sem_bs.at[c])
        return carry

    lax.fori_loop(0, chunks, sent, 0)


def shards(
    query_in,
    key_in,
    value_in,
    row_place,
    short_weight,
    long_filter,
    target,
    taxon_ids,
    taxon_weight,
):
    rows, channels = query_in.shape
    peers = lax.axis_size("ctx")
    groups = lax.axis_size("ch")
    taps = long_filter.shape[0]
    short_taps = short_weight.shape[1]
    width = channels // chunks
    col_tiles = channels // lanes
    tiles = width // lanes
    blocks = peers + 1
    slots = blocks * block_rows
    ext = rows + edge
    span = taps + ext
    payload = payload_rows(taps, short_taps)
    half_rows = payload // 2
    tables = []
    made = dft_tables(rows, taps)
    for name in table_names:
        high, low = split_constant(made[name])
        tables.append(jnp.asarray(high))
        tables.append(jnp.asarray(low))
    vm = pltpu.VMEM
    dma = pltpu.SemaphoreType.DMA
    shape = jax.ShapeDtypeStruct
    scratch = [
        vm((slots, 3 * rows), BF16),
        vm((3 * rows, slots), BF16),
        vm((slots, 3 * rows), BF16),
        vm((3 * rows, slots), BF16),
        vm((chunks, blocks, block_rows, width), BF16),
        vm((chunks, blocks, block_rows, width), BF16),
        vm((blocks, block_rows, lanes), BF16),
        vm((blocks, block_rows, lanes), BF16),
        vm((chunks, blocks, block_rows, width), BF16),
        vm((chunks, blocks, block_rows, width), BF16),
        vm((3, col_tiles, rows + 2 * edge, lanes), F32),
        vm((chunks, 3, tiles, edge, lanes), BF16),
        vm((chunks, 3, tiles, edge, lanes), BF16),
        vm((chunks, 2, tiles, edge, lanes), BF16),
        vm((chunks, 2, tiles, edge, lanes), BF16),
        vm((edge, channels), BF16),
        vm((edge, channels), BF16),
        vm((edge, lanes), F32),
        vm((edge, lanes), F32),
        vm((col_tiles, rows, lanes), F32),
        vm((col_tiles, ext, lanes), F32),
        vm((col_tiles, ext, lanes), F32),
        vm((col_tiles, ext, lanes), F32),
        vm((col_tiles, span, lanes), BF16),
        vm((col_tiles, span, lanes), BF16),
        vm((col_tiles, 2 * rows, lanes), F32),
        vm((3, 8, channels), F32),
        vm((3, ext, lanes), F32),
        vm((3 * rows, 2 * lanes), BF16),
        vm((rows, lanes), F32),
        vm((col_tiles, payload, lanes), F32),
        vm((2 * col_tiles, half_rows, lanes), BF16),
        vm((peers, half_rows, lanes), BF16),
        vm((half_rows, lanes), BF16),
        vm((peers, half_rows, lanes), BF16),
        vm((8, lanes), F32),
        vm((groups, 8, lanes), F32),
        vm((8, lanes), F32),
        vm((peers, 8, lanes), F32),
        dma((chunks,)),
        dma((chunks,)),
        dma((chunks,)),
        dma((chunks,)),
        dma((chunks,)),
        dma((chunks,)),
        dma((chunks,)),
        dma((chunks,)),
        dma((2 * chunks,)),
        dma((2 * chunks,)),
        dma((1,)),
        dma((1,)),
        dma((16,)),
    ]
    inputs = (
        query_in,
        key_in,
        value_in,
        row_place.reshape(1, rows),
        jnp.tile(row_place, 3).reshape(1, 3 * rows),
        short_weight,
        long_filter,
        target,
        taxon_ids.reshape(1, rows),
        taxon_weight.reshape(1, -1),
        *tables,
    )
    gated_out, query_grad, key_grad, value_grad, filter_grad, short_grad, losses = pl.pallas_call(
        lambda *refs: whole_kernel(peers, groups, *refs),
        out_shape=(
            shape((rows, channels), BF16),
            shape((rows, channels), BF16),
            shape((rows, channels), BF16),
            shape((rows, channels), BF16),
            shape((taps, channels), F32),
            shape((3, short_taps, channels), F32),
            shape((8, lanes), F32),
        ),
        in_specs=[pl.BlockSpec(memory_space=pltpu.VMEM)] * len(inputs),
        out_specs=[pl.BlockSpec(memory_space=pltpu.VMEM)] * 7,
        scratch_shapes=scratch,
        compiler_params=pltpu.CompilerParams(
            collective_id=0, has_side_effects=True, vmem_limit_bytes=63_000_000
        ),
        name="hyena",
    )(*inputs)
    return (
        gated_out,
        query_grad,
        key_grad,
        value_grad,
        filter_grad,
        short_grad,
        losses[0, : taxon_weight.shape[0]],
    )


def solution(mesh):
    placed = (
        P("ctx", "ch"),
        P("ctx", "ch"),
        P("ctx", "ch"),
        P("ctx"),
        P(None, None, "ch"),
        P(None, "ch"),
        P("ctx", "ch"),
        P("ctx"),
        P(),
    )
    return jax.shard_map(
        shards,
        mesh=mesh,
        in_specs=placed,
        out_specs=(
            P("ctx", "ch"),
            P("ctx", "ch"),
            P("ctx", "ch"),
            P("ctx", "ch"),
            P(None, "ch"),
            P(None, None, "ch"),
            P(),
        ),
        check_vma=False,
    )
```

```python
import math

import jax
import jax.numpy as jnp
import numpy as np
from jax import lax
from jax.experimental import pallas as pl
from jax.experimental.pallas import tpu as pltpu
from jax.sharding import PartitionSpec as P

MESH = pl.DeviceIdType.MESH
F32 = jnp.float32
BF16 = jnp.bfloat16
unit = 5
block_rows = 16
lanes = 128
edge = 16
chunks = 4
stream_step = 1024.0


def split_constant(array):
    high = array.astype(np.float32).astype(jnp.bfloat16)
    low = (array - high.astype(np.float64)).astype(np.float32).astype(jnp.bfloat16)
    return high, low


def dft_tables(rows, taps):
    half = rows
    size = 2 * rows
    span = taps + rows + edge
    theta = np.pi * (2 * np.arange(half) + 1) / size

    def ahead(index):
        angle = theta[:, None] * index[None, :]
        return np.concatenate([np.cos(angle), -np.sin(angle)], axis=0)

    def back(index):
        angle = theta[None, :] * index[:, None]
        return np.concatenate([np.cos(angle), -np.sin(angle)], axis=1) * (2.0 / size)

    tables = {
        "ahead": ahead(np.arange(span)),
        "own": ahead(np.arange(rows)),
        "later": ahead(np.arange(rows, rows + taps + edge)),
        "taps": ahead(np.arange(taps)),
        "mixed": back(np.arange(rows + edge) + taps),
        "gated": back(np.arange(rows + edge)),
        "filter": back(taps - np.arange(taps)),
    }
    return tables


table_names = ("taps", "ahead", "own", "later", "mixed", "gated", "filter")


def payload_rows(taps, short_taps):
    return -(-(taps + 3 * short_taps) // 32) * 32


def iota(shape, axis):
    return lax.broadcasted_iota(jnp.int32, shape, axis)


def slot_facts(index):
    block = lax.shift_right_logical(index, 4)
    row = jnp.bitwise_and(index, block_rows - 1)
    stream = jnp.where(row >= unit, 1, 0) + jnp.where(row >= 2 * unit, 1, 0)
    rank = row - unit * stream
    valid = row < 3 * unit
    return block, stream, rank, valid


def whole_kernel(
    peers,
    groups,
    place_ref,
    taxon_ref,
    weight_ref,
    short_ref,
    *refs,
):
    far = refs[:19]
    out_hbm, brecv_b, return_hbm, ag_r, loss_ref = refs[19:24]
    near = refs[24:43]
    (
        q_ref,
        k_ref,
        v_ref,
        target_ref,
        filter_ref,
        taps_hi,
        taps_lo,
        ahead_hi,
        ahead_lo,
        own_hi,
        own_lo,
        later_hi,
        later_lo,
        mixed_hi,
        mixed_lo,
        gated_hi,
        gated_lo,
        filter_hi,
        filter_lo,
    ) = near
    sem_in = refs[43]
    (
        out_ref,
        pack_m,
        unpack_m,
        place_m,
        return_m,
        send_b,
        recv_b,
        meta_s,
        meta_r,
        bsend_b,
        rows_b,
        prev_s,
        prev_r,
        next_s,
        next_r,
        tnext_s,
        tnext_r,
        wnext_s,
        wnext_r,
        qc_b,
        kc_b,
        vc_b,
        go_b,
        gext_b,
        gm_b,
        spec_b,
        short_b,
        gbuf,
        gr_b,
        lacc,
        par_b,
        rs_s,
        rs_r,
        ag_s,
        lch_s,
        lch_r,
        lct_s,
        lct_r,
        sem_as,
        sem_ar,
        sem_bs,
        sem_br,
        sem_ps,
        sem_pr,
        sem_ns,
        sem_nr,
        sem_gs,
        sem_gr,
        sem_ms,
        sem_mr,
        sem_rs,
        sem_rr,
        sem_out,
        sem_x,
    ) = refs[44:]
    rows, channels = q_ref.shape
    taps = filter_ref.shape[0]
    short_taps = short_ref.shape[1]
    width = channels // chunks
    col_tiles = channels // lanes
    tiles = width // lanes
    pairs = tiles // 2
    blocks = peers + 1
    slots = blocks * block_rows
    ext = rows + edge
    payload = payload_rows(taps, short_taps)
    share = peers // chunks
    half_rows = payload // 2
    me = lax.axis_index("ctx")
    ch = lax.axis_index("ch")
    right = lax.rem(me + 1, peers)
    left = lax.rem(me + peers - 1, peers)
    grad_scale = 1.0 / math.sqrt(rows * peers)
    loss_scale = 1.0 / math.sqrt(channels * groups * rows * peers / weight_ref.shape[1])

    barrier = pltpu.get_barrier_semaphore()

    def greet(step, carry):
        pl.semaphore_signal(
            barrier, inc=1, device_id=(lax.rem(me + step, peers), ch), device_id_type=MESH
        )
        return carry

    lax.fori_loop(1, peers, greet, 0)
    for step in range(1, groups):
        pl.semaphore_signal(
            barrier, inc=1, device_id=(me, lax.rem(ch + step, groups)), device_id_type=MESH
        )

    def fetch(index):
        return pltpu.make_async_copy(far[index], near[index], sem_in.at[index])

    for index in range(len(far)):
        fetch(index).start()

    def push(src, dst, send_sem, recv_sem, ctx_to, ch_to):
        return pltpu.make_async_remote_copy(
            src_ref=src,
            dst_ref=dst,
            send_sem=send_sem,
            recv_sem=recv_sem,
            device_id=(ctx_to, ch_to),
            device_id_type=MESH,
        )

    def drain(ref, sem):
        pltpu.make_async_copy(ref, ref, sem).wait()

    def column(row_vector, count):
        eye = iota((count, count), 0) == iota((count, count), 1)
        return jnp.sum(jnp.where(eye, row_vector, 0.0), axis=1, keepdims=True)

    place_row = place_ref[...].astype(F32)
    place3_row = jnp.concatenate([place_row] * 3, axis=1)
    owner_row = jnp.floor((place_row + 0.5) * (1.0 / rows))
    owner3_row = jnp.floor((place3_row + 0.5) * (1.0 / rows))
    owner_col = column(owner_row, rows)
    place_col = column(place_row, rows)
    local_col = place_col - owner_col * rows

    def slot_key(owner, rank):
        return jnp.where(
            rank < unit - 0.5, owner * unit + rank, float(peers * unit) + rank - unit
        )

    order3 = iota((rows, 3 * rows), 1)
    stream3 = jnp.where(order3 >= rows, 1, 0) + jnp.where(order3 >= 2 * rows, 1, 0)
    before3 = iota((rows, 3 * rows), 0) < order3 - rows * stream3
    rank3_row = jnp.sum(
        jnp.where(jnp.logical_and(owner_col == owner3_row, before3), 1.0, 0.0),
        axis=0,
        keepdims=True,
    )
    key3_row = slot_key(owner3_row, rank3_row)
    before = iota((rows, rows), 1) < iota((rows, rows), 0)
    rank_col = jnp.sum(
        jnp.where(jnp.logical_and(owner_col == owner_row, before), 1.0, 0.0),
        axis=1,
        keepdims=True,
    )
    key_col = slot_key(owner_col, rank_col)

    lane3 = iota((1, 3 * rows), 1)
    lane_stream = jnp.where(lane3 >= rows, 1, 0) + jnp.where(lane3 >= 2 * rows, 1, 0)
    lane_local = lane3 - rows * lane_stream

    def static_key(shape, axis):
        block, stream, rank, valid = slot_facts(iota(shape, axis))
        key = jnp.where(valid, stream * 1024 + block * unit + rank, -1)
        return key.astype(F32), jnp.where(valid, stream * 1024, -4096).astype(F32)

    slot_key_col, slot_stream_col = static_key((slots, 1), 0)
    slot_key_row, slot_stream_row = static_key((1, slots), 1)
    full3_row = key3_row + lane_stream.astype(F32) * stream_step
    pack_m[...] = jnp.where(slot_key_col == full3_row, 1.0, 0.0).astype(BF16)
    meta_col = jnp.broadcast_to(local_col + 1.0, (rows, lanes)).astype(BF16)
    meta3 = jnp.concatenate([meta_col] * 3, axis=0)
    meta_s[...] = (
        jnp.dot(pack_m[...], meta3, preferred_element_type=F32)
        .astype(BF16)
        .reshape(blocks, block_rows, lanes)
    )

    pair_lanes = 2 * lanes

    def pack(c, carry):
        def body(u, inner):
            base = pl.multiple_of(c * width + u * pair_lanes, pair_lanes)
            cols = pl.ds(base, pair_lanes)
            stacked = jnp.concatenate([q_ref[:, cols], k_ref[:, cols], v_ref[:, cols]], axis=0)
            packed = jnp.dot(pack_m[...], stacked, preferred_element_type=F32).astype(BF16)
            local = pl.ds(pl.multiple_of(u * pair_lanes, pair_lanes), pair_lanes)
            send_b[c, :, :, local] = packed.reshape(blocks, block_rows, pair_lanes)
            return inner

        lax.fori_loop(0, pairs, body, 0)
        return carry

    wait_for = peers - 1 + groups - 1

    def exchange(source, landing, send_sem, recv_sem):
        pltpu.make_async_copy(source.at[me], landing.at[me], recv_sem).start()
        push(source.at[peers], landing.at[peers], send_sem, recv_sem, right, ch).start()

        def body(step, carry):
            to = lax.rem(me + step, peers)
            push(source.at[to], landing.at[me], send_sem, recv_sem, to, ch).start()
            return carry

        lax.fori_loop(1, peers, body, 0)

    def exchange_back(source, landing, send_sem, recv_sem):
        pltpu.make_async_copy(source.at[me], landing.at[me], recv_sem).start()
        push(source.at[peers], landing.at[peers], send_sem, recv_sem, left, ch).start()

        def body(step, carry):
            to = lax.rem(me + step, peers)
            push(source.at[to], landing.at[me], send_sem, recv_sem, to, ch).start()
            return carry

        lax.fori_loop(1, peers, body, 0)

    for index in range(3):
        fetch(index).wait()
    pack(0, 0)
    pl.semaphore_wait(barrier, wait_for)
    exchange(meta_s, meta_r, sem_ms.at[0], sem_mr.at[0])
    target_push = push(tnext_s, tnext_r, sem_x.at[0], sem_x.at[1], left, ch)
    weight_push = push(wnext_s, wnext_r, sem_x.at[12], sem_x.at[13], left, ch)
    exchange(send_b.at[0], recv_b.at[0], sem_as.at[0], sem_ar.at[0])

    def pack_and_send(c, carry):
        pack(c, 0)
        exchange(send_b.at[c], recv_b.at[c], sem_as.at[c], sem_ar.at[c])
        return carry

    lax.fori_loop(1, chunks, pack_and_send, 0)
    fetch(3).wait()
    ids_row = taxon_ref[...].astype(F32)
    ids_col = column(ids_row, rows)
    count = weight_ref.shape[1]
    taxon_hot = iota((rows, lanes), 1).astype(F32) == ids_col
    weights = jnp.concatenate([weight_ref[...], jnp.zeros((1, lanes - count), F32)], axis=1)
    weight_col = jnp.sum(jnp.where(taxon_hot, weights, 0.0), axis=1, keepdims=True)
    tnext_s[...] = target_ref[0:edge, :]
    wnext_s[...] = jnp.broadcast_to(weight_col[0:edge], (edge, lanes))
    target_push.start()
    weight_push.start()
    for s in range(3):
        return_m[s * rows : (s + 1) * rows, :] = jnp.where(
            key_col + s * stream_step == slot_key_row, 1.0, 0.0
        ).astype(BF16)

    return_copy = pltpu.make_async_copy(return_m, return_hbm, sem_x.at[14])
    return_copy.start()
    for index in range(4, len(far)):
        fetch(index).wait()

    short_b[:, 0:short_taps, :] = short_ref[...].astype(F32)

    def filter_spectrum(u, carry):
        cols = pl.ds(pl.multiple_of(u * pair_lanes, pair_lanes), pair_lanes)
        x = filter_ref[:, cols]
        found = jnp.dot(taps_hi[...], x, preferred_element_type=F32) + jnp.dot(
            taps_lo[...], x, preferred_element_type=F32
        )
        spec_b[2 * u] = found[:, :lanes]
        spec_b[2 * u + 1] = found[:, lanes:]
        return carry

    lax.fori_loop(0, col_tiles // 2, filter_spectrum, 0)
    lacc[...] = jnp.zeros_like(lacc)
    par_b[...] = jnp.zeros_like(par_b)

    drain(meta_r, sem_mr.at[0])
    meta = meta_r[...].reshape(slots, lanes)
    pick = jnp.where(iota((8, lanes), 1) == 0, 1.0, 0.0).astype(BF16)
    found_row = lax.dot_general(
        pick, meta, (((1,), (1,)), ((), ())), preferred_element_type=F32
    )[0:1, :]
    landed_row = found_row + slot_stream_row
    landed_col = meta[:, 0:1].astype(F32) + slot_stream_col
    target_lane = (lane_local + 1).astype(F32) + lane_stream.astype(F32) * stream_step
    place_m[...] = jnp.where(landed_col == target_lane, 1.0, 0.0).astype(BF16)
    own_index = (iota((rows, 1), 0) + 1).astype(F32)
    for s in range(3):
        unpack_m[s * rows : (s + 1) * rows, :] = jnp.where(
            own_index + s * stream_step == landed_row, 1.0, 0.0
        ).astype(BF16)
    target_push.wait()
    weight_push.wait()
    not_first = jnp.where(me > 0, 1.0, 0.0)
    not_last = jnp.where(me < peers - 1, 1.0, 0.0)

    def tile_range(c):
        return pl.ds(c * tiles, tiles)

    def prev_push(c):
        return push(prev_s.at[c], prev_r.at[c], sem_ps.at[c], sem_pr.at[c], right, ch)

    def next_push(c):
        return push(next_s.at[c], next_r.at[c], sem_ns.at[c], sem_nr.at[c], left, ch)

    def gated_push(c):
        return push(
            gext_b.at[tile_range(c), taps_at : taps_at + taps, :],
            gext_b.at[tile_range(c), 0:taps, :],
            sem_gs.at[c],
            sem_gr.at[c],
            right,
            ch,
        )

    taps_at = rows

    def mixed_push(c):
        return push(
            gm_b.at[tile_range(c), 0 : taps + edge, :],
            gm_b.at[tile_range(c), rows : rows + taps + edge, :],
            sem_gs.at[chunks + c],
            sem_gr.at[chunks + c],
            left,
            ch,
        )

    def land(c):
        drain(recv_b.at[c], sem_ar.at[c])

        def body(u, carry):
            local = pl.ds(pl.multiple_of(u * pair_lanes, pair_lanes), pair_lanes)
            got = recv_b[c, :, :, local].reshape(slots, pair_lanes)
            placed = jnp.dot(unpack_m[...], got, preferred_element_type=F32)
            for part in range(2):
                at = c * tiles + 2 * u + part
                piece = placed[:, part * lanes : (part + 1) * lanes]
                for s in range(3):
                    rows_b[s, at, edge : edge + rows, :] = piece[s * rows : (s + 1) * rows]
                    prev_s[c, s, 2 * u + part] = piece[
                        (s + 1) * rows - edge : (s + 1) * rows
                    ].astype(BF16)
                    if s > 0:
                        next_s[c, s - 1, 2 * u + part] = piece[
                            s * rows : s * rows + edge
                        ].astype(BF16)
            return carry

        lax.fori_loop(0, pairs, body, 0)
        prev_push(c).start()
        next_push(c).start()

    def convolve(c):
        prev_push(c).wait()
        next_push(c).wait()

        def body(u, carry):
            at = c * tiles + u
            cols = pl.ds(pl.multiple_of(at * lanes, lanes), lanes)
            for s in range(3):
                rows_b[s, at, 0:edge, :] = prev_r[c, s, u].astype(F32) * not_first
            for s in range(2):
                rows_b[s + 1, at, edge + rows : 2 * edge + rows, :] = next_r[c, s, u].astype(F32)

            def conv(s, total):
                summed = None
                for j in range(short_taps):
                    term = (
                        short_b[s, j : j + 1, cols]
                        * rows_b[s, at, edge - j : edge - j + total, :]
                    )
                    summed = term if summed is None else summed + term
                return summed

            k_conv = conv(1, ext)
            v_conv = conv(2, ext)
            kc_b[at] = k_conv
            vc_b[at] = v_conv
            gext_b[at, taps : taps + ext, :] = (k_conv * v_conv).astype(BF16)
            q_conv = conv(0, rows)
            qc_b[at] = q_conv
            out_grad = weight_col[0:rows] * target_ref[:, cols].astype(F32)
            go_b[at, 0:rows, :] = out_grad
            go_b[at, rows:ext, :] = (
                wnext_r[...] * tnext_r[:, cols].astype(F32) * not_last
            )
            gm_b[at, 0:rows, :] = (out_grad * q_conv).astype(BF16)
            return carry

        lax.fori_loop(0, tiles, body, 0)
        gated_push(c).start()
        mixed_push(c).start()

    def both(high, low, x):
        return jnp.dot(high, x, preferred_element_type=F32) + jnp.dot(
            low, x, preferred_element_type=F32
        )

    def inverse(high, low, real, imag):
        y = jnp.concatenate([real, imag], axis=0)
        y_hi = y.astype(BF16)
        y_lo = (y - y_hi.astype(F32)).astype(BF16)
        return both(high[...], low[...], y_hi) + jnp.dot(
            high[...], y_lo, preferred_element_type=F32
        )

    def backward(c):
        gated_push(c).wait()
        mixed_push(c).wait()

        @pl.when(me == 0)
        def _():
            def clear(u, carry):
                gext_b[c * tiles + u, 0:taps, :] = jnp.zeros((taps, lanes), BF16)
                return carry

            lax.fori_loop(0, tiles, clear, 0)

        @pl.when(me == peers - 1)
        def _():
            def clear(u, carry):
                gm_b[c * tiles + u, rows : rows + taps + edge, :] = jnp.zeros(
                    (taps + edge, lanes), BF16
                )
                return carry

            lax.fori_loop(0, tiles, clear, 0)

        def body(u, carry):
            first = c * tiles + 2 * u
            gx = jnp.concatenate([gext_b[first], gext_b[first + 1]], axis=1)
            g_own = jnp.concatenate(
                [gm_b[first, 0:rows, :], gm_b[first + 1, 0:rows, :]], axis=1
            )
            g_later = jnp.concatenate(
                [
                    gm_b[first, rows : rows + taps + edge, :],
                    gm_b[first + 1, rows : rows + taps + edge, :],
                ],
                axis=1,
            )
            spec = jnp.concatenate([spec_b[first], spec_b[first + 1]], axis=1)
            fr, fi = spec[:rows], spec[rows:]
            sg = both(ahead_hi[...], ahead_lo[...], gx)
            gr, gi = sg[:rows], sg[rows:]
            mixed = inverse(mixed_hi, mixed_lo, fr * gr - fi * gi, fr * gi + fi * gr)
            so = both(own_hi[...], own_lo[...], g_own)
            mr, mi = so[:rows], so[rows:]
            taps_grad = inverse(filter_hi, filter_lo, mr * gr + mi * gi, mr * gi - mi * gr)
            sl = both(later_hi[...], later_lo[...], g_later)
            ar, ai = mr + sl[:rows], mi + sl[rows:]
            gated_grad = inverse(gated_hi, gated_lo, fr * ar + fi * ai, fr * ai - fi * ar)
            for part in range(2):
                at = first + part
                cols = pl.ds(pl.multiple_of(at * lanes, lanes), lanes)
                lane_cut = slice(part * lanes, (part + 1) * lanes)
                mix = mixed[:, lane_cut]
                gg = gated_grad[:, lane_cut]
                found_taps = taps_grad[:, lane_cut].astype(BF16)
                rs_s[2 * at] = found_taps[0:half_rows]
                rs_s[2 * at + 1, 0 : taps - half_rows, :] = found_taps[half_rows:]
                out = (qc_b[at] * mix[:rows]).astype(BF16)
                out_ref[:, cols] = out
                lacc[...] += out.astype(F32) * target_ref[:, cols].astype(F32)
                gbuf[0] = go_b[at] * mix
                gbuf[1] = gg * vc_b[at]
                gbuf[2] = gg * kc_b[at]
                for s in range(3):
                    own = gbuf[s, 0:rows, :]
                    back = None
                    for j in range(short_taps):
                        found = jnp.sum(
                            own * rows_b[s, at, edge - j : edge - j + rows, :],
                            axis=0,
                            keepdims=True,
                        )
                        par_b[s * short_taps + j : s * short_taps + j + 1, :] = found
                        term = short_b[s, j : j + 1, cols] * gbuf[s, j : j + rows, :]
                        back = term if back is None else back + term
                    gr_b[s * rows : (s + 1) * rows, lane_cut] = back.astype(BF16)
                rs_s[2 * at + 1, taps - half_rows : half_rows, :] = par_b[...].astype(BF16)
            local = pl.ds(pl.multiple_of(u * pair_lanes, pair_lanes), pair_lanes)
            packed = jnp.dot(place_m[...], gr_b[...], preferred_element_type=F32).astype(BF16)
            bsend_b[c, :, :, local] = packed.reshape(blocks, block_rows, pair_lanes)
            return carry

        lax.fori_loop(0, pairs, body, 0)
        out_copy(c).start()

        def scatter(i, carry):
            piece = c * share + i

            @pl.when(piece == me)
            def _():
                pltpu.make_async_copy(rs_s.at[piece], rs_r.at[me], sem_rr.at[0]).start()

            @pl.when(piece != me)
            def _():
                push(rs_s.at[piece], rs_r.at[me], sem_rs.at[0], sem_rr.at[0], piece, ch).start()

            return carry

        lax.fori_loop(0, share, scatter, 0)
        exchange_back(bsend_b.at[c], brecv_b.at[c], sem_bs.at[c], sem_br.at[c])

    def reduce(c):
        @pl.when(me // share == c)
        def _():
            drain(rs_r, sem_rr.at[0])

            def add(j, summed):
                return summed + rs_r[j].astype(F32)

            summed = lax.fori_loop(1, peers, add, rs_r[0].astype(F32))
            ag_s[...] = (summed * grad_scale).astype(BF16)

            def gather(step, carry):
                to = lax.rem(me + step, peers)
                push(ag_s, ag_r.at[me], sem_rs.at[1], sem_rr.at[1], to, ch).start()
                return carry

            pltpu.make_async_copy(ag_s, ag_r.at[me], sem_rr.at[1]).start()
            lax.fori_loop(1, peers, gather, 0)

    def out_copy(c):
        cols = pl.ds(pl.multiple_of(c * width, width), width)
        return pltpu.make_async_copy(out_ref.at[:, cols], out_hbm.at[:, cols], sem_out.at[c])

    def steps(t, carry):
        @pl.when(t < chunks)
        def _():
            land(t)

        @pl.when(jnp.logical_and(t >= 1, t < chunks + 1))
        def _():
            convolve(t - 1)

        @pl.when(t >= 2)
        def _():
            backward(t - 2)

        @pl.when(t >= 3)
        def _():
            reduce(t - 3)

        return carry

    lax.fori_loop(0, chunks + 2, steps, 0)

    row_loss = jnp.sum(lacc[...], axis=1, keepdims=True)
    taxon_part = (
        jnp.sum(jnp.where(taxon_hot[0:rows], row_loss, 0.0), axis=0, keepdims=True) * loss_scale
    )
    lch_s[...] = jnp.broadcast_to(taxon_part, (8, lanes))
    lch_r[ch] = jnp.broadcast_to(taxon_part, (8, lanes))

    def loss_push(step):
        return push(
            lch_s, lch_r.at[ch], sem_x.at[8 + step], sem_x.at[2], me, lax.rem(ch + step, groups)
        )

    for step in range(1, groups):
        loss_push(step).start()

    if groups > 1:
        drain(lch_r.at[0 : groups - 1], sem_x.at[2])
    total = lch_r[0]
    for g in range(1, groups):
        total = total + lch_r[g]
    lct_s[...] = total
    lct_r[me] = total

    def share_loss(step, carry):
        to = lax.rem(me + step, peers)
        push(lct_s, lct_r.at[me], sem_x.at[5], sem_x.at[6], to, ch).start()
        return carry

    lax.fori_loop(1, peers, share_loss, 0)

    reduce(chunks - 1)
    drain(lct_r.at[0 : peers - 1], sem_x.at[6])

    def add_loss(j, summed):
        return summed + lct_r[j]

    loss_ref[...] = lax.fori_loop(1, peers, add_loss, lct_r[0])

    def arrived(c, carry):
        drain(brecv_b.at[c], sem_br.at[c])
        out_copy(c).wait()
        return carry

    lax.fori_loop(0, chunks, arrived, 0)
    drain(ag_r, sem_rr.at[1])
    return_copy.wait()

    drain(meta_s.at[0:peers], sem_ms.at[0])
    for step in range(1, groups):
        loss_push(step).wait_send()
    drain(rs_s.at[0 : peers - 1], sem_rs.at[0])
    drain(lct_r.at[0 : peers - 1], sem_x.at[5])
    drain(rs_s.at[0 : peers - 1], sem_rs.at[1])

    def sent(c, carry):
        drain(send_b.at[c, 0:peers], sem_as.at[c])
        drain(bsend_b.at[c, 0:peers], sem_bs.at[c])
        return carry

    lax.fori_loop(0, chunks, sent, 0)


def finish_kernel(return_ref, back_ref, out_in, ag_ref, loss_in, out_ref, qg_ref, kg_ref, vg_ref, fg_ref, sg_ref, loss_ref, par_b):
    rows = out_in.shape[0]
    blocks, cols = back_ref.shape[1], back_ref.shape[3]
    taps, short_taps = fg_ref.shape[0], sg_ref.shape[1]
    half_rows = ag_ref.shape[1]
    got = back_ref[0].reshape(blocks * block_rows, cols)
    back = jnp.dot(return_ref[...], got, preferred_element_type=F32).astype(BF16)
    qg_ref[...] = back[0:rows]
    kg_ref[...] = back[rows : 2 * rows]
    vg_ref[...] = back[2 * rows : 3 * rows]
    out_ref[...] = out_in[...]
    loss_ref[...] = loss_in[0:1, 0 : loss_ref.shape[1]]
    for t in range(cols // lanes):
        cut = slice(t * lanes, (t + 1) * lanes)
        low = ag_ref[2 * t + 1].astype(F32)
        fg_ref[0:half_rows, cut] = ag_ref[2 * t].astype(F32)
        fg_ref[half_rows:taps, cut] = low[0 : taps - half_rows]
        par_b[...] = low[taps - half_rows :]
        for s in range(3):
            sg_ref[s, :, cut] = par_b[s * short_taps : (s + 1) * short_taps, :]


def shards(
    query_in,
    key_in,
    value_in,
    row_place,
    short_weight,
    long_filter,
    target,
    taxon_ids,
    taxon_weight,
):
    rows, channels = query_in.shape
    peers = lax.axis_size("ctx")
    groups = lax.axis_size("ch")
    taps = long_filter.shape[0]
    short_taps = short_weight.shape[1]
    width = channels // chunks
    col_tiles = channels // lanes
    tiles = width // lanes
    blocks = peers + 1
    slots = blocks * block_rows
    ext = rows + edge
    span = taps + ext
    payload = payload_rows(taps, short_taps)
    share = peers // chunks
    half_rows = payload // 2
    tables = []
    made = dft_tables(rows, taps)
    for name in table_names:
        high, low = split_constant(made[name])
        tables.append(jnp.asarray(high))
        tables.append(jnp.asarray(low))
    vm = pltpu.VMEM
    dma = pltpu.SemaphoreType.DMA
    shape = jax.ShapeDtypeStruct
    loaded = (query_in, key_in, value_in, target, long_filter, *tables)
    scratch = [
        *(vm(x.shape, x.dtype) for x in loaded),
        dma((len(loaded),)),
        vm((rows, channels), BF16),
        vm((slots, 3 * rows), BF16),
        vm((3 * rows, slots), BF16),
        vm((slots, 3 * rows), BF16),
        vm((3 * rows, slots), BF16),
        vm((chunks, blocks, block_rows, width), BF16),
        vm((chunks, blocks, block_rows, width), BF16),
        vm((blocks, block_rows, lanes), BF16),
        vm((blocks, block_rows, lanes), BF16),
        vm((chunks, blocks, block_rows, width), BF16),
        vm((3, col_tiles, rows + 2 * edge, lanes), F32),
        vm((chunks, 3, tiles, edge, lanes), BF16),
        vm((chunks, 3, tiles, edge, lanes), BF16),
        vm((chunks, 2, tiles, edge, lanes), BF16),
        vm((chunks, 2, tiles, edge, lanes), BF16),
        vm((edge, channels), BF16),
        vm((edge, channels), BF16),
        vm((edge, lanes), F32),
        vm((edge, lanes), F32),
        vm((col_tiles, rows, lanes), F32),
        vm((col_tiles, ext, lanes), F32),
        vm((col_tiles, ext, lanes), F32),
        vm((col_tiles, ext, lanes), F32),
        vm((col_tiles, span, lanes), BF16),
        vm((col_tiles, span, lanes), BF16),
        vm((col_tiles, 2 * rows, lanes), F32),
        vm((3, 8, channels), F32),
        vm((3, ext, lanes), F32),
        vm((3 * rows, 2 * lanes), BF16),
        vm((rows, lanes), F32),
        vm((payload - taps, lanes), F32),
        vm((peers, half_rows, lanes), BF16),
        vm((peers, half_rows, lanes), BF16),
        vm((half_rows, lanes), BF16),
        vm((8, lanes), F32),
        vm((groups, 8, lanes), F32),
        vm((8, lanes), F32),
        vm((peers, 8, lanes), F32),
        dma((chunks,)),
        dma((chunks,)),
        dma((chunks,)),
        dma((chunks,)),
        dma((chunks,)),
        dma((chunks,)),
        dma((chunks,)),
        dma((chunks,)),
        dma((2 * chunks,)),
        dma((2 * chunks,)),
        dma((1,)),
        dma((1,)),
        dma((2,)),
        dma((2,)),
        dma((chunks,)),
        dma((16,)),
    ]
    here = pl.BlockSpec(memory_space=pltpu.VMEM)
    away = pl.BlockSpec(memory_space=pl.ANY)
    gated_out, brought, returning, gathered, losses = pl.pallas_call(
        lambda *refs: whole_kernel(peers, groups, *refs),
        out_shape=(
            shape((rows, channels), BF16),
            shape((chunks, blocks, block_rows, width), BF16),
            shape((3 * rows, slots), BF16),
            shape((peers, half_rows, lanes), BF16),
            shape((8, lanes), F32),
        ),
        in_specs=[here] * 4 + [away] * len(loaded),
        out_specs=[away] * 4 + [here],
        scratch_shapes=scratch,
        compiler_params=pltpu.CompilerParams(
            collective_id=0, has_side_effects=True, vmem_limit_bytes=63_000_000
        ),
        name="hyena",
    )(
        row_place.reshape(1, rows),
        taxon_ids.reshape(1, rows),
        taxon_weight.reshape(1, -1),
        short_weight,
        *loaded,
    )
    cols = 2 * lanes
    steps = width // cols
    by_cols = lambda i: (0, i)
    count = taxon_weight.shape[0]
    gated_out, query_grad, key_grad, value_grad, filter_grad, short_grad, losses = pl.pallas_call(
        finish_kernel,
        grid=(channels // cols,),
        out_shape=(
            shape((rows, channels), BF16),
            shape((rows, channels), BF16),
            shape((rows, channels), BF16),
            shape((rows, channels), BF16),
            shape((taps, channels), F32),
            shape((3, short_taps, channels), F32),
            shape((1, count), F32),
        ),
        in_specs=[
            pl.BlockSpec((3 * rows, slots), lambda i: (0, 0)),
            pl.BlockSpec(
                (1, blocks, block_rows, cols), lambda i: (i // steps, 0, 0, i % steps)
            ),
            pl.BlockSpec((rows, cols), by_cols),
            pl.BlockSpec((2 * cols // lanes, half_rows, lanes), lambda i: (i, 0, 0)),
            pl.BlockSpec((8, lanes), lambda i: (0, 0)),
        ],
        out_specs=[pl.BlockSpec((rows, cols), by_cols)] * 4
        + [
            pl.BlockSpec((taps, cols), by_cols),
            pl.BlockSpec((3, short_taps, cols), lambda i: (0, 0, i)),
            pl.BlockSpec((1, count), lambda i: (0, 0)),
        ],
        scratch_shapes=[vm((payload - taps, lanes), F32)],
        name="finish",
    )(returning, brought, gated_out, gathered, losses)
    return (
        gated_out,
        query_grad,
        key_grad,
        value_grad,
        filter_grad,
        short_grad,
        losses.reshape(count),
    )


def solution(mesh):
    placed = (
        P("ctx", "ch"),
        P("ctx", "ch"),
        P("ctx", "ch"),
        P("ctx"),
        P(None, None, "ch"),
        P(None, "ch"),
        P("ctx", "ch"),
        P("ctx"),
        P(),
    )
    return jax.shard_map(
        shards,
        mesh=mesh,
        in_specs=placed,
        out_specs=(
            P("ctx", "ch"),
            P("ctx", "ch"),
            P("ctx", "ch"),
            P("ctx", "ch"),
            P(None, "ch"),
            P(None, None, "ch"),
            P(),
        ),
        check_vma=False,
    )
```

```python
import math

import jax
import jax.numpy as jnp
import numpy as np
from jax import lax
from jax.experimental import pallas as pl
from jax.experimental.pallas import tpu as pltpu
from jax.sharding import PartitionSpec as P

MESH = pl.DeviceIdType.MESH
F32 = jnp.float32
BF16 = jnp.bfloat16
unit = 5
block_rows = 16
lanes = 128
edge = 16
chunks = 4
stream_step = 1024.0


def split_constant(array):
    high = array.astype(np.float32).astype(jnp.bfloat16)
    low = (array - high.astype(np.float64)).astype(np.float32).astype(jnp.bfloat16)
    return high, low


def dft_tables(rows, taps):
    half = rows
    size = 2 * rows
    span = taps + rows + edge
    theta = np.pi * (2 * np.arange(half) + 1) / size

    def ahead(index):
        angle = theta[:, None] * index[None, :]
        return np.concatenate([np.cos(angle), -np.sin(angle)], axis=0)

    def back(index):
        angle = theta[None, :] * index[:, None]
        return np.concatenate([np.cos(angle), -np.sin(angle)], axis=1) * (2.0 / size)

    tables = {
        "ahead": ahead(np.arange(span)),
        "own": ahead(np.arange(rows)),
        "later": ahead(np.arange(rows, rows + taps + edge)),
        "taps": ahead(np.arange(taps)),
        "mixed": back(np.arange(rows + edge) + taps),
        "gated": back(np.arange(rows + edge)),
        "filter": back(taps - np.arange(taps)),
    }
    return tables


table_names = ("taps", "ahead", "own", "later", "mixed", "gated", "filter")


def payload_rows(taps, short_taps):
    return -(-(taps + 3 * short_taps) // 32) * 32


def iota(shape, axis):
    return lax.broadcasted_iota(jnp.int32, shape, axis)


def slot_facts(index):
    block = lax.shift_right_logical(index, 4)
    row = jnp.bitwise_and(index, block_rows - 1)
    stream = jnp.where(row >= unit, 1, 0) + jnp.where(row >= 2 * unit, 1, 0)
    rank = row - unit * stream
    valid = row < 3 * unit
    return block, stream, rank, valid


def whole_kernel(
    peers,
    groups,
    place_ref,
    taxon_ref,
    weight_ref,
    short_ref,
    *refs,
):
    far = refs[:19]
    out_hbm, qg_hbm, kg_hbm, vg_hbm, ag_r, loss_ref = refs[19:25]
    near = refs[25:44]
    (
        q_ref,
        k_ref,
        v_ref,
        target_ref,
        filter_ref,
        taps_hi,
        taps_lo,
        ahead_hi,
        ahead_lo,
        own_hi,
        own_lo,
        later_hi,
        later_lo,
        mixed_hi,
        mixed_lo,
        gated_hi,
        gated_lo,
        filter_hi,
        filter_lo,
    ) = near
    sem_in = refs[44]
    (
        out_ref,
        pack_m,
        unpack_m,
        place_m,
        return_m,
        send_b,
        recv_b,
        meta_s,
        meta_r,
        bsend_b,
        brecv_b,
        grads_b,
        rows_b,
        prev_s,
        prev_r,
        next_s,
        next_r,
        tnext_s,
        tnext_r,
        wnext_s,
        wnext_r,
        qc_b,
        kc_b,
        vc_b,
        go_b,
        gext_b,
        gm_b,
        spec_b,
        short_b,
        gbuf,
        gr_b,
        lacc,
        ids_b,
        par_b,
        half_b,
        half_r,
        z_s,
        z_r,
        y_s,
        y_r,
        f_s,
        lch_s,
        lch_r,
        lct_s,
        lct_r,
        sem_as,
        sem_ar,
        sem_bs,
        sem_br,
        sem_ps,
        sem_pr,
        sem_ns,
        sem_nr,
        sem_gs,
        sem_gr,
        sem_ms,
        sem_mr,
        sem_hs,
        sem_hr,
        sem_zs,
        sem_zr,
        sem_ys,
        sem_yr,
        sem_fs,
        sem_fr,
        sem_out,
        sem_x,
    ) = refs[45:]
    rows, channels = q_ref.shape
    taps = filter_ref.shape[0]
    short_taps = short_ref.shape[1]
    width = channels // chunks
    col_tiles = channels // lanes
    tiles = width // lanes
    pairs = tiles // 2
    blocks = peers + 1
    slots = blocks * block_rows
    ext = rows + edge
    payload = payload_rows(taps, short_taps)
    half_rows = payload // 2
    me = lax.axis_index("ctx")
    depth = tiles
    breadth = peers // (2 * depth)
    core = lax.rem(me, 2)
    my_y = lax.rem(me // 2, breadth)
    my_z = me // (2 * breadth)
    partner = me + 1 - 2 * core
    ch = lax.axis_index("ch")
    right = lax.rem(me + 1, peers)
    left = lax.rem(me + peers - 1, peers)
    grad_scale = 1.0 / math.sqrt(rows * peers)
    loss_scale = 1.0 / math.sqrt(channels * groups * rows * peers / weight_ref.shape[1])

    barrier = pltpu.get_barrier_semaphore()

    def greet(step, carry):
        pl.semaphore_signal(
            barrier, inc=1, device_id=(lax.rem(me + step, peers), ch), device_id_type=MESH
        )
        return carry

    lax.fori_loop(1, peers, greet, 0)
    for step in range(1, groups):
        pl.semaphore_signal(
            barrier, inc=1, device_id=(me, lax.rem(ch + step, groups)), device_id_type=MESH
        )

    def fetch(index):
        return pltpu.make_async_copy(far[index], near[index], sem_in.at[index])

    for index in range(len(far)):
        fetch(index).start()

    def push(src, dst, send_sem, recv_sem, ctx_to, ch_to):
        return pltpu.make_async_remote_copy(
            src_ref=src,
            dst_ref=dst,
            send_sem=send_sem,
            recv_sem=recv_sem,
            device_id=(ctx_to, ch_to),
            device_id_type=MESH,
        )

    def drain(ref, sem):
        pltpu.make_async_copy(ref, ref, sem).wait()

    def column(row_vector, count):
        eye = iota((count, count), 0) == iota((count, count), 1)
        return jnp.sum(jnp.where(eye, row_vector, 0.0), axis=1, keepdims=True)

    place_row = place_ref[...].astype(F32)
    place3_row = jnp.concatenate([place_row] * 3, axis=1)
    owner_row = jnp.floor((place_row + 0.5) * (1.0 / rows))
    owner3_row = jnp.floor((place3_row + 0.5) * (1.0 / rows))
    owner_col = column(owner_row, rows)
    place_col = column(place_row, rows)
    local_col = place_col - owner_col * rows

    def slot_key(owner, rank):
        return jnp.where(
            rank < unit - 0.5, owner * unit + rank, float(peers * unit) + rank - unit
        )

    order3 = iota((rows, 3 * rows), 1)
    stream3 = jnp.where(order3 >= rows, 1, 0) + jnp.where(order3 >= 2 * rows, 1, 0)
    before3 = iota((rows, 3 * rows), 0) < order3 - rows * stream3
    rank3_row = jnp.sum(
        jnp.where(jnp.logical_and(owner_col == owner3_row, before3), 1.0, 0.0),
        axis=0,
        keepdims=True,
    )
    key3_row = slot_key(owner3_row, rank3_row)
    before = iota((rows, rows), 1) < iota((rows, rows), 0)
    rank_col = jnp.sum(
        jnp.where(jnp.logical_and(owner_col == owner_row, before), 1.0, 0.0),
        axis=1,
        keepdims=True,
    )
    key_col = slot_key(owner_col, rank_col)

    lane3 = iota((1, 3 * rows), 1)
    lane_stream = jnp.where(lane3 >= rows, 1, 0) + jnp.where(lane3 >= 2 * rows, 1, 0)
    lane_local = lane3 - rows * lane_stream

    def static_key(shape, axis):
        block, stream, rank, valid = slot_facts(iota(shape, axis))
        key = jnp.where(valid, stream * 1024 + block * unit + rank, -1)
        return key.astype(F32), jnp.where(valid, stream * 1024, -4096).astype(F32)

    slot_key_col, slot_stream_col = static_key((slots, 1), 0)
    slot_key_row, slot_stream_row = static_key((1, slots), 1)
    full3_row = key3_row + lane_stream.astype(F32) * stream_step
    pack_m[...] = jnp.where(slot_key_col == full3_row, 1.0, 0.0).astype(BF16)
    meta_col = jnp.broadcast_to(local_col + 1.0, (rows, lanes)).astype(BF16)
    meta3 = jnp.concatenate([meta_col] * 3, axis=0)
    meta_s[...] = (
        jnp.dot(pack_m[...], meta3, preferred_element_type=F32)
        .astype(BF16)
        .reshape(blocks, block_rows, lanes)
    )

    pair_lanes = 2 * lanes

    def pack(c, carry):
        def body(u, inner):
            base = pl.multiple_of(c * width + u * pair_lanes, pair_lanes)
            cols = pl.ds(base, pair_lanes)
            stacked = jnp.concatenate([q_ref[:, cols], k_ref[:, cols], v_ref[:, cols]], axis=0)
            packed = jnp.dot(pack_m[...], stacked, preferred_element_type=F32).astype(BF16)
            local = pl.ds(pl.multiple_of(u * pair_lanes, pair_lanes), pair_lanes)
            send_b[c, :, :, local] = packed.reshape(blocks, block_rows, pair_lanes)
            return inner

        lax.fori_loop(0, pairs, body, 0)
        return carry

    wait_for = peers - 1 + groups - 1

    def exchange(source, landing, send_sem, recv_sem):
        pltpu.make_async_copy(source.at[me], landing.at[me], recv_sem).start()
        push(source.at[peers], landing.at[peers], send_sem, recv_sem, right, ch).start()

        def body(step, carry):
            to = lax.rem(me + step, peers)
            push(source.at[to], landing.at[me], send_sem, recv_sem, to, ch).start()
            return carry

        lax.fori_loop(1, peers, body, 0)

    def exchange_back(source, landing, send_sem, recv_sem):
        pltpu.make_async_copy(source.at[me], landing.at[me], recv_sem).start()
        push(source.at[peers], landing.at[peers], send_sem, recv_sem, left, ch).start()

        def body(step, carry):
            to = lax.rem(me + step, peers)
            push(source.at[to], landing.at[me], send_sem, recv_sem, to, ch).start()
            return carry

        lax.fori_loop(1, peers, body, 0)

    for index in range(3):
        fetch(index).wait()
    pack(0, 0)
    pl.semaphore_wait(barrier, wait_for)
    exchange(meta_s, meta_r, sem_ms.at[0], sem_mr.at[0])
    target_push = push(tnext_s, tnext_r, sem_x.at[0], sem_x.at[1], left, ch)
    weight_push = push(wnext_s, wnext_r, sem_x.at[12], sem_x.at[13], left, ch)
    exchange(send_b.at[0], recv_b.at[0], sem_as.at[0], sem_ar.at[0])

    def pack_and_send(c, carry):
        pack(c, 0)
        exchange(send_b.at[c], recv_b.at[c], sem_as.at[c], sem_ar.at[c])
        return carry

    lax.fori_loop(1, chunks, pack_and_send, 0)
    fetch(3).wait()
    ids_row = taxon_ref[...].astype(F32)
    ids_col = column(ids_row, rows)
    count = weight_ref.shape[1]
    taxon_hot = iota((rows, lanes), 1).astype(F32) == ids_col
    weights = jnp.concatenate([weight_ref[...], jnp.zeros((1, lanes - count), F32)], axis=1)
    weight_col = jnp.sum(jnp.where(taxon_hot, weights, 0.0), axis=1, keepdims=True)
    ids_b[...] = jnp.broadcast_to(ids_col, (rows, lanes))
    tnext_s[...] = target_ref[0:edge, :]
    wnext_s[...] = jnp.broadcast_to(weight_col[0:edge], (edge, lanes))
    target_push.start()
    weight_push.start()
    for s in range(3):
        return_m[s * rows : (s + 1) * rows, :] = jnp.where(
            key_col + s * stream_step == slot_key_row, 1.0, 0.0
        ).astype(BF16)

    for index in range(4, len(far)):
        fetch(index).wait()

    short_b[:, 0:short_taps, :] = short_ref[...].astype(F32)

    def filter_spectrum(u, carry):
        cols = pl.ds(pl.multiple_of(u * pair_lanes, pair_lanes), pair_lanes)
        x = filter_ref[:, cols]
        found = jnp.dot(taps_hi[...], x, preferred_element_type=F32) + jnp.dot(
            taps_lo[...], x, preferred_element_type=F32
        )
        spec_b[2 * u] = found[:, :lanes]
        spec_b[2 * u + 1] = found[:, lanes:]
        return carry

    lax.fori_loop(0, col_tiles // 2, filter_spectrum, 0)
    lacc[...] = jnp.zeros_like(lacc)
    par_b[...] = jnp.zeros_like(par_b)

    drain(meta_r, sem_mr.at[0])
    meta = meta_r[...].reshape(slots, lanes)
    pick = jnp.where(iota((8, lanes), 1) == 0, 1.0, 0.0).astype(BF16)
    found_row = lax.dot_general(
        pick, meta, (((1,), (1,)), ((), ())), preferred_element_type=F32
    )[0:1, :]
    landed_row = found_row + slot_stream_row
    landed_col = meta[:, 0:1].astype(F32) + slot_stream_col
    target_lane = (lane_local + 1).astype(F32) + lane_stream.astype(F32) * stream_step
    place_m[...] = jnp.where(landed_col == target_lane, 1.0, 0.0).astype(BF16)
    own_index = (iota((rows, 1), 0) + 1).astype(F32)
    for s in range(3):
        unpack_m[s * rows : (s + 1) * rows, :] = jnp.where(
            own_index + s * stream_step == landed_row, 1.0, 0.0
        ).astype(BF16)
    target_push.wait()
    weight_push.wait()
    not_first = jnp.where(me > 0, 1.0, 0.0)
    not_last = jnp.where(me < peers - 1, 1.0, 0.0)

    def tile_range(c):
        return pl.ds(c * tiles, tiles)

    def prev_push(c):
        return push(prev_s.at[c], prev_r.at[c], sem_ps.at[c], sem_pr.at[c], right, ch)

    def next_push(c):
        return push(next_s.at[c], next_r.at[c], sem_ns.at[c], sem_nr.at[c], left, ch)

    def gated_push(c):
        return push(
            gext_b.at[tile_range(c), taps_at : taps_at + taps, :],
            gext_b.at[tile_range(c), 0:taps, :],
            sem_gs.at[c],
            sem_gr.at[c],
            right,
            ch,
        )

    taps_at = rows

    def mixed_push(c):
        return push(
            gm_b.at[tile_range(c), 0 : taps + edge, :],
            gm_b.at[tile_range(c), rows : rows + taps + edge, :],
            sem_gs.at[chunks + c],
            sem_gr.at[chunks + c],
            left,
            ch,
        )

    def land(c):
        drain(recv_b.at[c], sem_ar.at[c])

        def body(u, carry):
            local = pl.ds(pl.multiple_of(u * pair_lanes, pair_lanes), pair_lanes)
            got = recv_b[c, :, :, local].reshape(slots, pair_lanes)
            placed = jnp.dot(unpack_m[...], got, preferred_element_type=F32)
            for part in range(2):
                at = c * tiles + 2 * u + part
                piece = placed[:, part * lanes : (part + 1) * lanes]
                for s in range(3):
                    rows_b[s, at, edge : edge + rows, :] = piece[s * rows : (s + 1) * rows]
                    prev_s[c, s, 2 * u + part] = piece[
                        (s + 1) * rows - edge : (s + 1) * rows
                    ].astype(BF16)
                    if s > 0:
                        next_s[c, s - 1, 2 * u + part] = piece[
                            s * rows : s * rows + edge
                        ].astype(BF16)
            return carry

        lax.fori_loop(0, pairs, body, 0)
        prev_push(c).start()
        next_push(c).start()

    def convolve(c):
        prev_push(c).wait()
        next_push(c).wait()

        def body(u, carry):
            at = c * tiles + u
            cols = pl.ds(pl.multiple_of(at * lanes, lanes), lanes)
            for s in range(3):
                rows_b[s, at, 0:edge, :] = prev_r[c, s, u].astype(F32) * not_first
            for s in range(2):
                rows_b[s + 1, at, edge + rows : 2 * edge + rows, :] = next_r[c, s, u].astype(F32)

            def conv(s, total):
                summed = None
                for j in range(short_taps):
                    term = (
                        short_b[s, j : j + 1, cols]
                        * rows_b[s, at, edge - j : edge - j + total, :]
                    )
                    summed = term if summed is None else summed + term
                return summed

            k_conv = conv(1, ext)
            v_conv = conv(2, ext)
            kc_b[at] = k_conv
            vc_b[at] = v_conv
            gext_b[at, taps : taps + ext, :] = (k_conv * v_conv).astype(BF16)
            q_conv = conv(0, rows)
            qc_b[at] = q_conv
            out_grad = weight_col[0:rows] * target_ref[:, cols].astype(F32)
            go_b[at, 0:rows, :] = out_grad
            go_b[at, rows:ext, :] = (
                wnext_r[...] * tnext_r[:, cols].astype(F32) * not_last
            )
            gm_b[at, 0:rows, :] = (out_grad * q_conv).astype(BF16)
            return carry

        lax.fori_loop(0, tiles, body, 0)
        gated_push(c).start()
        mixed_push(c).start()

    def both(high, low, x):
        return jnp.dot(high, x, preferred_element_type=F32) + jnp.dot(
            low, x, preferred_element_type=F32
        )

    def inverse(high, low, real, imag):
        y = jnp.concatenate([real, imag], axis=0)
        y_hi = y.astype(BF16)
        y_lo = (y - y_hi.astype(F32)).astype(BF16)
        return both(high[...], low[...], y_hi) + jnp.dot(
            high[...], y_lo, preferred_element_type=F32
        )

    def backward(c):
        gated_push(c).wait()
        mixed_push(c).wait()

        @pl.when(me == 0)
        def _():
            def clear(u, carry):
                gext_b[c * tiles + u, 0:taps, :] = jnp.zeros((taps, lanes), BF16)
                return carry

            lax.fori_loop(0, tiles, clear, 0)

        @pl.when(me == peers - 1)
        def _():
            def clear(u, carry):
                gm_b[c * tiles + u, rows : rows + taps + edge, :] = jnp.zeros(
                    (taps + edge, lanes), BF16
                )
                return carry

            lax.fori_loop(0, tiles, clear, 0)

        def body(u, carry):
            first = c * tiles + 2 * u
            gx = jnp.concatenate([gext_b[first], gext_b[first + 1]], axis=1)
            g_own = jnp.concatenate(
                [gm_b[first, 0:rows, :], gm_b[first + 1, 0:rows, :]], axis=1
            )
            g_later = jnp.concatenate(
                [
                    gm_b[first, rows : rows + taps + edge, :],
                    gm_b[first + 1, rows : rows + taps + edge, :],
                ],
                axis=1,
            )
            spec = jnp.concatenate([spec_b[first], spec_b[first + 1]], axis=1)
            fr, fi = spec[:rows], spec[rows:]
            sg = both(ahead_hi[...], ahead_lo[...], gx)
            gr, gi = sg[:rows], sg[rows:]
            mixed = inverse(mixed_hi, mixed_lo, fr * gr - fi * gi, fr * gi + fi * gr)
            so = both(own_hi[...], own_lo[...], g_own)
            mr, mi = so[:rows], so[rows:]
            taps_grad = inverse(filter_hi, filter_lo, mr * gr + mi * gi, mr * gi - mi * gr)
            sl = both(later_hi[...], later_lo[...], g_later)
            ar, ai = mr + sl[:rows], mi + sl[rows:]
            gated_grad = inverse(gated_hi, gated_lo, fr * ar + fi * ai, fr * ai - fi * ar)
            for part in range(2):
                at = first + part
                cols = pl.ds(pl.multiple_of(at * lanes, lanes), lanes)
                lane_cut = slice(part * lanes, (part + 1) * lanes)
                mix = mixed[:, lane_cut]
                gg = gated_grad[:, lane_cut]
                tile = 2 * u + part
                found_taps = taps_grad[:, lane_cut]
                half_b[c, 0, tile] = found_taps[0:half_rows]
                half_b[c, 1, tile, 0 : taps - half_rows, :] = found_taps[half_rows:]
                out = (qc_b[at] * mix[:rows]).astype(BF16)
                out_ref[:, cols] = out
                lacc[...] += out.astype(F32) * target_ref[:, cols].astype(F32)
                gbuf[0] = go_b[at] * mix
                gbuf[1] = gg * vc_b[at]
                gbuf[2] = gg * kc_b[at]
                for s in range(3):
                    own = gbuf[s, 0:rows, :]
                    back = None
                    for j in range(short_taps):
                        found = jnp.sum(
                            own * rows_b[s, at, edge - j : edge - j + rows, :],
                            axis=0,
                            keepdims=True,
                        )
                        par_b[s * short_taps + j : s * short_taps + j + 1, :] = found
                        term = short_b[s, j : j + 1, cols] * gbuf[s, j : j + rows, :]
                        back = term if back is None else back + term
                    gr_b[s * rows : (s + 1) * rows, lane_cut] = back.astype(BF16)
                half_b[c, 1, tile, taps - half_rows : half_rows, :] = par_b[...]
            local = pl.ds(pl.multiple_of(u * pair_lanes, pair_lanes), pair_lanes)
            packed = jnp.dot(place_m[...], gr_b[...], preferred_element_type=F32).astype(BF16)
            bsend_b[c, :, :, local] = packed.reshape(blocks, block_rows, pair_lanes)
            return carry

        lax.fori_loop(0, pairs, body, 0)
        out_copy(c).start()

        half_push(c).start()
        exchange_back(bsend_b.at[c], brecv_b.at[c], sem_bs.at[c], sem_br.at[c])

    def half_push(c):
        return push(
            half_b.at[c, 1 - core], half_r.at[c], sem_hs.at[c], sem_hr.at[c], partner, ch
        )

    def chip_sum(c):
        half_push(c).wait()

        def body(t, carry):
            z_s[c, t] = (half_b[c, core, t] + half_r[c, t]).astype(BF16)
            return carry

        lax.fori_loop(0, depth, body, 0)
        pltpu.make_async_copy(z_s.at[c, my_z], z_r.at[c, my_z], sem_zr.at[c]).start()

        def send(step, carry):
            z_to = lax.rem(my_z + step, depth)
            to = (z_to * breadth + my_y) * 2 + core
            push(z_s.at[c, z_to], z_r.at[c, my_z], sem_zs.at[c], sem_zr.at[c], to, ch).start()
            return carry

        lax.fori_loop(1, depth, send, 0)

    def line_sum(c):
        drain(z_r.at[c], sem_zr.at[c])
        summed = z_r[c, 0].astype(F32)
        for z in range(1, depth):
            summed = summed + z_r[c, z].astype(F32)
        y_s[c] = summed.astype(BF16)
        pltpu.make_async_copy(y_s.at[c], y_r.at[c, my_y], sem_yr.at[c]).start()

        def send(step, carry):
            y_to = lax.rem(my_y + step, breadth)
            to = (my_z * breadth + y_to) * 2 + core
            push(y_s.at[c], y_r.at[c, my_y], sem_ys.at[c], sem_yr.at[c], to, ch).start()
            return carry

        lax.fori_loop(1, breadth, send, 0)

    def plane_sum(c):
        drain(y_r.at[c], sem_yr.at[c])
        summed = y_r[c, 0].astype(F32)
        for y in range(1, breadth):
            summed = summed + y_r[c, y].astype(F32)
        f_s[c] = (summed * grad_scale).astype(BF16)
        piece = (c * depth + my_z) * 2 + core
        pltpu.make_async_copy(f_s.at[c], ag_r.at[piece], sem_fr.at[0]).start()
        push(f_s.at[c], ag_r.at[piece], sem_fs.at[c], sem_fr.at[0], partner, ch).start()

        def send(step, carry):
            z_to = lax.rem(my_z + step, depth)
            to = (z_to * breadth + my_y) * 2
            push(f_s.at[c], ag_r.at[piece], sem_fs.at[c], sem_fr.at[0], to, ch).start()
            push(f_s.at[c], ag_r.at[piece], sem_fs.at[c], sem_fr.at[0], to + 1, ch).start()
            return carry

        lax.fori_loop(1, depth, send, 0)

    def grad_copies(c):
        cols = pl.ds(pl.multiple_of(c * width, width), width)
        return [
            pltpu.make_async_copy(grads_b.at[s, :, cols], to.at[:, cols], sem_out.at[chunks + c])
            for s, to in enumerate((qg_hbm, kg_hbm, vg_hbm))
        ]

    def finish(c):
        drain(brecv_b.at[c], sem_br.at[c])

        def body(u, inner):
            local = pl.ds(pl.multiple_of(u * pair_lanes, pair_lanes), pair_lanes)
            cols = pl.ds(pl.multiple_of(c * width + u * pair_lanes, pair_lanes), pair_lanes)
            got = brecv_b[c, :, :, local].reshape(slots, pair_lanes)
            back = jnp.dot(return_m[...], got, preferred_element_type=F32).astype(BF16)
            for s in range(3):
                grads_b[s, :, cols] = back[s * rows : (s + 1) * rows]
            return inner

        lax.fori_loop(0, pairs, body, 0)
        for copy in grad_copies(c):
            copy.start()

    def out_copy(c):
        cols = pl.ds(pl.multiple_of(c * width, width), width)
        return pltpu.make_async_copy(out_ref.at[:, cols], out_hbm.at[:, cols], sem_out.at[c])

    def loss_push(step):
        return push(
            lch_s, lch_r.at[ch], sem_x.at[8 + step], sem_x.at[2], me, lax.rem(ch + step, groups)
        )

    def start_loss():
        row_loss = jnp.sum(lacc[...], axis=1, keepdims=True)
        hot = iota((rows, lanes), 1).astype(F32) == ids_b[...]
        taxon_part = jnp.sum(jnp.where(hot, row_loss, 0.0), axis=0, keepdims=True) * loss_scale
        lch_s[...] = jnp.broadcast_to(taxon_part, (8, lanes))
        lch_r[ch] = jnp.broadcast_to(taxon_part, (8, lanes))
        for step in range(1, groups):
            loss_push(step).start()

    def share_loss():
        if groups > 1:
            drain(lch_r.at[0 : groups - 1], sem_x.at[2])
        total = lch_r[0]
        for g in range(1, groups):
            total = total + lch_r[g]
        lct_s[...] = total
        lct_r[me] = total

        def send(step, carry):
            to = lax.rem(me + step, peers)
            push(lct_s, lct_r.at[me], sem_x.at[5], sem_x.at[6], to, ch).start()
            return carry

        lax.fori_loop(1, peers, send, 0)

    def steps(t, carry):
        @pl.when(t < chunks)
        def _():
            land(t)

        @pl.when(jnp.logical_and(t >= 1, t < chunks + 1))
        def _():
            convolve(t - 1)

        @pl.when(jnp.logical_and(t >= 3, t < chunks + 3))
        def _():
            chip_sum(t - 3)

        @pl.when(jnp.logical_and(t >= 4, t < chunks + 4))
        def _():
            line_sum(t - 4)

        @pl.when(t >= 5)
        def _():
            plane_sum(t - 5)

        @pl.when(jnp.logical_and(t >= 2, t < chunks + 2))
        def _():
            backward(t - 2)

        @pl.when(t == chunks + 1)
        def _():
            start_loss()

        @pl.when(t == chunks + 2)
        def _():
            share_loss()

        @pl.when(t >= 5)
        def _():
            finish(t - 5)

        return carry

    lax.fori_loop(0, chunks + 5, steps, 0)

    drain(lct_r.at[0 : peers - 1], sem_x.at[6])

    def add_loss(j, summed):
        return summed + lct_r[j]

    loss_ref[...] = lax.fori_loop(1, peers, add_loss, lct_r[0])
    for c in range(chunks):
        out_copy(c).wait()
        for copy in grad_copies(c):
            copy.wait()
    drain(ag_r, sem_fr.at[0])

    drain(meta_s.at[0:peers], sem_ms.at[0])
    for step in range(1, groups):
        loss_push(step).wait_send()
    drain(lct_r.at[0 : peers - 1], sem_x.at[5])

    def sent(c, carry):
        drain(send_b.at[c, 0:peers], sem_as.at[c])
        drain(bsend_b.at[c, 0:peers], sem_bs.at[c])
        drain(z_r.at[c, 0 : depth - 1], sem_zs.at[c])
        drain(y_r.at[c, 0 : breadth - 1], sem_ys.at[c])
        drain(ag_r.at[0 : 2 * depth - 1], sem_fs.at[c])
        return carry

    lax.fori_loop(0, chunks, sent, 0)


def finish_kernel(*refs):
    sources, loss_in = refs[0:5], refs[5]
    targets, loss_ref = refs[6:12], refs[12]
    held, par_b, sem_in, sem_out = refs[13:20], refs[20], refs[21], refs[22]
    ag_ref, fg_ref, sg_ref = held[4:7]
    taps, short_taps = fg_ref.shape[0], sg_ref.shape[1]
    half_rows = ag_ref.shape[1]
    ins = [pltpu.make_async_copy(sources[i], held[i], sem_in.at[i]) for i in range(5)]
    leaving = (0, 1, 2, 3, 5, 6)
    outs = [
        pltpu.make_async_copy(held[i], targets[n], sem_out.at[n]) for n, i in enumerate(leaving)
    ]
    for i in (4, 0, 1, 2, 3):
        ins[i].start()
    loss_ref[...] = loss_in[0:1, 0 : loss_ref.shape[1]]
    ins[4].wait()
    for t in range(fg_ref.shape[1] // lanes):
        cut = slice(t * lanes, (t + 1) * lanes)
        low = ag_ref[2 * t + 1].astype(F32)
        fg_ref[0:half_rows, cut] = ag_ref[2 * t].astype(F32)
        fg_ref[half_rows:taps, cut] = low[0 : taps - half_rows]
        par_b[...] = low[taps - half_rows :]
        for s in range(3):
            sg_ref[s, :, cut] = par_b[s * short_taps : (s + 1) * short_taps, :]
    outs[4].start()
    outs[5].start()
    for i in range(4):
        ins[i].wait()
        outs[i].start()
    for copy in outs:
        copy.wait()


def shards(
    query_in,
    key_in,
    value_in,
    row_place,
    short_weight,
    long_filter,
    target,
    taxon_ids,
    taxon_weight,
):
    rows, channels = query_in.shape
    peers = lax.axis_size("ctx")
    groups = lax.axis_size("ch")
    taps = long_filter.shape[0]
    short_taps = short_weight.shape[1]
    width = channels // chunks
    col_tiles = channels // lanes
    tiles = width // lanes
    blocks = peers + 1
    slots = blocks * block_rows
    ext = rows + edge
    span = taps + ext
    payload = payload_rows(taps, short_taps)
    half_rows = payload // 2
    tables = []
    made = dft_tables(rows, taps)
    for name in table_names:
        high, low = split_constant(made[name])
        tables.append(jnp.asarray(high))
        tables.append(jnp.asarray(low))
    vm = pltpu.VMEM
    dma = pltpu.SemaphoreType.DMA
    shape = jax.ShapeDtypeStruct
    loaded = (query_in, key_in, value_in, target, long_filter, *tables)
    scratch = [
        *(vm(x.shape, x.dtype) for x in loaded),
        dma((len(loaded),)),
        vm((rows, channels), BF16),
        vm((slots, 3 * rows), BF16),
        vm((3 * rows, slots), BF16),
        vm((slots, 3 * rows), BF16),
        vm((3 * rows, slots), BF16),
        vm((chunks, blocks, block_rows, width), BF16),
        vm((chunks, blocks, block_rows, width), BF16),
        vm((blocks, block_rows, lanes), BF16),
        vm((blocks, block_rows, lanes), BF16),
        vm((chunks, blocks, block_rows, width), BF16),
        vm((chunks, blocks, block_rows, width), BF16),
        vm((3, rows, channels), BF16),
        vm((3, col_tiles, rows + 2 * edge, lanes), F32),
        vm((chunks, 3, tiles, edge, lanes), BF16),
        vm((chunks, 3, tiles, edge, lanes), BF16),
        vm((chunks, 2, tiles, edge, lanes), BF16),
        vm((chunks, 2, tiles, edge, lanes), BF16),
        vm((edge, channels), BF16),
        vm((edge, channels), BF16),
        vm((edge, lanes), F32),
        vm((edge, lanes), F32),
        vm((col_tiles, rows, lanes), F32),
        vm((col_tiles, ext, lanes), F32),
        vm((col_tiles, ext, lanes), F32),
        vm((col_tiles, ext, lanes), F32),
        vm((col_tiles, span, lanes), BF16),
        vm((col_tiles, span, lanes), BF16),
        vm((col_tiles, 2 * rows, lanes), F32),
        vm((3, 8, channels), F32),
        vm((3, ext, lanes), F32),
        vm((3 * rows, 2 * lanes), BF16),
        vm((rows, lanes), F32),
        vm((rows, lanes), F32),
        vm((payload - taps, lanes), F32),
        vm((chunks, 2, tiles, half_rows, lanes), F32),
        vm((chunks, tiles, half_rows, lanes), F32),
        vm((chunks, tiles, half_rows, lanes), BF16),
        vm((chunks, tiles, half_rows, lanes), BF16),
        vm((chunks, half_rows, lanes), BF16),
        vm((chunks, peers // (2 * tiles), half_rows, lanes), BF16),
        vm((chunks, half_rows, lanes), BF16),
        vm((8, lanes), F32),
        vm((groups, 8, lanes), F32),
        vm((8, lanes), F32),
        vm((peers, 8, lanes), F32),
        dma((chunks,)),
        dma((chunks,)),
        dma((chunks,)),
        dma((chunks,)),
        dma((chunks,)),
        dma((chunks,)),
        dma((chunks,)),
        dma((chunks,)),
        dma((2 * chunks,)),
        dma((2 * chunks,)),
        dma((1,)),
        dma((1,)),
        dma((chunks,)),
        dma((chunks,)),
        dma((chunks,)),
        dma((chunks,)),
        dma((chunks,)),
        dma((chunks,)),
        dma((chunks,)),
        dma((1,)),
        dma((2 * chunks,)),
        dma((16,)),
    ]
    here = pl.BlockSpec(memory_space=pltpu.VMEM)
    away = pl.BlockSpec(memory_space=pl.ANY)
    *moved, gathered, losses = pl.pallas_call(
        lambda *refs: whole_kernel(peers, groups, *refs),
        out_shape=(
            *(shape((rows, channels), BF16) for _ in range(4)),
            shape((peers, half_rows, lanes), BF16),
            shape((8, lanes), F32),
        ),
        in_specs=[here] * 4 + [away] * len(loaded),
        out_specs=[away] * 5 + [here],
        scratch_shapes=scratch,
        compiler_params=pltpu.CompilerParams(
            collective_id=0, has_side_effects=True, vmem_limit_bytes=63_000_000
        ),
        name="hyena",
    )(
        row_place.reshape(1, rows),
        taxon_ids.reshape(1, rows),
        taxon_weight.reshape(1, -1),
        short_weight,
        *loaded,
    )
    count = taxon_weight.shape[0]
    gated_out, query_grad, key_grad, value_grad, filter_grad, short_grad, losses = pl.pallas_call(
        finish_kernel,
        out_shape=(
            *(shape((rows, channels), BF16) for _ in range(4)),
            shape((taps, channels), F32),
            shape((3, short_taps, channels), F32),
            shape((1, count), F32),
        ),
        in_specs=[away] * 5 + [here],
        out_specs=[away] * 6 + [here],
        scratch_shapes=[
            *(vm((rows, channels), BF16) for _ in range(4)),
            vm((peers, half_rows, lanes), BF16),
            vm((taps, channels), F32),
            vm((3, short_taps, channels), F32),
            vm((payload - taps, lanes), F32),
            dma((5,)),
            dma((6,)),
        ],
        name="finish",
    )(*moved, gathered, losses)
    return (
        gated_out,
        query_grad,
        key_grad,
        value_grad,
        filter_grad,
        short_grad,
        losses.reshape(count),
    )


def solution(mesh):
    placed = (
        P("ctx", "ch"),
        P("ctx", "ch"),
        P("ctx", "ch"),
        P("ctx"),
        P(None, None, "ch"),
        P(None, "ch"),
        P("ctx", "ch"),
        P("ctx"),
        P(),
    )
    return jax.shard_map(
        shards,
        mesh=mesh,
        in_specs=placed,
        out_specs=(
            P("ctx", "ch"),
            P("ctx", "ch"),
            P("ctx", "ch"),
            P("ctx", "ch"),
            P(None, "ch"),
            P(None, None, "ch"),
            P(),
        ),
        check_vma=False,
    )
```

```python
import math

import jax
import jax.numpy as jnp
import numpy as np
from jax import lax
from jax.experimental import pallas as pl
from jax.experimental.pallas import tpu as pltpu
from jax.sharding import PartitionSpec as P

MESH = pl.DeviceIdType.MESH
F32 = jnp.float32
BF16 = jnp.bfloat16
unit = 5
block_rows = 16
lanes = 128
edge = 16
chunks = 4
window = 2
stream_step = 1024.0


def split_constant(array):
    high = array.astype(np.float32).astype(jnp.bfloat16)
    low = (array - high.astype(np.float64)).astype(np.float32).astype(jnp.bfloat16)
    return high, low


def dft_tables(rows, taps):
    half = rows
    size = 2 * rows
    span = taps + rows + edge
    theta = np.pi * (2 * np.arange(half) + 1) / size

    def ahead(index):
        angle = theta[:, None] * index[None, :]
        return np.concatenate([np.cos(angle), -np.sin(angle)], axis=0)

    def back(index):
        angle = theta[None, :] * index[:, None]
        return np.concatenate([np.cos(angle), -np.sin(angle)], axis=1) * (2.0 / size)

    tables = {
        "ahead": ahead(np.arange(span)),
        "own": ahead(np.arange(rows)),
        "later": ahead(np.arange(rows, rows + taps + edge)),
        "taps": ahead(np.arange(taps)),
        "mixed": back(np.arange(rows + edge) + taps),
        "gated": back(np.arange(rows + edge)),
        "filter": back(taps - np.arange(taps)),
    }
    return tables


table_names = ("taps", "ahead", "own", "later", "mixed", "gated", "filter")


def payload_rows(taps, short_taps):
    return -(-(taps + 3 * short_taps) // 32) * 32


def iota(shape, axis):
    return lax.broadcasted_iota(jnp.int32, shape, axis)


def slot_facts(index):
    block = lax.shift_right_logical(index, 4)
    row = jnp.bitwise_and(index, block_rows - 1)
    stream = jnp.where(row >= unit, 1, 0) + jnp.where(row >= 2 * unit, 1, 0)
    rank = row - unit * stream
    valid = row < 3 * unit
    return block, stream, rank, valid


def whole_kernel(
    peers,
    groups,
    place_ref,
    taxon_ref,
    weight_ref,
    short_ref,
    *refs,
):
    far = refs[:19]
    out_hbm, qg_hbm, kg_hbm, vg_hbm, ag_r, loss_ref = refs[19:25]
    near = refs[25:44]
    (
        q_ref,
        k_ref,
        v_ref,
        target_ref,
        filter_ref,
        taps_hi,
        taps_lo,
        ahead_hi,
        ahead_lo,
        own_hi,
        own_lo,
        later_hi,
        later_lo,
        mixed_hi,
        mixed_lo,
        gated_hi,
        gated_lo,
        filter_hi,
        filter_lo,
    ) = near
    sem_in = refs[44]
    (
        out_ref,
        pack_m,
        unpack_m,
        place_m,
        return_m,
        send_b,
        recv_b,
        meta_s,
        meta_r,
        bsend_b,
        brecv_b,
        grads_b,
        rows_b,
        prev_s,
        prev_r,
        next_s,
        next_r,
        tnext_s,
        tnext_r,
        wnext_s,
        wnext_r,
        qc_b,
        kc_b,
        vc_b,
        go_b,
        gext_b,
        gm_b,
        spec_b,
        short_b,
        gbuf,
        gr_b,
        lacc,
        ids_b,
        par_b,
        half_b,
        half_r,
        z_s,
        z_r,
        y_s,
        y_r,
        f_s,
        lch_s,
        lch_r,
        lct_s,
        lct_r,
        sem_as,
        sem_ar,
        sem_bs,
        sem_br,
        sem_ps,
        sem_pr,
        sem_ns,
        sem_nr,
        sem_gs,
        sem_gr,
        sem_ms,
        sem_mr,
        sem_hs,
        sem_hr,
        sem_zs,
        sem_zr,
        sem_ys,
        sem_yr,
        sem_fs,
        sem_fr,
        sem_out,
        sem_x,
    ) = refs[45:]
    rows, channels = q_ref.shape
    taps = filter_ref.shape[0]
    short_taps = short_ref.shape[1]
    width = channels // chunks
    col_tiles = channels // lanes
    tiles = width // lanes
    pairs = tiles // 2
    blocks = peers + 1
    slots = blocks * block_rows
    ext = rows + edge
    payload = payload_rows(taps, short_taps)
    half_rows = payload // 2
    me = lax.axis_index("ctx")
    depth = tiles
    breadth = peers // (2 * depth)
    core = lax.rem(me, 2)
    my_y = lax.rem(me // 2, breadth)
    my_z = me // (2 * breadth)
    partner = me + 1 - 2 * core
    ch = lax.axis_index("ch")
    right = lax.rem(me + 1, peers)
    left = lax.rem(me + peers - 1, peers)
    grad_scale = 1.0 / math.sqrt(rows * peers)
    loss_scale = 1.0 / math.sqrt(channels * groups * rows * peers / weight_ref.shape[1])

    barrier = pltpu.get_barrier_semaphore()

    def greet(step, carry):
        pl.semaphore_signal(
            barrier, inc=1, device_id=(lax.rem(me + step, peers), ch), device_id_type=MESH
        )
        return carry

    lax.fori_loop(1, peers, greet, 0)
    for step in range(1, groups):
        pl.semaphore_signal(
            barrier, inc=1, device_id=(me, lax.rem(ch + step, groups)), device_id_type=MESH
        )

    def fetch(index):
        return pltpu.make_async_copy(far[index], near[index], sem_in.at[index])

    for index in range(len(far)):
        fetch(index).start()

    def push(src, dst, send_sem, recv_sem, ctx_to, ch_to):
        return pltpu.make_async_remote_copy(
            src_ref=src,
            dst_ref=dst,
            send_sem=send_sem,
            recv_sem=recv_sem,
            device_id=(ctx_to, ch_to),
            device_id_type=MESH,
        )

    def drain(ref, sem):
        pltpu.make_async_copy(ref, ref, sem).wait()

    def column(row_vector, count):
        eye = iota((count, count), 0) == iota((count, count), 1)
        return jnp.sum(jnp.where(eye, row_vector, 0.0), axis=1, keepdims=True)

    place_row = place_ref[...].astype(F32)
    place3_row = jnp.concatenate([place_row] * 3, axis=1)
    owner_row = jnp.floor((place_row + 0.5) * (1.0 / rows))
    owner3_row = jnp.floor((place3_row + 0.5) * (1.0 / rows))
    owner_col = column(owner_row, rows)
    place_col = column(place_row, rows)
    local_col = place_col - owner_col * rows

    def slot_key(owner, rank):
        return jnp.where(
            rank < unit - 0.5, owner * unit + rank, float(peers * unit) + rank - unit
        )

    order3 = iota((rows, 3 * rows), 1)
    stream3 = jnp.where(order3 >= rows, 1, 0) + jnp.where(order3 >= 2 * rows, 1, 0)
    before3 = iota((rows, 3 * rows), 0) < order3 - rows * stream3
    rank3_row = jnp.sum(
        jnp.where(jnp.logical_and(owner_col == owner3_row, before3), 1.0, 0.0),
        axis=0,
        keepdims=True,
    )
    key3_row = slot_key(owner3_row, rank3_row)
    before = iota((rows, rows), 1) < iota((rows, rows), 0)
    rank_col = jnp.sum(
        jnp.where(jnp.logical_and(owner_col == owner_row, before), 1.0, 0.0),
        axis=1,
        keepdims=True,
    )
    key_col = slot_key(owner_col, rank_col)

    lane3 = iota((1, 3 * rows), 1)
    lane_stream = jnp.where(lane3 >= rows, 1, 0) + jnp.where(lane3 >= 2 * rows, 1, 0)
    lane_local = lane3 - rows * lane_stream

    def static_key(shape, axis):
        block, stream, rank, valid = slot_facts(iota(shape, axis))
        key = jnp.where(valid, stream * 1024 + block * unit + rank, -1)
        return key.astype(F32), jnp.where(valid, stream * 1024, -4096).astype(F32)

    slot_key_col, slot_stream_col = static_key((slots, 1), 0)
    slot_key_row, slot_stream_row = static_key((1, slots), 1)
    full3_row = key3_row + lane_stream.astype(F32) * stream_step
    pack_m[...] = jnp.where(slot_key_col == full3_row, 1.0, 0.0).astype(BF16)
    meta_col = jnp.broadcast_to(local_col + 1.0, (rows, lanes)).astype(BF16)
    meta3 = jnp.concatenate([meta_col] * 3, axis=0)
    meta_s[...] = (
        jnp.dot(pack_m[...], meta3, preferred_element_type=F32)
        .astype(BF16)
        .reshape(blocks, block_rows, lanes)
    )

    pair_lanes = 2 * lanes

    def pack(c, carry):
        def body(u, inner):
            base = pl.multiple_of(c * width + u * pair_lanes, pair_lanes)
            cols = pl.ds(base, pair_lanes)
            stacked = jnp.concatenate([q_ref[:, cols], k_ref[:, cols], v_ref[:, cols]], axis=0)
            packed = jnp.dot(pack_m[...], stacked, preferred_element_type=F32).astype(BF16)
            local = pl.ds(pl.multiple_of(u * pair_lanes, pair_lanes), pair_lanes)
            send_b[c, :, :, local] = packed.reshape(blocks, block_rows, pair_lanes)
            return inner

        lax.fori_loop(0, pairs, body, 0)
        return carry

    wait_for = peers - 1 + groups - 1

    def exchange(source, landing, send_sem, recv_sem):
        pltpu.make_async_copy(source.at[me], landing.at[me], recv_sem).start()
        push(source.at[peers], landing.at[peers], send_sem, recv_sem, right, ch).start()

        def body(step, carry):
            to = lax.rem(me + step, peers)
            push(source.at[to], landing.at[me], send_sem, recv_sem, to, ch).start()
            return carry

        lax.fori_loop(1, peers, body, 0)

    near_peers = peers // 2

    def return_some(c, first, last):
        def body(step, carry):
            to = lax.rem(me + step, peers)
            push(bsend_b.at[c, to], brecv_b.at[c, me], sem_bs.at[c], sem_br.at[c], to, ch).start()
            return carry

        lax.fori_loop(first, last, body, 0)

    def return_first(c):
        pltpu.make_async_copy(bsend_b.at[c, me], brecv_b.at[c, me], sem_br.at[c]).start()
        push(
            bsend_b.at[c, peers], brecv_b.at[c, peers], sem_bs.at[c], sem_br.at[c], left, ch
        ).start()
        return_some(c, 1, near_peers)

    def return_rest(c):
        return_some(c, near_peers, peers)

    for index in range(3):
        fetch(index).wait()
    pack(0, 0)
    pl.semaphore_wait(barrier, wait_for)
    exchange(meta_s, meta_r, sem_ms.at[0], sem_mr.at[0])
    target_push = push(tnext_s, tnext_r, sem_x.at[0], sem_x.at[1], left, ch)
    weight_push = push(wnext_s, wnext_r, sem_x.at[12], sem_x.at[13], left, ch)
    exchange(send_b.at[0], recv_b.at[0], sem_as.at[0], sem_ar.at[0])

    def pack_and_send(c, carry):
        pack(c, 0)
        exchange(send_b.at[c], recv_b.at[c], sem_as.at[c], sem_ar.at[c])
        return carry

    lax.fori_loop(1, window, pack_and_send, 0)
    fetch(3).wait()
    ids_row = taxon_ref[...].astype(F32)
    ids_col = column(ids_row, rows)
    count = weight_ref.shape[1]
    taxon_hot = iota((rows, lanes), 1).astype(F32) == ids_col
    weights = jnp.concatenate([weight_ref[...], jnp.zeros((1, lanes - count), F32)], axis=1)
    weight_col = jnp.sum(jnp.where(taxon_hot, weights, 0.0), axis=1, keepdims=True)
    ids_b[...] = jnp.broadcast_to(ids_col, (rows, lanes))
    tnext_s[...] = target_ref[0:edge, :]
    wnext_s[...] = jnp.broadcast_to(weight_col[0:edge], (edge, lanes))
    target_push.start()
    weight_push.start()
    for s in range(3):
        return_m[s * rows : (s + 1) * rows, :] = jnp.where(
            key_col + s * stream_step == slot_key_row, 1.0, 0.0
        ).astype(BF16)

    lax.fori_loop(window, chunks, pack, 0)
    for index in range(4, len(far)):
        fetch(index).wait()

    short_b[:, 0:short_taps, :] = short_ref[...].astype(F32)

    def filter_spectrum(u, carry):
        cols = pl.ds(pl.multiple_of(u * pair_lanes, pair_lanes), pair_lanes)
        x = filter_ref[:, cols]
        found = jnp.dot(taps_hi[...], x, preferred_element_type=F32) + jnp.dot(
            taps_lo[...], x, preferred_element_type=F32
        )
        spec_b[2 * u] = found[:, :lanes]
        spec_b[2 * u + 1] = found[:, lanes:]
        return carry

    lax.fori_loop(0, col_tiles // 2, filter_spectrum, 0)
    lacc[...] = jnp.zeros_like(lacc)
    par_b[...] = jnp.zeros_like(par_b)

    drain(meta_r, sem_mr.at[0])
    meta = meta_r[...].reshape(slots, lanes)
    pick = jnp.where(iota((8, lanes), 1) == 0, 1.0, 0.0).astype(BF16)
    found_row = lax.dot_general(
        pick, meta, (((1,), (1,)), ((), ())), preferred_element_type=F32
    )[0:1, :]
    landed_row = found_row + slot_stream_row
    landed_col = meta[:, 0:1].astype(F32) + slot_stream_col
    target_lane = (lane_local + 1).astype(F32) + lane_stream.astype(F32) * stream_step
    place_m[...] = jnp.where(landed_col == target_lane, 1.0, 0.0).astype(BF16)
    own_index = (iota((rows, 1), 0) + 1).astype(F32)
    for s in range(3):
        unpack_m[s * rows : (s + 1) * rows, :] = jnp.where(
            own_index + s * stream_step == landed_row, 1.0, 0.0
        ).astype(BF16)
    target_push.wait()
    weight_push.wait()
    not_first = jnp.where(me > 0, 1.0, 0.0)
    not_last = jnp.where(me < peers - 1, 1.0, 0.0)

    def tile_range(c):
        return pl.ds(c * tiles, tiles)

    def prev_push(c):
        return push(prev_s.at[c], prev_r.at[c], sem_ps.at[c], sem_pr.at[c], right, ch)

    def next_push(c):
        return push(next_s.at[c], next_r.at[c], sem_ns.at[c], sem_nr.at[c], left, ch)

    def gated_push(c):
        return push(
            gext_b.at[tile_range(c), taps_at : taps_at + taps, :],
            gext_b.at[tile_range(c), 0:taps, :],
            sem_gs.at[c],
            sem_gr.at[c],
            right,
            ch,
        )

    taps_at = rows

    def mixed_push(c):
        return push(
            gm_b.at[tile_range(c), 0 : taps + edge, :],
            gm_b.at[tile_range(c), rows : rows + taps + edge, :],
            sem_gs.at[chunks + c],
            sem_gr.at[chunks + c],
            left,
            ch,
        )

    def land(c):
        drain(recv_b.at[c], sem_ar.at[c])

        def body(u, carry):
            local = pl.ds(pl.multiple_of(u * pair_lanes, pair_lanes), pair_lanes)
            got = recv_b[c, :, :, local].reshape(slots, pair_lanes)
            placed = jnp.dot(unpack_m[...], got, preferred_element_type=F32)
            for part in range(2):
                at = c * tiles + 2 * u + part
                piece = placed[:, part * lanes : (part + 1) * lanes]
                for s in range(3):
                    rows_b[s, at, edge : edge + rows, :] = piece[s * rows : (s + 1) * rows]
                    prev_s[c, s, 2 * u + part] = piece[
                        (s + 1) * rows - edge : (s + 1) * rows
                    ].astype(BF16)
                    if s > 0:
                        next_s[c, s - 1, 2 * u + part] = piece[
                            s * rows : s * rows + edge
                        ].astype(BF16)
            return carry

        lax.fori_loop(0, pairs, body, 0)
        prev_push(c).start()
        next_push(c).start()

    def convolve(c):
        prev_push(c).wait()
        next_push(c).wait()

        def body(u, carry):
            at = c * tiles + u
            cols = pl.ds(pl.multiple_of(at * lanes, lanes), lanes)
            for s in range(3):
                rows_b[s, at, 0:edge, :] = prev_r[c, s, u].astype(F32) * not_first
            for s in range(2):
                rows_b[s + 1, at, edge + rows : 2 * edge + rows, :] = next_r[c, s, u].astype(F32)

            def conv(s, total):
                summed = None
                for j in range(short_taps):
                    term = (
                        short_b[s, j : j + 1, cols]
                        * rows_b[s, at, edge - j : edge - j + total, :]
                    )
                    summed = term if summed is None else summed + term
                return summed

            k_conv = conv(1, ext)
            v_conv = conv(2, ext)
            kc_b[at] = k_conv
            vc_b[at] = v_conv
            gext_b[at, taps : taps + ext, :] = (k_conv * v_conv).astype(BF16)
            q_conv = conv(0, rows)
            qc_b[at] = q_conv
            out_grad = weight_col[0:rows] * target_ref[:, cols].astype(F32)
            go_b[at, 0:rows, :] = out_grad
            go_b[at, rows:ext, :] = (
                wnext_r[...] * tnext_r[:, cols].astype(F32) * not_last
            )
            gm_b[at, 0:rows, :] = (out_grad * q_conv).astype(BF16)
            return carry

        lax.fori_loop(0, tiles, body, 0)
        gated_push(c).start()
        mixed_push(c).start()

    def both(high, low, x):
        return jnp.dot(high, x, preferred_element_type=F32) + jnp.dot(
            low, x, preferred_element_type=F32
        )

    def inverse(high, low, real, imag):
        y = jnp.concatenate([real, imag], axis=0)
        y_hi = y.astype(BF16)
        y_lo = (y - y_hi.astype(F32)).astype(BF16)
        return both(high[...], low[...], y_hi) + jnp.dot(
            high[...], y_lo, preferred_element_type=F32
        )

    def backward(c):
        gated_push(c).wait()
        mixed_push(c).wait()

        @pl.when(me == 0)
        def _():
            def clear(u, carry):
                gext_b[c * tiles + u, 0:taps, :] = jnp.zeros((taps, lanes), BF16)
                return carry

            lax.fori_loop(0, tiles, clear, 0)

        @pl.when(me == peers - 1)
        def _():
            def clear(u, carry):
                gm_b[c * tiles + u, rows : rows + taps + edge, :] = jnp.zeros(
                    (taps + edge, lanes), BF16
                )
                return carry

            lax.fori_loop(0, tiles, clear, 0)

        def body(u, carry):
            first = c * tiles + 2 * u
            gx = jnp.concatenate([gext_b[first], gext_b[first + 1]], axis=1)
            g_own = jnp.concatenate(
                [gm_b[first, 0:rows, :], gm_b[first + 1, 0:rows, :]], axis=1
            )
            g_later = jnp.concatenate(
                [
                    gm_b[first, rows : rows + taps + edge, :],
                    gm_b[first + 1, rows : rows + taps + edge, :],
                ],
                axis=1,
            )
            spec = jnp.concatenate([spec_b[first], spec_b[first + 1]], axis=1)
            fr, fi = spec[:rows], spec[rows:]
            sg = both(ahead_hi[...], ahead_lo[...], gx)
            gr, gi = sg[:rows], sg[rows:]
            mixed = inverse(mixed_hi, mixed_lo, fr * gr - fi * gi, fr * gi + fi * gr)
            so = both(own_hi[...], own_lo[...], g_own)
            mr, mi = so[:rows], so[rows:]
            taps_grad = inverse(filter_hi, filter_lo, mr * gr + mi * gi, mr * gi - mi * gr)
            sl = both(later_hi[...], later_lo[...], g_later)
            ar, ai = mr + sl[:rows], mi + sl[rows:]
            gated_grad = inverse(gated_hi, gated_lo, fr * ar + fi * ai, fr * ai - fi * ar)
            for part in range(2):
                at = first + part
                cols = pl.ds(pl.multiple_of(at * lanes, lanes), lanes)
                lane_cut = slice(part * lanes, (part + 1) * lanes)
                mix = mixed[:, lane_cut]
                gg = gated_grad[:, lane_cut]
                tile = 2 * u + part
                found_taps = taps_grad[:, lane_cut]
                half_b[c, 0, tile] = found_taps[0:half_rows]
                half_b[c, 1, tile, 0 : taps - half_rows, :] = found_taps[half_rows:]
                out = (qc_b[at] * mix[:rows]).astype(BF16)
                out_ref[:, cols] = out
                lacc[...] += out.astype(F32) * target_ref[:, cols].astype(F32)
                gbuf[0] = go_b[at] * mix
                gbuf[1] = gg * vc_b[at]
                gbuf[2] = gg * kc_b[at]
                for s in range(3):
                    own = gbuf[s, 0:rows, :]
                    back = None
                    for j in range(short_taps):
                        found = jnp.sum(
                            own * rows_b[s, at, edge - j : edge - j + rows, :],
                            axis=0,
                            keepdims=True,
                        )
                        par_b[s * short_taps + j : s * short_taps + j + 1, :] = found
                        term = short_b[s, j : j + 1, cols] * gbuf[s, j : j + rows, :]
                        back = term if back is None else back + term
                    gr_b[s * rows : (s + 1) * rows, lane_cut] = back.astype(BF16)
                half_b[c, 1, tile, taps - half_rows : half_rows, :] = par_b[...]
            local = pl.ds(pl.multiple_of(u * pair_lanes, pair_lanes), pair_lanes)
            packed = jnp.dot(place_m[...], gr_b[...], preferred_element_type=F32).astype(BF16)
            bsend_b[c, :, :, local] = packed.reshape(blocks, block_rows, pair_lanes)
            return carry

        lax.fori_loop(0, pairs, body, 0)
        out_copy(c).start()

        half_push(c).start()

    def half_push(c):
        return push(
            half_b.at[c, 1 - core], half_r.at[c], sem_hs.at[c], sem_hr.at[c], partner, ch
        )

    def chip_sum(c):
        half_push(c).wait()

        def body(t, carry):
            z_s[c, t] = (half_b[c, core, t] + half_r[c, t]).astype(BF16)
            return carry

        lax.fori_loop(0, depth, body, 0)
        pltpu.make_async_copy(z_s.at[c, my_z], z_r.at[c, my_z], sem_zr.at[c]).start()

        def send(step, carry):
            z_to = lax.rem(my_z + step, depth)
            to = (z_to * breadth + my_y) * 2 + core
            push(z_s.at[c, z_to], z_r.at[c, my_z], sem_zs.at[c], sem_zr.at[c], to, ch).start()
            return carry

        lax.fori_loop(1, depth, send, 0)

    def line_sum(c):
        drain(z_r.at[c], sem_zr.at[c])
        summed = z_r[c, 0].astype(F32)
        for z in range(1, depth):
            summed = summed + z_r[c, z].astype(F32)
        y_s[c] = summed.astype(BF16)
        pltpu.make_async_copy(y_s.at[c], y_r.at[c, my_y], sem_yr.at[c]).start()

        def send(step, carry):
            y_to = lax.rem(my_y + step, breadth)
            to = (my_z * breadth + y_to) * 2 + core
            push(y_s.at[c], y_r.at[c, my_y], sem_ys.at[c], sem_yr.at[c], to, ch).start()
            return carry

        lax.fori_loop(1, breadth, send, 0)

    def plane_sum(c):
        drain(y_r.at[c], sem_yr.at[c])
        summed = y_r[c, 0].astype(F32)
        for y in range(1, breadth):
            summed = summed + y_r[c, y].astype(F32)
        f_s[c] = (summed * grad_scale).astype(BF16)
        piece = (c * depth + my_z) * 2 + core
        pltpu.make_async_copy(f_s.at[c], ag_r.at[piece], sem_fr.at[0]).start()
        push(f_s.at[c], ag_r.at[piece], sem_fs.at[c], sem_fr.at[0], partner, ch).start()

        def send(step, carry):
            z_to = lax.rem(my_z + step, depth)
            to = (z_to * breadth + my_y) * 2
            push(f_s.at[c], ag_r.at[piece], sem_fs.at[c], sem_fr.at[0], to, ch).start()
            push(f_s.at[c], ag_r.at[piece], sem_fs.at[c], sem_fr.at[0], to + 1, ch).start()
            return carry

        lax.fori_loop(1, depth, send, 0)

    def grad_copies(c):
        cols = pl.ds(pl.multiple_of(c * width, width), width)
        return [
            pltpu.make_async_copy(grads_b.at[s, :, cols], to.at[:, cols], sem_out.at[chunks + c])
            for s, to in enumerate((qg_hbm, kg_hbm, vg_hbm))
        ]

    def finish(c):
        drain(brecv_b.at[c], sem_br.at[c])

        def body(u, inner):
            local = pl.ds(pl.multiple_of(u * pair_lanes, pair_lanes), pair_lanes)
            cols = pl.ds(pl.multiple_of(c * width + u * pair_lanes, pair_lanes), pair_lanes)
            got = brecv_b[c, :, :, local].reshape(slots, pair_lanes)
            back = jnp.dot(return_m[...], got, preferred_element_type=F32).astype(BF16)
            for s in range(3):
                grads_b[s, :, cols] = back[s * rows : (s + 1) * rows]
            return inner

        lax.fori_loop(0, pairs, body, 0)
        for copy in grad_copies(c):
            copy.start()

    def finish_step(c, carry):
        finish(c)
        return carry

    def out_copy(c):
        cols = pl.ds(pl.multiple_of(c * width, width), width)
        return pltpu.make_async_copy(out_ref.at[:, cols], out_hbm.at[:, cols], sem_out.at[c])

    def loss_push(step):
        return push(
            lch_s, lch_r.at[ch], sem_x.at[8 + step], sem_x.at[2], me, lax.rem(ch + step, groups)
        )

    def start_loss():
        row_loss = jnp.sum(lacc[...], axis=1, keepdims=True)
        hot = iota((rows, lanes), 1).astype(F32) == ids_b[...]
        taxon_part = jnp.sum(jnp.where(hot, row_loss, 0.0), axis=0, keepdims=True) * loss_scale
        lch_s[...] = jnp.broadcast_to(taxon_part, (8, lanes))
        lch_r[ch] = jnp.broadcast_to(taxon_part, (8, lanes))
        for step in range(1, groups):
            loss_push(step).start()

    def share_loss():
        if groups > 1:
            drain(lch_r.at[0 : groups - 1], sem_x.at[2])
        total = lch_r[0]
        for g in range(1, groups):
            total = total + lch_r[g]
        lct_s[...] = total
        lct_r[me] = total

        def send(step, carry):
            to = lax.rem(me + step, peers)
            push(lct_s, lct_r.at[me], sem_x.at[5], sem_x.at[6], to, ch).start()
            return carry

        lax.fori_loop(1, peers, send, 0)

    def steps(t, carry):
        @pl.when(t < chunks)
        def _():
            land(t)

        @pl.when(jnp.logical_and(t >= 1, t < chunks + 1))
        def _():
            convolve(t - 1)

        @pl.when(t >= 3)
        def _():
            chip_sum(t - 3)

        @pl.when(t >= 4)
        def _():
            line_sum(t - 4)

        @pl.when(t >= 5)
        def _():
            plane_sum(t - 5)

        @pl.when(t + window < chunks)
        def _():
            later = t + window
            exchange(send_b.at[later], recv_b.at[later], sem_as.at[later], sem_ar.at[later])

        @pl.when(t >= 3)
        def _():
            return_rest(t - 3)

        @pl.when(t >= 2)
        def _():
            backward(t - 2)

        @pl.when(t == chunks + 1)
        def _():
            chip_sum(t - 2)

        @pl.when(t >= 2)
        def _():
            return_first(t - 2)

        return carry

    lax.fori_loop(0, chunks + 2, steps, 0)
    last = chunks - 1
    start_loss()
    line_sum(last - 1)
    plane_sum(last - 2)
    finish(0)
    line_sum(last)
    return_rest(last)
    share_loss()
    plane_sum(last - 1)
    finish(1)
    plane_sum(last)
    lax.fori_loop(2, chunks, finish_step, 0)

    drain(lct_r.at[0 : peers - 1], sem_x.at[6])

    def add_loss(j, summed):
        return summed + lct_r[j]

    loss_ref[...] = lax.fori_loop(1, peers, add_loss, lct_r[0])
    for c in range(chunks):
        out_copy(c).wait()
        for copy in grad_copies(c):
            copy.wait()
    drain(ag_r, sem_fr.at[0])

    drain(meta_s.at[0:peers], sem_ms.at[0])
    for step in range(1, groups):
        loss_push(step).wait_send()
    drain(lct_r.at[0 : peers - 1], sem_x.at[5])

    def sent(c, carry):
        drain(send_b.at[c, 0:peers], sem_as.at[c])
        drain(bsend_b.at[c, 0:peers], sem_bs.at[c])
        drain(z_r.at[c, 0 : depth - 1], sem_zs.at[c])
        drain(y_r.at[c, 0 : breadth - 1], sem_ys.at[c])
        drain(ag_r.at[0 : 2 * depth - 1], sem_fs.at[c])
        return carry

    lax.fori_loop(0, chunks, sent, 0)


def finish_kernel(*refs):
    sources, loss_in = refs[0:5], refs[5]
    targets, loss_ref = refs[6:12], refs[12]
    held, par_b, sem_in, sem_out = refs[13:20], refs[20], refs[21], refs[22]
    ag_ref, fg_ref, sg_ref = held[4:7]
    taps, short_taps = fg_ref.shape[0], sg_ref.shape[1]
    half_rows = ag_ref.shape[1]
    ins = [pltpu.make_async_copy(sources[i], held[i], sem_in.at[i]) for i in range(5)]
    leaving = (0, 1, 2, 3, 5, 6)
    outs = [
        pltpu.make_async_copy(held[i], targets[n], sem_out.at[n]) for n, i in enumerate(leaving)
    ]
    for i in (4, 0, 1, 2, 3):
        ins[i].start()
    loss_ref[...] = loss_in[0:1, 0 : loss_ref.shape[1]]
    ins[4].wait()
    for t in range(fg_ref.shape[1] // lanes):
        cut = slice(t * lanes, (t + 1) * lanes)
        low = ag_ref[2 * t + 1].astype(F32)
        fg_ref[0:half_rows, cut] = ag_ref[2 * t].astype(F32)
        fg_ref[half_rows:taps, cut] = low[0 : taps - half_rows]
        par_b[...] = low[taps - half_rows :]
        for s in range(3):
            sg_ref[s, :, cut] = par_b[s * short_taps : (s + 1) * short_taps, :]
    outs[4].start()
    outs[5].start()
    for i in range(4):
        ins[i].wait()
        outs[i].start()
    for copy in outs:
        copy.wait()


def shards(
    query_in,
    key_in,
    value_in,
    row_place,
    short_weight,
    long_filter,
    target,
    taxon_ids,
    taxon_weight,
):
    rows, channels = query_in.shape
    peers = lax.axis_size("ctx")
    groups = lax.axis_size("ch")
    taps = long_filter.shape[0]
    short_taps = short_weight.shape[1]
    width = channels // chunks
    col_tiles = channels // lanes
    tiles = width // lanes
    blocks = peers + 1
    slots = blocks * block_rows
    ext = rows + edge
    span = taps + ext
    payload = payload_rows(taps, short_taps)
    half_rows = payload // 2
    tables = []
    made = dft_tables(rows, taps)
    for name in table_names:
        high, low = split_constant(made[name])
        tables.append(jnp.asarray(high))
        tables.append(jnp.asarray(low))
    vm = pltpu.VMEM
    dma = pltpu.SemaphoreType.DMA
    shape = jax.ShapeDtypeStruct
    loaded = (query_in, key_in, value_in, target, long_filter, *tables)
    scratch = [
        *(vm(x.shape, x.dtype) for x in loaded),
        dma((len(loaded),)),
        vm((rows, channels), BF16),
        vm((slots, 3 * rows), BF16),
        vm((3 * rows, slots), BF16),
        vm((slots, 3 * rows), BF16),
        vm((3 * rows, slots), BF16),
        vm((chunks, blocks, block_rows, width), BF16),
        vm((chunks, blocks, block_rows, width), BF16),
        vm((blocks, block_rows, lanes), BF16),
        vm((blocks, block_rows, lanes), BF16),
        vm((chunks, blocks, block_rows, width), BF16),
        vm((chunks, blocks, block_rows, width), BF16),
        vm((3, rows, channels), BF16),
        vm((3, col_tiles, rows + 2 * edge, lanes), F32),
        vm((chunks, 3, tiles, edge, lanes), BF16),
        vm((chunks, 3, tiles, edge, lanes), BF16),
        vm((chunks, 2, tiles, edge, lanes), BF16),
        vm((chunks, 2, tiles, edge, lanes), BF16),
        vm((edge, channels), BF16),
        vm((edge, channels), BF16),
        vm((edge, lanes), F32),
        vm((edge, lanes), F32),
        vm((col_tiles, rows, lanes), F32),
        vm((col_tiles, ext, lanes), F32),
        vm((col_tiles, ext, lanes), F32),
        vm((col_tiles, ext, lanes), F32),
        vm((col_tiles, span, lanes), BF16),
        vm((col_tiles, span, lanes), BF16),
        vm((col_tiles, 2 * rows, lanes), F32),
        vm((3, 8, channels), F32),
        vm((3, ext, lanes), F32),
        vm((3 * rows, 2 * lanes), BF16),
        vm((rows, lanes), F32),
        vm((rows, lanes), F32),
        vm((payload - taps, lanes), F32),
        vm((chunks, 2, tiles, half_rows, lanes), F32),
        vm((chunks, tiles, half_rows, lanes), F32),
        vm((chunks, tiles, half_rows, lanes), BF16),
        vm((chunks, tiles, half_rows, lanes), BF16),
        vm((chunks, half_rows, lanes), BF16),
        vm((chunks, peers // (2 * tiles), half_rows, lanes), BF16),
        vm((chunks, half_rows, lanes), BF16),
        vm((8, lanes), F32),
        vm((groups, 8, lanes), F32),
        vm((8, lanes), F32),
        vm((peers, 8, lanes), F32),
        dma((chunks,)),
        dma((chunks,)),
        dma((chunks,)),
        dma((chunks,)),
        dma((chunks,)),
        dma((chunks,)),
        dma((chunks,)),
        dma((chunks,)),
        dma((2 * chunks,)),
        dma((2 * chunks,)),
        dma((1,)),
        dma((1,)),
        dma((chunks,)),
        dma((chunks,)),
        dma((chunks,)),
        dma((chunks,)),
        dma((chunks,)),
        dma((chunks,)),
        dma((chunks,)),
        dma((1,)),
        dma((2 * chunks,)),
        dma((16,)),
    ]
    here = pl.BlockSpec(memory_space=pltpu.VMEM)
    away = pl.BlockSpec(memory_space=pl.ANY)
    *moved, gathered, losses = pl.pallas_call(
        lambda *refs: whole_kernel(peers, groups, *refs),
        out_shape=(
            *(shape((rows, channels), BF16) for _ in range(4)),
            shape((peers, half_rows, lanes), BF16),
            shape((8, lanes), F32),
        ),
        in_specs=[here] * 4 + [away] * len(loaded),
        out_specs=[away] * 5 + [here],
        scratch_shapes=scratch,
        compiler_params=pltpu.CompilerParams(
            collective_id=0, has_side_effects=True, vmem_limit_bytes=63_000_000
        ),
        name="hyena",
    )(
        row_place.reshape(1, rows),
        taxon_ids.reshape(1, rows),
        taxon_weight.reshape(1, -1),
        short_weight,
        *loaded,
    )
    count = taxon_weight.shape[0]
    gated_out, query_grad, key_grad, value_grad, filter_grad, short_grad, losses = pl.pallas_call(
        finish_kernel,
        out_shape=(
            *(shape((rows, channels), BF16) for _ in range(4)),
            shape((taps, channels), F32),
            shape((3, short_taps, channels), F32),
            shape((1, count), F32),
        ),
        in_specs=[away] * 5 + [here],
        out_specs=[away] * 6 + [here],
        scratch_shapes=[
            *(vm((rows, channels), BF16) for _ in range(4)),
            vm((peers, half_rows, lanes), BF16),
            vm((taps, channels), F32),
            vm((3, short_taps, channels), F32),
            vm((payload - taps, lanes), F32),
            dma((5,)),
            dma((6,)),
        ],
        name="finish",
    )(*moved, gathered, losses)
    return (
        gated_out,
        query_grad,
        key_grad,
        value_grad,
        filter_grad,
        short_grad,
        losses.reshape(count),
    )


def solution(mesh):
    placed = (
        P("ctx", "ch"),
        P("ctx", "ch"),
        P("ctx", "ch"),
        P("ctx"),
        P(None, None, "ch"),
        P(None, "ch"),
        P("ctx", "ch"),
        P("ctx"),
        P(),
    )
    return jax.shard_map(
        shards,
        mesh=mesh,
        in_specs=placed,
        out_specs=(
            P("ctx", "ch"),
            P("ctx", "ch"),
            P("ctx", "ch"),
            P("ctx", "ch"),
            P(None, "ch"),
            P(None, None, "ch"),
            P(),
        ),
        check_vma=False,
    )
```

```python
import math

import jax
import jax.numpy as jnp
import numpy as np
from jax import lax
from jax.experimental import pallas as pl
from jax.experimental.pallas import tpu as pltpu
from jax.sharding import PartitionSpec as P

MESH = pl.DeviceIdType.MESH
F32 = jnp.float32
BF16 = jnp.bfloat16
unit = 5
block_rows = 16
lanes = 128
edge = 16
chunks = 4
stride = 7
window = 2
stream_step = 1024.0


def split_constant(array):
    high = array.astype(np.float32).astype(jnp.bfloat16)
    low = (array - high.astype(np.float64)).astype(np.float32).astype(jnp.bfloat16)
    return high, low


def dft_tables(rows, taps):
    half = rows
    size = 2 * rows
    span = taps + rows + edge
    theta = np.pi * (2 * np.arange(half) + 1) / size

    def ahead(index):
        angle = theta[:, None] * index[None, :]
        return np.concatenate([np.cos(angle), -np.sin(angle)], axis=0)

    def back(index):
        angle = theta[None, :] * index[:, None]
        return np.concatenate([np.cos(angle), -np.sin(angle)], axis=1) * (2.0 / size)

    tables = {
        "ahead": ahead(np.arange(span)),
        "own": ahead(np.arange(rows)),
        "later": ahead(np.arange(rows, rows + taps + edge)),
        "taps": ahead(np.arange(taps)),
        "mixed": back(np.arange(rows + edge) + taps),
        "gated": back(np.arange(rows + edge)),
        "filter": back(taps - np.arange(taps)),
    }
    return tables


back_names = ("mixed", "gated", "filter")
table_names = ("taps", "ahead", "own", "later", "mixed", "gated", "filter")


def payload_rows(taps, short_taps):
    return -(-(taps + 3 * short_taps) // 32) * 32


def iota(shape, axis):
    return lax.broadcasted_iota(jnp.int32, shape, axis)


def slot_facts(index):
    block = lax.shift_right_logical(index, 4)
    row = jnp.bitwise_and(index, block_rows - 1)
    stream = jnp.where(row >= unit, 1, 0) + jnp.where(row >= 2 * unit, 1, 0)
    rank = row - unit * stream
    valid = row < 3 * unit
    return block, stream, rank, valid


def whole_kernel(
    peers,
    groups,
    place_ref,
    taxon_ref,
    weight_ref,
    short_ref,
    *refs,
):
    far = refs[:12]
    out_hbm, qg_hbm, kg_hbm, vg_hbm, ag_r, loss_ref = refs[12:18]
    near = refs[18:30]
    (
        q_ref,
        k_ref,
        v_ref,
        target_ref,
        filter_ref,
        taps_t,
        ahead_t,
        own_t,
        later_t,
        mixed_t,
        gated_t,
        filter_t,
    ) = near
    sem_in = refs[30]
    (
        out_ref,
        pack_m,
        unpack_m,
        place_m,
        return_m,
        send_b,
        recv_b,
        meta_s,
        meta_r,
        bsend_b,
        brecv_b,
        grads_b,
        rows_b,
        prev_s,
        prev_r,
        next_s,
        next_r,
        tnext_s,
        tnext_r,
        wnext_s,
        wnext_r,
        qc_b,
        kc_b,
        vc_b,
        go_b,
        gext_b,
        gm_b,
        spec_b,
        short_b,
        gbuf,
        gr_b,
        lacc,
        ids_b,
        par_b,
        half_b,
        half_r,
        z_s,
        z_r,
        y_s,
        y_r,
        f_s,
        lch_s,
        lch_r,
        lct_s,
        lct_r,
        sem_as,
        sem_ar,
        sem_bs,
        sem_br,
        sem_ps,
        sem_pr,
        sem_ns,
        sem_nr,
        sem_gs,
        sem_gr,
        sem_ms,
        sem_mr,
        sem_hs,
        sem_hr,
        sem_zs,
        sem_zr,
        sem_ys,
        sem_yr,
        sem_fs,
        sem_fr,
        sem_out,
        sem_x,
    ) = refs[31:]
    rows, channels = q_ref.shape
    taps = filter_ref.shape[0]
    short_taps = short_ref.shape[1]
    width = channels // chunks
    col_tiles = channels // lanes
    tiles = width // lanes
    pairs = tiles // 2
    blocks = peers + 1
    slots = blocks * block_rows
    ext = rows + edge
    payload = payload_rows(taps, short_taps)
    half_rows = payload // 2
    me = lax.axis_index("ctx")
    depth = tiles
    breadth = peers // (2 * depth)
    core = lax.rem(me, 2)
    my_y = lax.rem(me // 2, breadth)
    my_z = me // (2 * breadth)
    partner = me + 1 - 2 * core
    ch = lax.axis_index("ch")
    right = lax.rem(me + 1, peers)
    left = lax.rem(me + peers - 1, peers)
    grad_scale = 1.0 / math.sqrt(rows * peers)
    loss_scale = 1.0 / math.sqrt(channels * groups * rows * peers / weight_ref.shape[1])

    barrier = pltpu.get_barrier_semaphore()

    def greet(step, carry):
        pl.semaphore_signal(
            barrier, inc=1, device_id=(lax.rem(me + step, peers), ch), device_id_type=MESH
        )
        return carry

    lax.fori_loop(1, peers, greet, 0)
    for step in range(1, groups):
        pl.semaphore_signal(
            barrier, inc=1, device_id=(me, lax.rem(ch + step, groups)), device_id_type=MESH
        )

    def fetch(index):
        return pltpu.make_async_copy(far[index], near[index], sem_in.at[index])

    for index in range(len(far)):
        fetch(index).start()

    def push(src, dst, send_sem, recv_sem, ctx_to, ch_to):
        return pltpu.make_async_remote_copy(
            src_ref=src,
            dst_ref=dst,
            send_sem=send_sem,
            recv_sem=recv_sem,
            device_id=(ctx_to, ch_to),
            device_id_type=MESH,
        )

    def drain(ref, sem):
        pltpu.make_async_copy(ref, ref, sem).wait()

    def column(row_vector, count):
        eye = iota((count, count), 0) == iota((count, count), 1)
        return jnp.sum(jnp.where(eye, row_vector, 0.0), axis=1, keepdims=True)

    place_row = place_ref[...].astype(F32)
    place3_row = jnp.concatenate([place_row] * 3, axis=1)
    owner_row = jnp.floor((place_row + 0.5) * (1.0 / rows))
    owner3_row = jnp.floor((place3_row + 0.5) * (1.0 / rows))
    owner_col = column(owner_row, rows)
    place_col = column(place_row, rows)
    local_col = place_col - owner_col * rows

    def slot_key(owner, rank):
        return jnp.where(
            rank < unit - 0.5, owner * unit + rank, float(peers * unit) + rank - unit
        )

    order3 = iota((rows, 3 * rows), 1)
    stream3 = jnp.where(order3 >= rows, 1, 0) + jnp.where(order3 >= 2 * rows, 1, 0)
    before3 = iota((rows, 3 * rows), 0) < order3 - rows * stream3
    rank3_row = jnp.sum(
        jnp.where(jnp.logical_and(owner_col == owner3_row, before3), 1.0, 0.0),
        axis=0,
        keepdims=True,
    )
    key3_row = slot_key(owner3_row, rank3_row)
    before = iota((rows, rows), 1) < iota((rows, rows), 0)
    rank_col = jnp.sum(
        jnp.where(jnp.logical_and(owner_col == owner_row, before), 1.0, 0.0),
        axis=1,
        keepdims=True,
    )
    key_col = slot_key(owner_col, rank_col)

    lane3 = iota((1, 3 * rows), 1)
    lane_stream = jnp.where(lane3 >= rows, 1, 0) + jnp.where(lane3 >= 2 * rows, 1, 0)
    lane_local = lane3 - rows * lane_stream

    def static_key(shape, axis):
        block, stream, rank, valid = slot_facts(iota(shape, axis))
        key = jnp.where(valid, stream * 1024 + block * unit + rank, -1)
        return key.astype(F32), jnp.where(valid, stream * 1024, -4096).astype(F32)

    slot_key_col, slot_stream_col = static_key((slots, 1), 0)
    slot_key_row, slot_stream_row = static_key((1, slots), 1)
    full3_row = key3_row + lane_stream.astype(F32) * stream_step
    pack_m[...] = jnp.where(slot_key_col == full3_row, 1.0, 0.0).astype(BF16)
    meta_col = jnp.broadcast_to(local_col + 1.0, (rows, lanes)).astype(BF16)
    meta3 = jnp.concatenate([meta_col] * 3, axis=0)
    meta_s[...] = (
        jnp.dot(pack_m[...], meta3, preferred_element_type=F32)
        .astype(BF16)
        .reshape(blocks, block_rows, lanes)
    )

    pair_lanes = 2 * lanes

    def pack(c, carry):
        def body(u, inner):
            base = pl.multiple_of(c * width + u * pair_lanes, pair_lanes)
            cols = pl.ds(base, pair_lanes)
            stacked = jnp.concatenate([q_ref[:, cols], k_ref[:, cols], v_ref[:, cols]], axis=0)
            packed = jnp.dot(pack_m[...], stacked, preferred_element_type=F32).astype(BF16)
            local = pl.ds(pl.multiple_of(u * pair_lanes, pair_lanes), pair_lanes)
            send_b[c, :, :, local] = packed.reshape(blocks, block_rows, pair_lanes)
            return inner

        lax.fori_loop(0, pairs, body, 0)
        return carry

    wait_for = peers - 1 + groups - 1

    def exchange(source, landing, send_sem, recv_sem):
        pltpu.make_async_copy(source.at[me], landing.at[me], recv_sem).start()
        push(source.at[peers], landing.at[peers], send_sem, recv_sem, right, ch).start()

        def body(step, carry):
            to = lax.rem(me + step * stride, peers)
            push(source.at[to], landing.at[me], send_sem, recv_sem, to, ch).start()
            return carry

        lax.fori_loop(1, peers, body, 0)

    near_peers = peers // 2

    def return_some(c, first, last):
        def body(step, carry):
            to = lax.rem(me + step * stride, peers)
            push(bsend_b.at[c, to], brecv_b.at[c, me], sem_bs.at[c], sem_br.at[c], to, ch).start()
            return carry

        lax.fori_loop(first, last, body, 0)

    def return_first(c):
        pltpu.make_async_copy(bsend_b.at[c, me], brecv_b.at[c, me], sem_br.at[c]).start()
        push(
            bsend_b.at[c, peers], brecv_b.at[c, peers], sem_bs.at[c], sem_br.at[c], left, ch
        ).start()
        return_some(c, 1, near_peers)

    def return_rest(c):
        return_some(c, near_peers, peers)

    for index in range(3):
        fetch(index).wait()
    pack(0, 0)
    pl.semaphore_wait(barrier, wait_for)
    exchange(meta_s, meta_r, sem_ms.at[0], sem_mr.at[0])
    target_push = push(tnext_s, tnext_r, sem_x.at[0], sem_x.at[1], left, ch)
    weight_push = push(wnext_s, wnext_r, sem_x.at[12], sem_x.at[13], left, ch)
    exchange(send_b.at[0], recv_b.at[0], sem_as.at[0], sem_ar.at[0])

    def pack_and_send(c, carry):
        pack(c, 0)
        exchange(send_b.at[c], recv_b.at[c], sem_as.at[c], sem_ar.at[c])
        return carry

    lax.fori_loop(1, window, pack_and_send, 0)
    fetch(3).wait()
    ids_row = taxon_ref[...].astype(F32)
    ids_col = column(ids_row, rows)
    count = weight_ref.shape[1]
    taxon_hot = iota((rows, lanes), 1).astype(F32) == ids_col
    weights = jnp.concatenate([weight_ref[...], jnp.zeros((1, lanes - count), F32)], axis=1)
    weight_col = jnp.sum(jnp.where(taxon_hot, weights, 0.0), axis=1, keepdims=True)
    ids_b[...] = jnp.broadcast_to(ids_col, (rows, lanes))
    tnext_s[...] = target_ref[0:edge, :]
    wnext_s[...] = jnp.broadcast_to(weight_col[0:edge], (edge, lanes))
    target_push.start()
    weight_push.start()
    for s in range(3):
        return_m[s * rows : (s + 1) * rows, :] = jnp.where(
            key_col + s * stream_step == slot_key_row, 1.0, 0.0
        ).astype(BF16)

    lax.fori_loop(window, chunks, pack, 0)
    for index in range(4, len(far)):
        fetch(index).wait()

    short_b[:, 0:short_taps, :] = short_ref[...].astype(F32)

    def both(table, x):
        return jnp.dot(
            table[...], jnp.concatenate([x, x], axis=0), preferred_element_type=F32
        )

    def filter_spectrum(u, carry):
        cols = pl.ds(pl.multiple_of(u * pair_lanes, pair_lanes), pair_lanes)
        x = filter_ref[:, cols]
        found = both(taps_t, x)
        spec_b[2 * u] = found[:, :lanes]
        spec_b[2 * u + 1] = found[:, lanes:]
        return carry

    lax.fori_loop(0, col_tiles // 2, filter_spectrum, 0)
    lacc[...] = jnp.zeros_like(lacc)
    par_b[...] = jnp.zeros_like(par_b)

    drain(meta_r, sem_mr.at[0])
    meta = meta_r[...].reshape(slots, lanes)
    pick = jnp.where(iota((8, lanes), 1) == 0, 1.0, 0.0).astype(BF16)
    found_row = lax.dot_general(
        pick, meta, (((1,), (1,)), ((), ())), preferred_element_type=F32
    )[0:1, :]
    landed_row = found_row + slot_stream_row
    landed_col = meta[:, 0:1].astype(F32) + slot_stream_col
    target_lane = (lane_local + 1).astype(F32) + lane_stream.astype(F32) * stream_step
    place_m[...] = jnp.where(landed_col == target_lane, 1.0, 0.0).astype(BF16)
    own_index = (iota((rows, 1), 0) + 1).astype(F32)
    for s in range(3):
        unpack_m[s * rows : (s + 1) * rows, :] = jnp.where(
            own_index + s * stream_step == landed_row, 1.0, 0.0
        ).astype(BF16)
    target_push.wait()
    weight_push.wait()
    not_first = jnp.where(me > 0, 1.0, 0.0)
    not_last = jnp.where(me < peers - 1, 1.0, 0.0)

    def tile_range(c):
        return pl.ds(c * tiles, tiles)

    def prev_push(c):
        return push(prev_s.at[c], prev_r.at[c], sem_ps.at[c], sem_pr.at[c], right, ch)

    def next_push(c):
        return push(next_s.at[c], next_r.at[c], sem_ns.at[c], sem_nr.at[c], left, ch)

    def gated_push(c):
        return push(
            gext_b.at[tile_range(c), taps_at : taps_at + taps, :],
            gext_b.at[tile_range(c), 0:taps, :],
            sem_gs.at[c],
            sem_gr.at[c],
            right,
            ch,
        )

    taps_at = rows

    def mixed_push(c):
        return push(
            gm_b.at[tile_range(c), 0 : taps + edge, :],
            gm_b.at[tile_range(c), rows : rows + taps + edge, :],
            sem_gs.at[chunks + c],
            sem_gr.at[chunks + c],
            left,
            ch,
        )

    def land(c):
        drain(recv_b.at[c], sem_ar.at[c])

        def body(u, carry):
            local = pl.ds(pl.multiple_of(u * pair_lanes, pair_lanes), pair_lanes)
            got = recv_b[c, :, :, local].reshape(slots, pair_lanes)
            placed = jnp.dot(unpack_m[...], got, preferred_element_type=F32)
            for part in range(2):
                at = c * tiles + 2 * u + part
                piece = placed[:, part * lanes : (part + 1) * lanes]
                for s in range(3):
                    rows_b[s, at, edge : edge + rows, :] = piece[s * rows : (s + 1) * rows]
                    prev_s[c, s, 2 * u + part] = piece[
                        (s + 1) * rows - edge : (s + 1) * rows
                    ].astype(BF16)
                    if s > 0:
                        next_s[c, s - 1, 2 * u + part] = piece[
                            s * rows : s * rows + edge
                        ].astype(BF16)
            return carry

        lax.fori_loop(0, pairs, body, 0)
        prev_push(c).start()
        next_push(c).start()

    def convolve(c):
        prev_push(c).wait()
        next_push(c).wait()

        def body(u, carry):
            at = c * tiles + u
            cols = pl.ds(pl.multiple_of(at * lanes, lanes), lanes)
            for s in range(3):
                rows_b[s, at, 0:edge, :] = prev_r[c, s, u].astype(F32) * not_first
            for s in range(2):
                rows_b[s + 1, at, edge + rows : 2 * edge + rows, :] = next_r[c, s, u].astype(F32)

            def conv(s, total):
                summed = None
                for j in range(short_taps):
                    term = (
                        short_b[s, j : j + 1, cols]
                        * rows_b[s, at, edge - j : edge - j + total, :]
                    )
                    summed = term if summed is None else summed + term
                return summed

            k_conv = conv(1, ext)
            v_conv = conv(2, ext)
            kc_b[at] = k_conv
            vc_b[at] = v_conv
            gext_b[at, taps : taps + ext, :] = (k_conv * v_conv).astype(BF16)
            q_conv = conv(0, rows)
            qc_b[at] = q_conv
            out_grad = weight_col[0:rows] * target_ref[:, cols].astype(F32)
            go_b[at, 0:rows, :] = out_grad
            go_b[at, rows:ext, :] = (
                wnext_r[...] * tnext_r[:, cols].astype(F32) * not_last
            )
            gm_b[at, 0:rows, :] = (out_grad * q_conv).astype(BF16)
            return carry

        lax.fori_loop(0, tiles, body, 0)
        gated_push(c).start()
        mixed_push(c).start()

    def inverse(table, real, imag):
        y = jnp.concatenate([real, imag], axis=0)
        y_hi = y.astype(BF16)
        y_lo = (y - y_hi.astype(F32)).astype(BF16)
        stacked = jnp.concatenate([y_hi, y_lo, y_hi], axis=0)
        return jnp.dot(table[...], stacked, preferred_element_type=F32)

    def backward(c):
        gated_push(c).wait()
        mixed_push(c).wait()

        @pl.when(me == 0)
        def _():
            def clear(u, carry):
                gext_b[c * tiles + u, 0:taps, :] = jnp.zeros((taps, lanes), BF16)
                return carry

            lax.fori_loop(0, tiles, clear, 0)

        @pl.when(me == peers - 1)
        def _():
            def clear(u, carry):
                gm_b[c * tiles + u, rows : rows + taps + edge, :] = jnp.zeros(
                    (taps + edge, lanes), BF16
                )
                return carry

            lax.fori_loop(0, tiles, clear, 0)

        def body(u, carry):
            first = c * tiles + 2 * u
            gx = jnp.concatenate([gext_b[first], gext_b[first + 1]], axis=1)
            g_own = jnp.concatenate(
                [gm_b[first, 0:rows, :], gm_b[first + 1, 0:rows, :]], axis=1
            )
            g_later = jnp.concatenate(
                [
                    gm_b[first, rows : rows + taps + edge, :],
                    gm_b[first + 1, rows : rows + taps + edge, :],
                ],
                axis=1,
            )
            spec = jnp.concatenate([spec_b[first], spec_b[first + 1]], axis=1)
            fr, fi = spec[:rows], spec[rows:]
            sg = both(ahead_t, gx)
            gr, gi = sg[:rows], sg[rows:]
            mixed = inverse(mixed_t, fr * gr - fi * gi, fr * gi + fi * gr)
            so = both(own_t, g_own)
            mr, mi = so[:rows], so[rows:]
            taps_grad = inverse(filter_t, mr * gr + mi * gi, mr * gi - mi * gr)
            sl = both(later_t, g_later)
            ar, ai = mr + sl[:rows], mi + sl[rows:]
            gated_grad = inverse(gated_t, fr * ar + fi * ai, fr * ai - fi * ar)
            for part in range(2):
                at = first + part
                cols = pl.ds(pl.multiple_of(at * lanes, lanes), lanes)
                lane_cut = slice(part * lanes, (part + 1) * lanes)
                mix = mixed[:, lane_cut]
                gg = gated_grad[:, lane_cut]
                tile = 2 * u + part
                found_taps = taps_grad[:, lane_cut]
                half_b[c, 0, tile] = found_taps[0:half_rows]
                half_b[c, 1, tile, 0 : taps - half_rows, :] = found_taps[half_rows:]
                out = (qc_b[at] * mix[:rows]).astype(BF16)
                out_ref[:, cols] = out
                lacc[...] += out.astype(F32) * target_ref[:, cols].astype(F32)
                gbuf[0] = go_b[at] * mix
                gbuf[1] = gg * vc_b[at]
                gbuf[2] = gg * kc_b[at]
                for s in range(3):
                    own = rows_b[s, at, edge : edge + rows, :]
                    back = None
                    for j in range(short_taps):
                        ahead = gbuf[s, j : j + rows, :]
                        found = jnp.sum(ahead * own, axis=0, keepdims=True)
                        par_b[s * short_taps + j : s * short_taps + j + 1, :] = found
                        term = short_b[s, j : j + 1, cols] * ahead
                        back = term if back is None else back + term
                    gr_b[s * rows : (s + 1) * rows, lane_cut] = back.astype(BF16)
                half_b[c, 1, tile, taps - half_rows : half_rows, :] = par_b[...]
            local = pl.ds(pl.multiple_of(u * pair_lanes, pair_lanes), pair_lanes)
            packed = jnp.dot(place_m[...], gr_b[...], preferred_element_type=F32).astype(BF16)
            bsend_b[c, :, :, local] = packed.reshape(blocks, block_rows, pair_lanes)
            return carry

        lax.fori_loop(0, pairs, body, 0)
        out_copy(c).start()

        half_push(c).start()

    def half_push(c):
        return push(
            half_b.at[c, 1 - core], half_r.at[c], sem_hs.at[c], sem_hr.at[c], partner, ch
        )

    def chip_sum(c):
        half_push(c).wait()

        def body(t, carry):
            z_s[c, t] = (half_b[c, core, t] + half_r[c, t]).astype(BF16)
            return carry

        lax.fori_loop(0, depth, body, 0)
        pltpu.make_async_copy(z_s.at[c, my_z], z_r.at[c, my_z], sem_zr.at[c]).start()

        def send(step, carry):
            z_to = lax.rem(my_z + step, depth)
            to = (z_to * breadth + my_y) * 2 + core
            push(z_s.at[c, z_to], z_r.at[c, my_z], sem_zs.at[c], sem_zr.at[c], to, ch).start()
            return carry

        lax.fori_loop(1, depth, send, 0)

    def line_sum(c):
        drain(z_r.at[c], sem_zr.at[c])
        summed = z_r[c, 0].astype(F32)
        for z in range(1, depth):
            summed = summed + z_r[c, z].astype(F32)
        y_s[c] = summed.astype(BF16)
        pltpu.make_async_copy(y_s.at[c], y_r.at[c, my_y], sem_yr.at[c]).start()

        def send(step, carry):
            y_to = lax.rem(my_y + step, breadth)
            to = (my_z * breadth + y_to) * 2 + core
            push(y_s.at[c], y_r.at[c, my_y], sem_ys.at[c], sem_yr.at[c], to, ch).start()
            return carry

        lax.fori_loop(1, breadth, send, 0)

    def plane_sum(c):
        drain(y_r.at[c], sem_yr.at[c])
        summed = y_r[c, 0].astype(F32)
        for y in range(1, breadth):
            summed = summed + y_r[c, y].astype(F32)
        f_s[c] = (summed * grad_scale).astype(BF16)
        piece = (c * depth + my_z) * 2 + core
        pltpu.make_async_copy(f_s.at[c], ag_r.at[piece], sem_fr.at[0]).start()
        push(f_s.at[c], ag_r.at[piece], sem_fs.at[c], sem_fr.at[0], partner, ch).start()

        def send(step, carry):
            z_to = lax.rem(my_z + step, depth)
            to = (z_to * breadth + my_y) * 2
            push(f_s.at[c], ag_r.at[piece], sem_fs.at[c], sem_fr.at[0], to, ch).start()
            push(f_s.at[c], ag_r.at[piece], sem_fs.at[c], sem_fr.at[0], to + 1, ch).start()
            return carry

        lax.fori_loop(1, depth, send, 0)

    def grad_copies(c):
        cols = pl.ds(pl.multiple_of(c * width, width), width)
        return [
            pltpu.make_async_copy(grads_b.at[s, :, cols], to.at[:, cols], sem_out.at[chunks + c])
            for s, to in enumerate((qg_hbm, kg_hbm, vg_hbm))
        ]

    def finish(c):
        drain(brecv_b.at[c], sem_br.at[c])

        def body(u, inner):
            local = pl.ds(pl.multiple_of(u * pair_lanes, pair_lanes), pair_lanes)
            cols = pl.ds(pl.multiple_of(c * width + u * pair_lanes, pair_lanes), pair_lanes)
            got = brecv_b[c, :, :, local].reshape(slots, pair_lanes)
            back = jnp.dot(return_m[...], got, preferred_element_type=F32).astype(BF16)
            for s in range(3):
                grads_b[s, :, cols] = back[s * rows : (s + 1) * rows]
            return inner

        lax.fori_loop(0, pairs, body, 0)
        for copy in grad_copies(c):
            copy.start()

    def finish_step(c, carry):
        finish(c)
        return carry

    def out_copy(c):
        cols = pl.ds(pl.multiple_of(c * width, width), width)
        return pltpu.make_async_copy(out_ref.at[:, cols], out_hbm.at[:, cols], sem_out.at[c])

    def loss_push(step):
        return push(
            lch_s, lch_r.at[ch], sem_x.at[8 + step], sem_x.at[2], me, lax.rem(ch + step, groups)
        )

    def start_loss():
        row_loss = jnp.sum(lacc[...], axis=1, keepdims=True)
        hot = iota((rows, lanes), 1).astype(F32) == ids_b[...]
        taxon_part = jnp.sum(jnp.where(hot, row_loss, 0.0), axis=0, keepdims=True) * loss_scale
        lch_s[...] = jnp.broadcast_to(taxon_part, (8, lanes))
        lch_r[ch] = jnp.broadcast_to(taxon_part, (8, lanes))
        for step in range(1, groups):
            loss_push(step).start()

    def share_loss():
        if groups > 1:
            drain(lch_r.at[0 : groups - 1], sem_x.at[2])
        total = lch_r[0]
        for g in range(1, groups):
            total = total + lch_r[g]
        lct_s[...] = total
        lct_r[me] = total

        def send(step, carry):
            to = lax.rem(me + step, peers)
            push(lct_s, lct_r.at[me], sem_x.at[5], sem_x.at[6], to, ch).start()
            return carry

        lax.fori_loop(1, peers, send, 0)

    def steps(t, carry):
        @pl.when(t < chunks)
        def _():
            land(t)

        @pl.when(jnp.logical_and(t >= 1, t < chunks + 1))
        def _():
            convolve(t - 1)

        @pl.when(t >= 3)
        def _():
            chip_sum(t - 3)

        @pl.when(t >= 4)
        def _():
            line_sum(t - 4)

        @pl.when(t >= 5)
        def _():
            plane_sum(t - 5)

        @pl.when(t + window < chunks)
        def _():
            later = t + window
            exchange(send_b.at[later], recv_b.at[later], sem_as.at[later], sem_ar.at[later])

        @pl.when(t >= 3)
        def _():
            return_rest(t - 3)

        @pl.when(t >= 2)
        def _():
            backward(t - 2)

        @pl.when(t == chunks + 1)
        def _():
            chip_sum(t - 2)

        @pl.when(t >= 2)
        def _():
            return_first(t - 2)

        return carry

    lax.fori_loop(0, chunks + 2, steps, 0)
    last = chunks - 1
    start_loss()
    line_sum(last - 1)
    plane_sum(last - 2)
    finish(0)
    line_sum(last)
    return_rest(last)
    share_loss()
    plane_sum(last - 1)
    finish(1)
    plane_sum(last)
    lax.fori_loop(2, chunks, finish_step, 0)

    drain(lct_r.at[0 : peers - 1], sem_x.at[6])

    def add_loss(j, summed):
        return summed + lct_r[j]

    loss_ref[...] = lax.fori_loop(1, peers, add_loss, lct_r[0])
    for c in range(chunks):
        out_copy(c).wait()
        for copy in grad_copies(c):
            copy.wait()
    drain(ag_r, sem_fr.at[0])

    drain(meta_s.at[0:peers], sem_ms.at[0])
    for step in range(1, groups):
        loss_push(step).wait_send()
    drain(lct_r.at[0 : peers - 1], sem_x.at[5])

    def sent(c, carry):
        drain(send_b.at[c, 0:peers], sem_as.at[c])
        drain(bsend_b.at[c, 0:peers], sem_bs.at[c])
        drain(z_r.at[c, 0 : depth - 1], sem_zs.at[c])
        drain(y_r.at[c, 0 : breadth - 1], sem_ys.at[c])
        drain(ag_r.at[0 : 2 * depth - 1], sem_fs.at[c])
        return carry

    lax.fori_loop(0, chunks, sent, 0)


def finish_kernel(*refs):
    sources, loss_in = refs[0:5], refs[5]
    targets, loss_ref = refs[6:12], refs[12]
    held, par_b, sem_in, sem_out = refs[13:20], refs[20], refs[21], refs[22]
    ag_ref, fg_ref, sg_ref = held[4:7]
    taps, short_taps = fg_ref.shape[0], sg_ref.shape[1]
    half_rows = ag_ref.shape[1]
    ins = [pltpu.make_async_copy(sources[i], held[i], sem_in.at[i]) for i in range(5)]
    leaving = (0, 1, 2, 3, 5, 6)
    outs = [
        pltpu.make_async_copy(held[i], targets[n], sem_out.at[n]) for n, i in enumerate(leaving)
    ]
    for i in (4, 0, 1, 2, 3):
        ins[i].start()
    loss_ref[...] = loss_in[0:1, 0 : loss_ref.shape[1]]
    ins[4].wait()
    for t in range(fg_ref.shape[1] // lanes):
        cut = slice(t * lanes, (t + 1) * lanes)
        low = ag_ref[2 * t + 1].astype(F32)
        fg_ref[0:half_rows, cut] = ag_ref[2 * t].astype(F32)
        fg_ref[half_rows:taps, cut] = low[0 : taps - half_rows]
        par_b[...] = low[taps - half_rows :]
        for s in range(3):
            sg_ref[s, :, cut] = par_b[s * short_taps : (s + 1) * short_taps, :]
    outs[4].start()
    outs[5].start()
    for i in range(4):
        ins[i].wait()
        outs[i].start()
    for copy in outs:
        copy.wait()


def shards(
    query_in,
    key_in,
    value_in,
    row_place,
    short_weight,
    long_filter,
    target,
    taxon_ids,
    taxon_weight,
):
    rows, channels = query_in.shape
    peers = lax.axis_size("ctx")
    groups = lax.axis_size("ch")
    taps = long_filter.shape[0]
    short_taps = short_weight.shape[1]
    width = channels // chunks
    col_tiles = channels // lanes
    tiles = width // lanes
    blocks = peers + 1
    slots = blocks * block_rows
    ext = rows + edge
    span = taps + ext
    payload = payload_rows(taps, short_taps)
    half_rows = payload // 2
    tables = []
    made = dft_tables(rows, taps)
    for name in table_names:
        high, low = split_constant(made[name])
        parts = (high, high, low) if name in back_names else (high, low)
        tables.append(jnp.asarray(np.concatenate(parts, axis=1)))
    vm = pltpu.VMEM
    dma = pltpu.SemaphoreType.DMA
    shape = jax.ShapeDtypeStruct
    loaded = (query_in, key_in, value_in, target, long_filter, *tables)
    scratch = [
        *(vm(x.shape, x.dtype) for x in loaded),
        dma((len(loaded),)),
        vm((rows, channels), BF16),
        vm((slots, 3 * rows), BF16),
        vm((3 * rows, slots), BF16),
        vm((slots, 3 * rows), BF16),
        vm((3 * rows, slots), BF16),
        vm((chunks, blocks, block_rows, width), BF16),
        vm((chunks, blocks, block_rows, width), BF16),
        vm((blocks, block_rows, lanes), BF16),
        vm((blocks, block_rows, lanes), BF16),
        vm((chunks, blocks, block_rows, width), BF16),
        vm((chunks, blocks, block_rows, width), BF16),
        vm((3, rows, channels), BF16),
        vm((3, col_tiles, rows + 2 * edge, lanes), F32),
        vm((chunks, 3, tiles, edge, lanes), BF16),
        vm((chunks, 3, tiles, edge, lanes), BF16),
        vm((chunks, 2, tiles, edge, lanes), BF16),
        vm((chunks, 2, tiles, edge, lanes), BF16),
        vm((edge, channels), BF16),
        vm((edge, channels), BF16),
        vm((edge, lanes), F32),
        vm((edge, lanes), F32),
        vm((col_tiles, rows, lanes), F32),
        vm((col_tiles, ext, lanes), F32),
        vm((col_tiles, ext, lanes), F32),
        vm((col_tiles, ext, lanes), F32),
        vm((col_tiles, span, lanes), BF16),
        vm((col_tiles, span, lanes), BF16),
        vm((col_tiles, 2 * rows, lanes), F32),
        vm((3, 8, channels), F32),
        vm((3, ext, lanes), F32),
        vm((3 * rows, 2 * lanes), BF16),
        vm((rows, lanes), F32),
        vm((rows, lanes), F32),
        vm((payload - taps, lanes), F32),
        vm((chunks, 2, tiles, half_rows, lanes), F32),
        vm((chunks, tiles, half_rows, lanes), F32),
        vm((chunks, tiles, half_rows, lanes), BF16),
        vm((chunks, tiles, half_rows, lanes), BF16),
        vm((chunks, half_rows, lanes), BF16),
        vm((chunks, peers // (2 * tiles), half_rows, lanes), BF16),
        vm((chunks, half_rows, lanes), BF16),
        vm((8, lanes), F32),
        vm((groups, 8, lanes), F32),
        vm((8, lanes), F32),
        vm((peers, 8, lanes), F32),
        dma((chunks,)),
        dma((chunks,)),
        dma((chunks,)),
        dma((chunks,)),
        dma((chunks,)),
        dma((chunks,)),
        dma((chunks,)),
        dma((chunks,)),
        dma((2 * chunks,)),
        dma((2 * chunks,)),
        dma((1,)),
        dma((1,)),
        dma((chunks,)),
        dma((chunks,)),
        dma((chunks,)),
        dma((chunks,)),
        dma((chunks,)),
        dma((chunks,)),
        dma((chunks,)),
        dma((1,)),
        dma((2 * chunks,)),
        dma((16,)),
    ]
    here = pl.BlockSpec(memory_space=pltpu.VMEM)
    away = pl.BlockSpec(memory_space=pl.ANY)
    *moved, gathered, losses = pl.pallas_call(
        lambda *refs: whole_kernel(peers, groups, *refs),
        out_shape=(
            *(shape((rows, channels), BF16) for _ in range(4)),
            shape((peers, half_rows, lanes), BF16),
            shape((8, lanes), F32),
        ),
        in_specs=[here] * 4 + [away] * len(loaded),
        out_specs=[away] * 5 + [here],
        scratch_shapes=scratch,
        compiler_params=pltpu.CompilerParams(
            collective_id=0, has_side_effects=True, vmem_limit_bytes=63_000_000
        ),
        name="hyena",
    )(
        row_place.reshape(1, rows),
        taxon_ids.reshape(1, rows),
        taxon_weight.reshape(1, -1),
        short_weight,
        *loaded,
    )
    count = taxon_weight.shape[0]
    gated_out, query_grad, key_grad, value_grad, filter_grad, short_grad, losses = pl.pallas_call(
        finish_kernel,
        out_shape=(
            *(shape((rows, channels), BF16) for _ in range(4)),
            shape((taps, channels), F32),
            shape((3, short_taps, channels), F32),
            shape((1, count), F32),
        ),
        in_specs=[away] * 5 + [here],
        out_specs=[away] * 6 + [here],
        scratch_shapes=[
            *(vm((rows, channels), BF16) for _ in range(4)),
            vm((peers, half_rows, lanes), BF16),
            vm((taps, channels), F32),
            vm((3, short_taps, channels), F32),
            vm((payload - taps, lanes), F32),
            dma((5,)),
            dma((6,)),
        ],
        name="finish",
    )(*moved, gathered, losses)
    return (
        gated_out,
        query_grad,
        key_grad,
        value_grad,
        filter_grad,
        short_grad,
        losses.reshape(count),
    )


def solution(mesh):
    placed = (
        P("ctx", "ch"),
        P("ctx", "ch"),
        P("ctx", "ch"),
        P("ctx"),
        P(None, None, "ch"),
        P(None, "ch"),
        P("ctx", "ch"),
        P("ctx"),
        P(),
    )
    return jax.shard_map(
        shards,
        mesh=mesh,
        in_specs=placed,
        out_specs=(
            P("ctx", "ch"),
            P("ctx", "ch"),
            P("ctx", "ch"),
            P("ctx", "ch"),
            P(None, "ch"),
            P(None, None, "ch"),
            P(),
        ),
        check_vma=False,
    )
```

```python
import math

import jax
import jax.numpy as jnp
import numpy as np
from jax import lax
from jax.experimental import pallas as pl
from jax.experimental.pallas import tpu as pltpu
from jax.sharding import PartitionSpec as P

MESH = pl.DeviceIdType.MESH
F32 = jnp.float32
BF16 = jnp.bfloat16
unit = 5
block_rows = 16
lanes = 128
edge = 16
chunks = 4
stride = 7
window = 2
stream_step = 1024.0


def split_constant(array):
    high = array.astype(np.float32).astype(jnp.bfloat16)
    low = (array - high.astype(np.float64)).astype(np.float32).astype(jnp.bfloat16)
    return high, low


def dft_tables(rows, taps):
    half = rows
    size = 2 * rows
    span = taps + rows + edge
    theta = np.pi * (2 * np.arange(half) + 1) / size

    def ahead(index):
        angle = theta[:, None] * index[None, :]
        return np.concatenate([np.cos(angle), -np.sin(angle)], axis=0)

    def back(index):
        angle = theta[None, :] * index[:, None]
        return np.concatenate([np.cos(angle), -np.sin(angle)], axis=1) * (2.0 / size)

    tables = {
        "ahead": ahead(np.arange(span)),
        "own": ahead(np.arange(rows)),
        "later": ahead(np.arange(rows, rows + taps + edge)),
        "taps": ahead(np.arange(taps)),
        "mixed": back(np.arange(rows + edge) + taps),
        "gated": back(np.arange(rows + edge)),
        "filter": back(taps - np.arange(taps)),
    }
    return tables


back_names = ("mixed", "gated", "filter")
table_names = ("taps", "ahead", "own", "later", "mixed", "gated", "filter")


def payload_rows(taps, short_taps):
    return -(-(taps + 3 * short_taps) // 32) * 32


def iota(shape, axis):
    return lax.broadcasted_iota(jnp.int32, shape, axis)


def slot_facts(index):
    block = lax.shift_right_logical(index, 4)
    row = jnp.bitwise_and(index, block_rows - 1)
    stream = jnp.where(row >= unit, 1, 0) + jnp.where(row >= 2 * unit, 1, 0)
    rank = row - unit * stream
    valid = row < 3 * unit
    return block, stream, rank, valid


def whole_kernel(
    peers,
    groups,
    place_ref,
    taxon_ref,
    weight_ref,
    short_ref,
    *refs,
):
    far = refs[:12]
    out_hbm, qg_hbm, kg_hbm, vg_hbm, ag_r, loss_ref = refs[12:18]
    near = refs[18:30]
    (
        q_ref,
        k_ref,
        v_ref,
        target_ref,
        filter_ref,
        taps_t,
        ahead_t,
        own_t,
        later_t,
        mixed_t,
        gated_t,
        filter_t,
    ) = near
    sem_in = refs[30]
    (
        out_ref,
        pack_m,
        unpack_m,
        place_m,
        return_m,
        send_b,
        recv_b,
        meta_s,
        meta_r,
        bsend_b,
        brecv_b,
        grads_b,
        rows_b,
        prev_s,
        prev_r,
        next_s,
        next_r,
        tnext_s,
        tnext_r,
        wnext_s,
        wnext_r,
        qc_b,
        kc_b,
        vc_b,
        go_b,
        gext_b,
        gm_b,
        spec_b,
        short_b,
        gbuf,
        gr_b,
        lacc,
        ids_b,
        par_b,
        half_b,
        half_r,
        z_s,
        z_r,
        y_s,
        y_r,
        f_s,
        lch_s,
        lch_r,
        lct_s,
        lct_r,
        sem_as,
        sem_ar,
        sem_bs,
        sem_br,
        sem_ps,
        sem_pr,
        sem_ns,
        sem_nr,
        sem_gs,
        sem_gr,
        sem_ms,
        sem_mr,
        sem_hs,
        sem_hr,
        sem_zs,
        sem_zr,
        sem_ys,
        sem_yr,
        sem_fs,
        sem_fr,
        sem_out,
        sem_x,
    ) = refs[31:]
    rows, channels = q_ref.shape
    taps = filter_ref.shape[0]
    short_taps = short_ref.shape[1]
    width = channels // chunks
    col_tiles = channels // lanes
    tiles = width // lanes
    pairs = tiles // 2
    blocks = peers + 1
    slots = blocks * block_rows
    ext = rows + edge
    payload = payload_rows(taps, short_taps)
    half_rows = payload // 2
    me = lax.axis_index("ctx")
    depth = tiles
    breadth = peers // (2 * depth)
    core = lax.rem(me, 2)
    my_y = lax.rem(me // 2, breadth)
    my_z = me // (2 * breadth)
    partner = me + 1 - 2 * core
    ch = lax.axis_index("ch")
    right = lax.rem(me + 1, peers)
    left = lax.rem(me + peers - 1, peers)
    grad_scale = 1.0 / math.sqrt(rows * peers)
    loss_scale = 1.0 / math.sqrt(channels * groups * rows * peers / weight_ref.shape[1])

    barrier = pltpu.get_barrier_semaphore()

    def greet(step, carry):
        pl.semaphore_signal(
            barrier, inc=1, device_id=(lax.rem(me + step, peers), ch), device_id_type=MESH
        )
        return carry

    lax.fori_loop(1, peers, greet, 0)
    for step in range(1, groups):
        pl.semaphore_signal(
            barrier, inc=1, device_id=(me, lax.rem(ch + step, groups)), device_id_type=MESH
        )

    def fetch(index):
        return pltpu.make_async_copy(far[index], near[index], sem_in.at[index])

    for index in range(len(far)):
        fetch(index).start()

    def push(src, dst, send_sem, recv_sem, ctx_to, ch_to):
        return pltpu.make_async_remote_copy(
            src_ref=src,
            dst_ref=dst,
            send_sem=send_sem,
            recv_sem=recv_sem,
            device_id=(ctx_to, ch_to),
            device_id_type=MESH,
        )

    def drain(ref, sem):
        pltpu.make_async_copy(ref, ref, sem).wait()

    def column(row_vector, count):
        eye = iota((count, count), 0) == iota((count, count), 1)
        return jnp.sum(jnp.where(eye, row_vector, 0.0), axis=1, keepdims=True)

    place_row = place_ref[...].astype(F32)
    place3_row = jnp.concatenate([place_row] * 3, axis=1)
    owner_row = jnp.floor((place_row + 0.5) * (1.0 / rows))
    owner3_row = jnp.floor((place3_row + 0.5) * (1.0 / rows))
    owner_col = column(owner_row, rows)
    place_col = column(place_row, rows)
    local_col = place_col - owner_col * rows

    def slot_key(owner, rank):
        return jnp.where(
            rank < unit - 0.5, owner * unit + rank, float(peers * unit) + rank - unit
        )

    order3 = iota((rows, 3 * rows), 1)
    stream3 = jnp.where(order3 >= rows, 1, 0) + jnp.where(order3 >= 2 * rows, 1, 0)
    before3 = iota((rows, 3 * rows), 0) < order3 - rows * stream3
    rank3_row = jnp.sum(
        jnp.where(jnp.logical_and(owner_col == owner3_row, before3), 1.0, 0.0),
        axis=0,
        keepdims=True,
    )
    key3_row = slot_key(owner3_row, rank3_row)
    before = iota((rows, rows), 1) < iota((rows, rows), 0)
    rank_col = jnp.sum(
        jnp.where(jnp.logical_and(owner_col == owner_row, before), 1.0, 0.0),
        axis=1,
        keepdims=True,
    )
    key_col = slot_key(owner_col, rank_col)

    lane3 = iota((1, 3 * rows), 1)
    lane_stream = jnp.where(lane3 >= rows, 1, 0) + jnp.where(lane3 >= 2 * rows, 1, 0)
    lane_local = lane3 - rows * lane_stream

    def static_key(shape, axis):
        block, stream, rank, valid = slot_facts(iota(shape, axis))
        key = jnp.where(valid, stream * 1024 + block * unit + rank, -1)
        return key.astype(F32), jnp.where(valid, stream * 1024, -4096).astype(F32)

    slot_key_col, slot_stream_col = static_key((slots, 1), 0)
    slot_key_row, slot_stream_row = static_key((1, slots), 1)
    full3_row = key3_row + lane_stream.astype(F32) * stream_step
    pack_m[...] = jnp.where(slot_key_col == full3_row, 1.0, 0.0).astype(BF16)
    meta_col = jnp.broadcast_to(local_col + 1.0, (rows, lanes)).astype(BF16)
    meta3 = jnp.concatenate([meta_col] * 3, axis=0)
    meta_s[...] = (
        jnp.dot(pack_m[...], meta3, preferred_element_type=F32)
        .astype(BF16)
        .reshape(blocks, block_rows, lanes)
    )

    pair_lanes = 2 * lanes

    def pack(c, carry):
        def body(u, inner):
            base = pl.multiple_of(c * width + u * pair_lanes, pair_lanes)
            cols = pl.ds(base, pair_lanes)
            stacked = jnp.concatenate([q_ref[:, cols], k_ref[:, cols], v_ref[:, cols]], axis=0)
            packed = jnp.dot(pack_m[...], stacked, preferred_element_type=F32).astype(BF16)
            local = pl.ds(pl.multiple_of(u * pair_lanes, pair_lanes), pair_lanes)
            send_b[c, :, :, local] = packed.reshape(blocks, block_rows, pair_lanes)
            return inner

        lax.fori_loop(0, pairs, body, 0)
        return carry

    wait_for = peers - 1 + groups - 1

    def exchange(source, landing, send_sem, recv_sem):
        pltpu.make_async_copy(source.at[me], landing.at[me], recv_sem).start()
        push(source.at[peers], landing.at[peers], send_sem, recv_sem, right, ch).start()

        def body(step, carry):
            to = lax.rem(me + step * stride, peers)
            push(source.at[to], landing.at[me], send_sem, recv_sem, to, ch).start()
            return carry

        lax.fori_loop(1, peers, body, 0)

    near_peers = 3 * peers // 4

    def return_some(c, first, last):
        def body(step, carry):
            to = lax.rem(me + step * stride, peers)
            push(bsend_b.at[c, to], brecv_b.at[c, me], sem_bs.at[c], sem_br.at[c], to, ch).start()
            return carry

        lax.fori_loop(first, last, body, 0)

    def return_first(c):
        pltpu.make_async_copy(bsend_b.at[c, me], brecv_b.at[c, me], sem_br.at[c]).start()
        push(
            bsend_b.at[c, peers], brecv_b.at[c, peers], sem_bs.at[c], sem_br.at[c], left, ch
        ).start()
        return_some(c, 1, near_peers)

    def return_rest(c):
        return_some(c, near_peers, peers)

    for index in range(3):
        fetch(index).wait()
    pack(0, 0)
    pl.semaphore_wait(barrier, wait_for)
    exchange(meta_s, meta_r, sem_ms.at[0], sem_mr.at[0])
    target_push = push(tnext_s, tnext_r, sem_x.at[0], sem_x.at[1], left, ch)
    weight_push = push(wnext_s, wnext_r, sem_x.at[12], sem_x.at[13], left, ch)
    exchange(send_b.at[0], recv_b.at[0], sem_as.at[0], sem_ar.at[0])

    def pack_and_send(c, carry):
        pack(c, 0)
        exchange(send_b.at[c], recv_b.at[c], sem_as.at[c], sem_ar.at[c])
        return carry

    lax.fori_loop(1, window, pack_and_send, 0)
    fetch(3).wait()
    ids_row = taxon_ref[...].astype(F32)
    ids_col = column(ids_row, rows)
    count = weight_ref.shape[1]
    taxon_hot = iota((rows, lanes), 1).astype(F32) == ids_col
    weights = jnp.concatenate([weight_ref[...], jnp.zeros((1, lanes - count), F32)], axis=1)
    weight_col = jnp.sum(jnp.where(taxon_hot, weights, 0.0), axis=1, keepdims=True)
    ids_b[...] = jnp.broadcast_to(ids_col, (rows, lanes))
    tnext_s[...] = target_ref[0:edge, :]
    wnext_s[...] = jnp.broadcast_to(weight_col[0:edge], (edge, lanes))
    target_push.start()
    weight_push.start()
    for s in range(3):
        return_m[s * rows : (s + 1) * rows, :] = jnp.where(
            key_col + s * stream_step == slot_key_row, 1.0, 0.0
        ).astype(BF16)

    lax.fori_loop(window, chunks, pack, 0)
    for index in range(4, len(far)):
        fetch(index).wait()

    short_b[:, 0:short_taps, :] = short_ref[...].astype(F32)

    def both(table, x):
        return jnp.dot(
            table[...], jnp.concatenate([x, x], axis=0), preferred_element_type=F32
        )

    def filter_spectrum(u, carry):
        cols = pl.ds(pl.multiple_of(u * pair_lanes, pair_lanes), pair_lanes)
        x = filter_ref[:, cols]
        found = both(taps_t, x)
        spec_b[2 * u] = found[:, :lanes]
        spec_b[2 * u + 1] = found[:, lanes:]
        return carry

    lax.fori_loop(0, col_tiles // 2, filter_spectrum, 0)
    lacc[...] = jnp.zeros_like(lacc)
    par_b[...] = jnp.zeros_like(par_b)

    drain(meta_r, sem_mr.at[0])
    meta = meta_r[...].reshape(slots, lanes)
    pick = jnp.where(iota((8, lanes), 1) == 0, 1.0, 0.0).astype(BF16)
    found_row = lax.dot_general(
        pick, meta, (((1,), (1,)), ((), ())), preferred_element_type=F32
    )[0:1, :]
    landed_row = found_row + slot_stream_row
    landed_col = meta[:, 0:1].astype(F32) + slot_stream_col
    target_lane = (lane_local + 1).astype(F32) + lane_stream.astype(F32) * stream_step
    place_m[...] = jnp.where(landed_col == target_lane, 1.0, 0.0).astype(BF16)
    own_index = (iota((rows, 1), 0) + 1).astype(F32)
    for s in range(3):
        unpack_m[s * rows : (s + 1) * rows, :] = jnp.where(
            own_index + s * stream_step == landed_row, 1.0, 0.0
        ).astype(BF16)
    target_push.wait()
    weight_push.wait()
    not_first = jnp.where(me > 0, 1.0, 0.0)
    not_last = jnp.where(me < peers - 1, 1.0, 0.0)

    def tile_range(c):
        return pl.ds(c * tiles, tiles)

    def prev_push(c):
        return push(prev_s.at[c], prev_r.at[c], sem_ps.at[c], sem_pr.at[c], right, ch)

    def next_push(c):
        return push(next_s.at[c], next_r.at[c], sem_ns.at[c], sem_nr.at[c], left, ch)

    def gated_push(c):
        return push(
            gext_b.at[tile_range(c), taps_at : taps_at + taps, :],
            gext_b.at[tile_range(c), 0:taps, :],
            sem_gs.at[c],
            sem_gr.at[c],
            right,
            ch,
        )

    taps_at = rows

    def mixed_push(c):
        return push(
            gm_b.at[tile_range(c), 0 : taps + edge, :],
            gm_b.at[tile_range(c), rows : rows + taps + edge, :],
            sem_gs.at[chunks + c],
            sem_gr.at[chunks + c],
            left,
            ch,
        )

    def land(c):
        drain(recv_b.at[c], sem_ar.at[c])

        def body(u, carry):
            local = pl.ds(pl.multiple_of(u * pair_lanes, pair_lanes), pair_lanes)
            got = recv_b[c, :, :, local].reshape(slots, pair_lanes)
            placed = jnp.dot(unpack_m[...], got, preferred_element_type=F32)
            for part in range(2):
                at = c * tiles + 2 * u + part
                piece = placed[:, part * lanes : (part + 1) * lanes]
                for s in range(3):
                    rows_b[s, at, edge : edge + rows, :] = piece[s * rows : (s + 1) * rows]
                    prev_s[c, s, 2 * u + part] = piece[
                        (s + 1) * rows - edge : (s + 1) * rows
                    ].astype(BF16)
                    if s > 0:
                        next_s[c, s - 1, 2 * u + part] = piece[
                            s * rows : s * rows + edge
                        ].astype(BF16)
            return carry

        lax.fori_loop(0, pairs, body, 0)
        prev_push(c).start()
        next_push(c).start()

    def convolve(c):
        prev_push(c).wait()
        next_push(c).wait()

        def body(u, carry):
            at = c * tiles + u
            cols = pl.ds(pl.multiple_of(at * lanes, lanes), lanes)
            for s in range(3):
                rows_b[s, at, 0:edge, :] = prev_r[c, s, u].astype(F32) * not_first
            for s in range(2):
                rows_b[s + 1, at, edge + rows : 2 * edge + rows, :] = next_r[c, s, u].astype(F32)

            def conv(s, total):
                summed = None
                for j in range(short_taps):
                    term = (
                        short_b[s, j : j + 1, cols]
                        * rows_b[s, at, edge - j : edge - j + total, :]
                    )
                    summed = term if summed is None else summed + term
                return summed

            k_conv = conv(1, ext)
            v_conv = conv(2, ext)
            kc_b[at] = k_conv
            vc_b[at] = v_conv
            gext_b[at, taps : taps + ext, :] = (k_conv * v_conv).astype(BF16)
            q_conv = conv(0, rows)
            qc_b[at] = q_conv
            out_grad = weight_col[0:rows] * target_ref[:, cols].astype(F32)
            go_b[at, 0:rows, :] = out_grad
            go_b[at, rows:ext, :] = (
                wnext_r[...] * tnext_r[:, cols].astype(F32) * not_last
            )
            gm_b[at, 0:rows, :] = (out_grad * q_conv).astype(BF16)
            return carry

        lax.fori_loop(0, tiles, body, 0)
        gated_push(c).start()
        mixed_push(c).start()

    def inverse(table, real, imag):
        y = jnp.concatenate([real, imag], axis=0)
        y_hi = y.astype(BF16)
        y_lo = (y - y_hi.astype(F32)).astype(BF16)
        stacked = jnp.concatenate([y_hi, y_lo, y_hi], axis=0)
        return jnp.dot(table[...], stacked, preferred_element_type=F32)

    def backward(c):
        gated_push(c).wait()
        mixed_push(c).wait()

        @pl.when(me == 0)
        def _():
            def clear(u, carry):
                gext_b[c * tiles + u, 0:taps, :] = jnp.zeros((taps, lanes), BF16)
                return carry

            lax.fori_loop(0, tiles, clear, 0)

        @pl.when(me == peers - 1)
        def _():
            def clear(u, carry):
                gm_b[c * tiles + u, rows : rows + taps + edge, :] = jnp.zeros(
                    (taps + edge, lanes), BF16
                )
                return carry

            lax.fori_loop(0, tiles, clear, 0)

        def body(u, carry):
            first = c * tiles + 2 * u
            gx = jnp.concatenate([gext_b[first], gext_b[first + 1]], axis=1)
            g_own = jnp.concatenate(
                [gm_b[first, 0:rows, :], gm_b[first + 1, 0:rows, :]], axis=1
            )
            g_later = jnp.concatenate(
                [
                    gm_b[first, rows : rows + taps + edge, :],
                    gm_b[first + 1, rows : rows + taps + edge, :],
                ],
                axis=1,
            )
            spec = jnp.concatenate([spec_b[first], spec_b[first + 1]], axis=1)
            fr, fi = spec[:rows], spec[rows:]
            sg = both(ahead_t, gx)
            gr, gi = sg[:rows], sg[rows:]
            mixed = inverse(mixed_t, fr * gr - fi * gi, fr * gi + fi * gr)
            so = both(own_t, g_own)
            mr, mi = so[:rows], so[rows:]
            taps_grad = inverse(filter_t, mr * gr + mi * gi, mr * gi - mi * gr)
            sl = both(later_t, g_later)
            ar, ai = mr + sl[:rows], mi + sl[rows:]
            gated_grad = inverse(gated_t, fr * ar + fi * ai, fr * ai - fi * ar)
            for part in range(2):
                at = first + part
                cols = pl.ds(pl.multiple_of(at * lanes, lanes), lanes)
                lane_cut = slice(part * lanes, (part + 1) * lanes)
                mix = mixed[:, lane_cut]
                gg = gated_grad[:, lane_cut]
                tile = 2 * u + part
                found_taps = taps_grad[:, lane_cut]
                half_b[c, 0, tile] = found_taps[0:half_rows]
                half_b[c, 1, tile, 0 : taps - half_rows, :] = found_taps[half_rows:]
                out = (qc_b[at] * mix[:rows]).astype(BF16)
                out_ref[:, cols] = out
                lacc[...] += out.astype(F32) * target_ref[:, cols].astype(F32)
                gbuf[0] = go_b[at] * mix
                gbuf[1] = gg * vc_b[at]
                gbuf[2] = gg * kc_b[at]
                for s in range(3):
                    own = rows_b[s, at, edge : edge + rows, :]
                    back = None
                    for j in range(short_taps):
                        ahead = gbuf[s, j : j + rows, :]
                        found = jnp.sum(ahead * own, axis=0, keepdims=True)
                        par_b[s * short_taps + j : s * short_taps + j + 1, :] = found
                        term = short_b[s, j : j + 1, cols] * ahead
                        back = term if back is None else back + term
                    gr_b[s * rows : (s + 1) * rows, lane_cut] = back.astype(BF16)
                half_b[c, 1, tile, taps - half_rows : half_rows, :] = par_b[...]
            local = pl.ds(pl.multiple_of(u * pair_lanes, pair_lanes), pair_lanes)
            packed = jnp.dot(place_m[...], gr_b[...], preferred_element_type=F32).astype(BF16)
            bsend_b[c, :, :, local] = packed.reshape(blocks, block_rows, pair_lanes)
            return carry

        lax.fori_loop(0, pairs, body, 0)
        out_copy(c).start()

        half_push(c).start()

    def half_push(c):
        return push(
            half_b.at[c, 1 - core], half_r.at[c], sem_hs.at[c], sem_hr.at[c], partner, ch
        )

    def chip_sum(c):
        half_push(c).wait()

        def body(t, carry):
            z_s[c, t] = (half_b[c, core, t] + half_r[c, t]).astype(BF16)
            return carry

        lax.fori_loop(0, depth, body, 0)
        pltpu.make_async_copy(z_s.at[c, my_z], z_r.at[c, my_z], sem_zr.at[c]).start()

        def send(step, carry):
            z_to = lax.rem(my_z + step, depth)
            to = (z_to * breadth + my_y) * 2 + core
            push(z_s.at[c, z_to], z_r.at[c, my_z], sem_zs.at[c], sem_zr.at[c], to, ch).start()
            return carry

        lax.fori_loop(1, depth, send, 0)

    def line_sum(c):
        drain(z_r.at[c], sem_zr.at[c])
        summed = z_r[c, 0].astype(F32)
        for z in range(1, depth):
            summed = summed + z_r[c, z].astype(F32)
        y_s[c] = summed.astype(BF16)
        pltpu.make_async_copy(y_s.at[c], y_r.at[c, my_y], sem_yr.at[c]).start()

        def send(step, carry):
            y_to = lax.rem(my_y + step, breadth)
            to = (my_z * breadth + y_to) * 2 + core
            push(y_s.at[c], y_r.at[c, my_y], sem_ys.at[c], sem_yr.at[c], to, ch).start()
            return carry

        lax.fori_loop(1, breadth, send, 0)

    def plane_sum(c):
        drain(y_r.at[c], sem_yr.at[c])
        summed = y_r[c, 0].astype(F32)
        for y in range(1, breadth):
            summed = summed + y_r[c, y].astype(F32)
        f_s[c] = (summed * grad_scale).astype(BF16)
        piece = (c * depth + my_z) * 2 + core
        pltpu.make_async_copy(f_s.at[c], ag_r.at[piece], sem_fr.at[0]).start()
        push(f_s.at[c], ag_r.at[piece], sem_fs.at[c], sem_fr.at[0], partner, ch).start()

        def send(step, carry):
            z_to = lax.rem(my_z + step, depth)
            to = (z_to * breadth + my_y) * 2
            push(f_s.at[c], ag_r.at[piece], sem_fs.at[c], sem_fr.at[0], to, ch).start()
            push(f_s.at[c], ag_r.at[piece], sem_fs.at[c], sem_fr.at[0], to + 1, ch).start()
            return carry

        lax.fori_loop(1, depth, send, 0)

    def grad_copies(c):
        cols = pl.ds(pl.multiple_of(c * width, width), width)
        return [
            pltpu.make_async_copy(grads_b.at[s, :, cols], to.at[:, cols], sem_out.at[chunks + c])
            for s, to in enumerate((qg_hbm, kg_hbm, vg_hbm))
        ]

    def finish(c):
        drain(brecv_b.at[c], sem_br.at[c])

        def body(u, inner):
            local = pl.ds(pl.multiple_of(u * pair_lanes, pair_lanes), pair_lanes)
            cols = pl.ds(pl.multiple_of(c * width + u * pair_lanes, pair_lanes), pair_lanes)
            got = brecv_b[c, :, :, local].reshape(slots, pair_lanes)
            back = jnp.dot(return_m[...], got, preferred_element_type=F32).astype(BF16)
            for s in range(3):
                grads_b[s, :, cols] = back[s * rows : (s + 1) * rows]
            return inner

        lax.fori_loop(0, pairs, body, 0)
        for copy in grad_copies(c):
            copy.start()

    def finish_step(c, carry):
        finish(c)
        return carry

    def out_copy(c):
        cols = pl.ds(pl.multiple_of(c * width, width), width)
        return pltpu.make_async_copy(out_ref.at[:, cols], out_hbm.at[:, cols], sem_out.at[c])

    def loss_push(step):
        return push(
            lch_s, lch_r.at[ch], sem_x.at[8 + step], sem_x.at[2], me, lax.rem(ch + step, groups)
        )

    def start_loss():
        row_loss = jnp.sum(lacc[...], axis=1, keepdims=True)
        hot = iota((rows, lanes), 1).astype(F32) == ids_b[...]
        taxon_part = jnp.sum(jnp.where(hot, row_loss, 0.0), axis=0, keepdims=True) * loss_scale
        lch_s[...] = jnp.broadcast_to(taxon_part, (8, lanes))
        lch_r[ch] = jnp.broadcast_to(taxon_part, (8, lanes))
        for step in range(1, groups):
            loss_push(step).start()

    def share_loss():
        if groups > 1:
            drain(lch_r.at[0 : groups - 1], sem_x.at[2])
        total = lch_r[0]
        for g in range(1, groups):
            total = total + lch_r[g]
        lct_s[...] = total
        lct_r[me] = total

        def send(step, carry):
            to = lax.rem(me + step, peers)
            push(lct_s, lct_r.at[me], sem_x.at[5], sem_x.at[6], to, ch).start()
            return carry

        lax.fori_loop(1, peers, send, 0)

    def steps(t, carry):
        @pl.when(t < chunks)
        def _():
            land(t)

        @pl.when(jnp.logical_and(t >= 1, t < chunks + 1))
        def _():
            convolve(t - 1)

        @pl.when(t >= 3)
        def _():
            chip_sum(t - 3)

        @pl.when(t >= 4)
        def _():
            line_sum(t - 4)

        @pl.when(t >= 5)
        def _():
            plane_sum(t - 5)

        @pl.when(t + window < chunks)
        def _():
            later = t + window
            exchange(send_b.at[later], recv_b.at[later], sem_as.at[later], sem_ar.at[later])

        @pl.when(t >= 3)
        def _():
            return_rest(t - 3)

        @pl.when(t >= 2)
        def _():
            backward(t - 2)

        @pl.when(t == chunks + 1)
        def _():
            chip_sum(t - 2)

        @pl.when(t >= 2)
        def _():
            return_first(t - 2)

        return carry

    lax.fori_loop(0, chunks + 2, steps, 0)
    last = chunks - 1
    start_loss()
    line_sum(last - 1)
    plane_sum(last - 2)
    finish(0)
    line_sum(last)
    return_rest(last)
    share_loss()
    plane_sum(last - 1)
    finish(1)
    plane_sum(last)
    lax.fori_loop(2, chunks, finish_step, 0)

    drain(lct_r.at[0 : peers - 1], sem_x.at[6])

    def add_loss(j, summed):
        return summed + lct_r[j]

    loss_ref[...] = lax.fori_loop(1, peers, add_loss, lct_r[0])
    for c in range(chunks):
        out_copy(c).wait()
        for copy in grad_copies(c):
            copy.wait()
    drain(ag_r, sem_fr.at[0])

    drain(meta_s.at[0:peers], sem_ms.at[0])
    for step in range(1, groups):
        loss_push(step).wait_send()
    drain(lct_r.at[0 : peers - 1], sem_x.at[5])

    def sent(c, carry):
        drain(send_b.at[c, 0:peers], sem_as.at[c])
        drain(bsend_b.at[c, 0:peers], sem_bs.at[c])
        drain(z_r.at[c, 0 : depth - 1], sem_zs.at[c])
        drain(y_r.at[c, 0 : breadth - 1], sem_ys.at[c])
        drain(ag_r.at[0 : 2 * depth - 1], sem_fs.at[c])
        return carry

    lax.fori_loop(0, chunks, sent, 0)


def finish_kernel(*refs):
    sources, loss_in = refs[0:5], refs[5]
    targets, loss_ref = refs[6:12], refs[12]
    held, par_b, sem_in, sem_out = refs[13:20], refs[20], refs[21], refs[22]
    ag_ref, fg_ref, sg_ref = held[4:7]
    taps, short_taps = fg_ref.shape[0], sg_ref.shape[1]
    half_rows = ag_ref.shape[1]
    ins = [pltpu.make_async_copy(sources[i], held[i], sem_in.at[i]) for i in range(5)]
    leaving = (0, 1, 2, 3, 5, 6)
    outs = [
        pltpu.make_async_copy(held[i], targets[n], sem_out.at[n]) for n, i in enumerate(leaving)
    ]
    for i in (0, 4, 1, 2, 3):
        ins[i].start()
    loss_ref[...] = loss_in[0:1, 0 : loss_ref.shape[1]]
    ins[0].wait()
    outs[0].start()
    ins[4].wait()
    for t in range(fg_ref.shape[1] // lanes):
        cut = slice(t * lanes, (t + 1) * lanes)
        low = ag_ref[2 * t + 1].astype(F32)
        fg_ref[0:half_rows, cut] = ag_ref[2 * t].astype(F32)
        fg_ref[half_rows:taps, cut] = low[0 : taps - half_rows]
        par_b[...] = low[taps - half_rows :]
        for s in range(3):
            sg_ref[s, :, cut] = par_b[s * short_taps : (s + 1) * short_taps, :]
    outs[4].start()
    outs[5].start()
    for i in range(1, 4):
        ins[i].wait()
        outs[i].start()
    for copy in outs:
        copy.wait()


def shards(
    query_in,
    key_in,
    value_in,
    row_place,
    short_weight,
    long_filter,
    target,
    taxon_ids,
    taxon_weight,
):
    rows, channels = query_in.shape
    peers = lax.axis_size("ctx")
    groups = lax.axis_size("ch")
    taps = long_filter.shape[0]
    short_taps = short_weight.shape[1]
    width = channels // chunks
    col_tiles = channels // lanes
    tiles = width // lanes
    blocks = peers + 1
    slots = blocks * block_rows
    ext = rows + edge
    span = taps + ext
    payload = payload_rows(taps, short_taps)
    half_rows = payload // 2
    tables = []
    made = dft_tables(rows, taps)
    for name in table_names:
        high, low = split_constant(made[name])
        parts = (high, high, low) if name in back_names else (high, low)
        tables.append(jnp.asarray(np.concatenate(parts, axis=1)))
    vm = pltpu.VMEM
    dma = pltpu.SemaphoreType.DMA
    shape = jax.ShapeDtypeStruct
    loaded = (query_in, key_in, value_in, target, long_filter, *tables)
    scratch = [
        *(vm(x.shape, x.dtype) for x in loaded),
        dma((len(loaded),)),
        vm((rows, channels), BF16),
        vm((slots, 3 * rows), BF16),
        vm((3 * rows, slots), BF16),
        vm((slots, 3 * rows), BF16),
        vm((3 * rows, slots), BF16),
        vm((chunks, blocks, block_rows, width), BF16),
        vm((chunks, blocks, block_rows, width), BF16),
        vm((blocks, block_rows, lanes), BF16),
        vm((blocks, block_rows, lanes), BF16),
        vm((chunks, blocks, block_rows, width), BF16),
        vm((chunks, blocks, block_rows, width), BF16),
        vm((3, rows, channels), BF16),
        vm((3, col_tiles, rows + 2 * edge, lanes), F32),
        vm((chunks, 3, tiles, edge, lanes), BF16),
        vm((chunks, 3, tiles, edge, lanes), BF16),
        vm((chunks, 2, tiles, edge, lanes), BF16),
        vm((chunks, 2, tiles, edge, lanes), BF16),
        vm((edge, channels), BF16),
        vm((edge, channels), BF16),
        vm((edge, lanes), F32),
        vm((edge, lanes), F32),
        vm((col_tiles, rows, lanes), F32),
        vm((col_tiles, ext, lanes), F32),
        vm((col_tiles, ext, lanes), F32),
        vm((col_tiles, ext, lanes), F32),
        vm((col_tiles, span, lanes), BF16),
        vm((col_tiles, span, lanes), BF16),
        vm((col_tiles, 2 * rows, lanes), F32),
        vm((3, 8, channels), F32),
        vm((3, ext, lanes), F32),
        vm((3 * rows, 2 * lanes), BF16),
        vm((rows, lanes), F32),
        vm((rows, lanes), F32),
        vm((payload - taps, lanes), F32),
        vm((chunks, 2, tiles, half_rows, lanes), F32),
        vm((chunks, tiles, half_rows, lanes), F32),
        vm((chunks, tiles, half_rows, lanes), BF16),
        vm((chunks, tiles, half_rows, lanes), BF16),
        vm((chunks, half_rows, lanes), BF16),
        vm((chunks, peers // (2 * tiles), half_rows, lanes), BF16),
        vm((chunks, half_rows, lanes), BF16),
        vm((8, lanes), F32),
        vm((groups, 8, lanes), F32),
        vm((8, lanes), F32),
        vm((peers, 8, lanes), F32),
        dma((chunks,)),
        dma((chunks,)),
        dma((chunks,)),
        dma((chunks,)),
        dma((chunks,)),
        dma((chunks,)),
        dma((chunks,)),
        dma((chunks,)),
        dma((2 * chunks,)),
        dma((2 * chunks,)),
        dma((1,)),
        dma((1,)),
        dma((chunks,)),
        dma((chunks,)),
        dma((chunks,)),
        dma((chunks,)),
        dma((chunks,)),
        dma((chunks,)),
        dma((chunks,)),
        dma((1,)),
        dma((2 * chunks,)),
        dma((16,)),
    ]
    here = pl.BlockSpec(memory_space=pltpu.VMEM)
    away = pl.BlockSpec(memory_space=pl.ANY)
    *moved, gathered, losses = pl.pallas_call(
        lambda *refs: whole_kernel(peers, groups, *refs),
        out_shape=(
            *(shape((rows, channels), BF16) for _ in range(4)),
            shape((peers, half_rows, lanes), BF16),
            shape((8, lanes), F32),
        ),
        in_specs=[here] * 4 + [away] * len(loaded),
        out_specs=[away] * 5 + [here],
        scratch_shapes=scratch,
        compiler_params=pltpu.CompilerParams(
            collective_id=0, has_side_effects=True, vmem_limit_bytes=63_000_000
        ),
        name="hyena",
    )(
        row_place.reshape(1, rows),
        taxon_ids.reshape(1, rows),
        taxon_weight.reshape(1, -1),
        short_weight,
        *loaded,
    )
    count = taxon_weight.shape[0]
    gated_out, query_grad, key_grad, value_grad, filter_grad, short_grad, losses = pl.pallas_call(
        finish_kernel,
        out_shape=(
            *(shape((rows, channels), BF16) for _ in range(4)),
            shape((taps, channels), F32),
            shape((3, short_taps, channels), F32),
            shape((1, count), F32),
        ),
        in_specs=[away] * 5 + [here],
        out_specs=[away] * 6 + [here],
        scratch_shapes=[
            *(vm((rows, channels), BF16) for _ in range(4)),
            vm((peers, half_rows, lanes), BF16),
            vm((taps, channels), F32),
            vm((3, short_taps, channels), F32),
            vm((payload - taps, lanes), F32),
            dma((5,)),
            dma((6,)),
        ],
        name="finish",
    )(*moved, gathered, losses)
    return (
        gated_out,
        query_grad,
        key_grad,
        value_grad,
        filter_grad,
        short_grad,
        losses.reshape(count),
    )


def solution(mesh):
    placed = (
        P("ctx", "ch"),
        P("ctx", "ch"),
        P("ctx", "ch"),
        P("ctx"),
        P(None, None, "ch"),
        P(None, "ch"),
        P("ctx", "ch"),
        P("ctx"),
        P(),
    )
    return jax.shard_map(
        shards,
        mesh=mesh,
        in_specs=placed,
        out_specs=(
            P("ctx", "ch"),
            P("ctx", "ch"),
            P("ctx", "ch"),
            P("ctx", "ch"),
            P(None, "ch"),
            P(None, None, "ch"),
            P(),
        ),
        check_vma=False,
    )
```
